32 devices in a mesh: fsdp: 8 (over y, x, core), seq: 4 (over z).
Axes of the slice: x: 2, y: 2, z: 4, core: 2. Of those that a mesh axis runs over, the one named last changes fastest.
Arguments:
- layer_input: bfloat16 [16, 2048, 512], P('fsdp', 'seq'), may hold values from -6 to 6
- neighbour_ids: int32 [16, 2048, 4], P('fsdp', 'seq'), may hold values from 0 to 2047, as said below
- out_grad: bfloat16 [16, 2048, 512], P('fsdp', 'seq'), may hold values from -6 to 6
- attn_norm_gain: bfloat16 [512], P('fsdp'), may hold values from 0.099609375 to 1.8984375
- attn_norm_bias: bfloat16 [512], P('fsdp'), may hold values from -3 to 3
- attn_project: bfloat16 [512, 1536], P('fsdp'), may hold values from -0.25 to 0.25
- attn_merge: bfloat16 [512, 512], P('fsdp'), may hold values from -2 to 2
- position_bias: bfloat16 [256], P('fsdp'), may hold values from -4 to 4
- ffn_norm_gain: bfloat16 [512], P('fsdp'), may hold values from 0.099609375 to 1.8984375
- ffn_norm_bias: bfloat16 [512], P('fsdp'), may hold values from -3 to 3
- ffn_expand: bfloat16 [512, 2048], P('fsdp'), may hold values from -0.25 to 0.25
- expand_bias: bfloat16 [2048], P('fsdp'), may hold values from -3 to 3
- ffn_reduce: bfloat16 [2048, 512], P('fsdp'), may hold values from -0.125 to 0.125
- reduce_bias: bfloat16 [512], P('fsdp'), may hold values from -3 to 3
- near_query: bfloat16 [512, 512], P('fsdp'), may hold values from -0.25 to 0.25
- near_keys: bfloat16 [512, 1024], P('fsdp'), may hold values from -0.25 to 0.25
- near_merge: bfloat16 [512, 512], P('fsdp'), may hold values from -0.375 to 0.375
- gate_vector: bfloat16 [512], P('fsdp'), may hold values from -0.1875 to 0.1875
Outputs:
- layer_output: bfloat16 [16, 2048, 512], P('fsdp', 'seq')
- input_grad: float32 [16, 2048, 512], P('fsdp', 'seq')
- grad_attn_norm_gain: float32 [512], P('fsdp')
- grad_attn_norm_bias: float32 [512], P('fsdp')
- grad_attn_project: float32 [512, 1536], P('fsdp')
- grad_attn_merge: float32 [512, 512], P('fsdp')
- grad_position_bias: float32 [256], P('fsdp')
- grad_ffn_norm_gain: float32 [512], P('fsdp')
- grad_ffn_norm_bias: float32 [512], P('fsdp')
- grad_ffn_expand: float32 [512, 2048], P('fsdp')
- grad_expand_bias: float32 [2048], P('fsdp')
- grad_ffn_reduce: float32 [2048, 512], P('fsdp')
- grad_reduce_bias: float32 [512], P('fsdp')
- grad_near_query: float32 [512, 512], P('fsdp')
- grad_near_keys: float32 [512, 1024], P('fsdp')
- grad_near_merge: float32 [512, 512], P('fsdp')
- grad_gate_vector: float32 [512], P('fsdp')
The draws below stay inside these ranges and needn't reach their ends.
Inputs may be any that keep to these rules, and one draw needn't show every extreme that they name: neighbour_ids[s, t, k] names a place of sequence s that is not later than t; the last token of a sequence names itself among its neighbours.
All inputs are finite; a program needn't handle non-finite values.
Results may differ from the reference program's by a relative error of at most 0.025.
Values may be sent and summed in bfloat16 or wider, within the bound.
No kernel may reach another device: no remote copies, remote signals or barrier semaphores. Data moves between devices by JAX's collectives and lax.ppermute only.
A program may use at most 320 MiB of HBM per device.

```python
import jax
import jax.numpy as jnp
from jax import lax

D = 512
H = 8
HD = 64
FF = 2048
K = 4
SEG = 512
NB = 32
LENGTH = 2048
SEQS = 16


def draw_neighbour_ids(key, part):
    positions = lax.broadcasted_iota(jnp.int32, (SEQS, LENGTH, K), 1)
    slots = lax.broadcasted_iota(jnp.int32, (SEQS, LENGTH, K), 2)
    drawn = jax.random.randint(key, (SEQS, LENGTH, K), 0, positions + 1, dtype=jnp.int32)
    own_place = (positions == LENGTH - 1) & (slots == 0)
    return jnp.where(own_place, positions, drawn)


def levels(stream_key, extent, shards, least, high):
    def one(dim, blocks):
        draws = jax.random.uniform(jax.random.fold_in(jax.random.fold_in(stream_key, 6), dim), (blocks,), jnp.float32, least / len(shards), high / len(shards))
        return jnp.repeat(jnp.exp(draws), extent[dim] // blocks).reshape((-1,) + (1,) * (len(extent) - dim - 1))

    loudness = one(*shards[0])
    for cut in shards[1:]:
        loudness = loudness * one(*cut)
    return loudness


def bell_draw(own_key, shape, deviation, limit, shards=(), kind=jnp.bfloat16):
    result = deviation * jax.random.normal(own_key, shape, jnp.float32)
    if shards:
        result = result * levels(own_key, shape, shards, -0.22, 0.18)
    return jnp.clip(result, -limit, limit).astype(kind)


def setup_inputs(seed: int = 0) -> dict:
    arg_keys = jax.random.split(jax.random.key(seed), 19)
    layer_input = bell_draw(arg_keys[0], (SEQS, LENGTH, D), 1.0, 6.0, ((0, 8), (1, 4)))
    neighbour_ids = draw_neighbour_ids(jax.random.fold_in(arg_keys[18], 71), 0)
    out_grad = bell_draw(arg_keys[2], (SEQS, LENGTH, D), 1.0, 6.0, ((0, 8), (1, 4)))
    attn_norm_gain = jnp.clip(1.0 + 0.18 * jax.random.normal(arg_keys[3], (D,), jnp.float32), 0.099609375, 1.8984375).astype(jnp.bfloat16)
    attn_norm_bias = bell_draw(arg_keys[4], (D,), 0.3, 3.0, ((0, 8),))
    attn_project = bell_draw(arg_keys[5], (D, 3 * D), D ** -0.5, 0.25, ((0, 8),))
    attn_merge = bell_draw(arg_keys[6], (D, D), (max(D * D // (64 * SEG), 1)) ** -0.5, 2.0, ((0, 8),))
    position_bias = bell_draw(arg_keys[7], (NB * H,), 1.0, 4.0, ((0, 8),))
    ffn_norm_gain = jnp.clip(1.0 + 0.18 * jax.random.normal(arg_keys[8], (D,), jnp.float32), 0.099609375, 1.8984375).astype(jnp.bfloat16)
    ffn_norm_bias = bell_draw(arg_keys[9], (D,), 0.3, 3.0, ((0, 8),))
    ffn_expand = bell_draw(arg_keys[10], (D, FF), D ** -0.5, 0.25, ((0, 8),))
    expand_bias = bell_draw(arg_keys[11], (FF,), 0.3, 3.0, ((0, 8),))
    ffn_reduce = bell_draw(arg_keys[12], (FF, D), FF ** -0.5, 0.125, ((0, 8),))
    reduce_bias = bell_draw(arg_keys[13], (D,), 0.3, 3.0, ((0, 8),))
    near_query = bell_draw(arg_keys[14], (D, D), D ** -0.5, 0.25, ((0, 8),))
    near_keys = bell_draw(arg_keys[15], (D, 2 * D), D ** -0.5, 0.25, ((0, 8),))
    near_merge = bell_draw(arg_keys[16], (D, D), (D // 2) ** -0.5, 0.375, ((0, 8),))
    gate_vector = bell_draw(arg_keys[17], (D,), (2 * D) ** -0.5, 0.1875, ((0, 8),))
    return dict(layer_input=layer_input, neighbour_ids=neighbour_ids, out_grad=out_grad, attn_norm_gain=attn_norm_gain, attn_norm_bias=attn_norm_bias, attn_project=attn_project, attn_merge=attn_merge, position_bias=position_bias, ffn_norm_gain=ffn_norm_gain, ffn_norm_bias=ffn_norm_bias, ffn_expand=ffn_expand, expand_bias=expand_bias, ffn_reduce=ffn_reduce, reduce_bias=reduce_bias, near_query=near_query, near_keys=near_keys, near_merge=near_merge, gate_vector=gate_vector)


@jax.custom_vjp
def low(v):
    return lax.optimization_barrier(v.astype(jnp.bfloat16)).astype(jnp.float32)

@jax.custom_vjp
def low_back(v):
    return v

def low_keep(v):
    return (low(v), None)

def low_pass(kept, grad):
    return (grad,)

def back_keep(v):
    return (v, None)

def back_low(kept, grad):
    return (low(grad),)
low.defvjp(low_keep, low_pass)
low_back.defvjp(back_keep, back_low)
EPS = 1e-05
HIGH = lax.Precision.HIGHEST
MASKED = -1000000000.0

def matmul(left, right):
    return jnp.dot(left, right, precision=HIGH)

def layer_norm(values, gain, shift):
    average = lax.optimization_barrier(jnp.mean(values, axis=-1, keepdims=True))
    centred = values - average
    variance = lax.optimization_barrier(jnp.mean(centred * centred, axis=-1, keepdims=True))
    return centred * lax.rsqrt(variance + EPS) * gain + shift

def thresholds(seg_len, bucket_count):
    half_count = bucket_count // 2
    spread_ratio = 2.0 * seg_len / half_count
    exact_part = list(range(1, half_count))
    log_part = [int(half_count * spread_ratio ** ((bucket_index - half_count) / half_count)) for bucket_index in range(half_count, bucket_count)]
    return exact_part + log_part

def bucket_grid(row_start, row_count):
    query_pos = lax.broadcasted_iota(jnp.int32, (row_count, 2 * SEG), 0) + jnp.int32(row_start)
    key_pos = lax.broadcasted_iota(jnp.int32, (row_count, 2 * SEG), 1)
    distance = query_pos - key_pos + jnp.int32(SEG)
    bucket = jnp.zeros((row_count, 2 * SEG), jnp.int32)
    for threshold in thresholds(SEG, NB):
        bucket = bucket + (distance >= threshold).astype(jnp.int32)
    return (distance, bucket)

def segment_attention(queries, key_all, value_all, rel_table, segment_index):
    distance, bucket = bucket_grid(0, SEG)
    key_pos = lax.broadcasted_iota(jnp.int32, (SEG, 2 * SEG), 1)
    allowed = jnp.where(key_pos < SEG, segment_index.astype(jnp.int32) > 0, distance >= 0)
    position_grid = jnp.transpose(jnp.take(rel_table, bucket, axis=0), (2, 0, 1))
    scores = jnp.einsum('qhd,khd->hqk', queries, key_all, precision=HIGH) * HD ** (-0.5) + position_grid
    scores = jnp.where(allowed[None], low_back(scores), MASKED)
    attn_probs = jax.nn.softmax(scores, axis=-1)
    return jnp.einsum('hqk,khd->qhd', low(attn_probs), value_all, precision=HIGH)

def sequence_forward(params, inputs, neighbour_rows):
    attn_gain, attn_shift, attn_project, attn_merge, position_flat, ffn_gain, ffn_shift, ffn_expand, expand_bias, ffn_reduce, reduce_bias, near_query, near_keys, near_merge, gate_vector = params
    length = inputs.shape[0]
    segments = length // SEG
    normed = low(layer_norm(inputs, attn_gain, attn_shift))
    joined_rows = low(low_back(matmul(normed, attn_project))).reshape(segments, SEG, 3, H, HD)
    queries = joined_rows[:, :, 0]
    key_rows = joined_rows[:, :, 1]
    value_rows = joined_rows[:, :, 2]
    no_memory = jnp.zeros_like(key_rows[:1])
    key_all = jnp.concatenate([jnp.concatenate([no_memory, key_rows[:-1]], axis=0), key_rows], axis=1)
    value_all = jnp.concatenate([jnp.concatenate([no_memory, value_rows[:-1]], axis=0), value_rows], axis=1)
    rel_table = position_flat.reshape(NB, H)

    def one_segment(element):
        return jax.checkpoint(segment_attention)(element[0], element[1], element[2], rel_table, element[3])
    attended = lax.map(one_segment, (queries, key_all, value_all, jnp.arange(segments, dtype=jnp.int32)))
    attended = low(low_back(attended.reshape(length, D)))
    after_attn = inputs + low_back(matmul(attended, attn_merge))
    ffn_normed = low(layer_norm(after_attn, ffn_gain, ffn_shift))
    pre_active = low_back(matmul(ffn_normed, ffn_expand) + expand_bias)
    active = low(jax.nn.gelu(pre_active, approximate=False))
    after_ffn = after_attn + low_back(matmul(active, ffn_reduce) + reduce_bias)
    near_queries = low(low_back(matmul(low(after_ffn), near_query))).reshape(length, H, HD)
    near_rows = jnp.take(inputs, neighbour_rows.reshape(-1).astype(jnp.int32), axis=0)
    near_kv = low(low_back(matmul(near_rows, near_keys))).reshape(length, K, 2, H, HD)
    near_scores = jnp.einsum('thd,tkhd->thk', near_queries, near_kv[:, :, 0], precision=HIGH) * HD ** (-0.5)
    near_probs = jax.nn.softmax(near_scores, axis=-1)
    near_mixed = jnp.einsum('thk,tkhd->thd', near_probs, near_kv[:, :, 1], precision=HIGH)
    near_mixed = low(low_back(near_mixed.reshape(length, D)))
    near_out = low_back(matmul(near_mixed, near_merge))
    gate_value = jax.nn.sigmoid(lax.optimization_barrier(jnp.sum(after_ffn * gate_vector, axis=-1, keepdims=True)))
    return gate_value * after_ffn + (1.0 - gate_value) * near_out

def reference(layer_input, neighbour_ids, out_grad, attn_norm_gain, attn_norm_bias, attn_project, attn_merge, position_bias, ffn_norm_gain, ffn_norm_bias, ffn_expand, expand_bias, ffn_reduce, reduce_bias, near_query, near_keys, near_merge, gate_vector):
    params = tuple((weight.astype(jnp.float32) for weight in (attn_norm_gain, attn_norm_bias, attn_project, attn_merge, position_bias, ffn_norm_gain, ffn_norm_bias, ffn_expand, expand_bias, ffn_reduce, reduce_bias, near_query, near_keys, near_merge, gate_vector)))

    def one_sequence(totals, element):
        inputs, neighbour_rows, cotangent = element
        output, pullback = jax.vjp(lambda p, v: sequence_forward(p, v, neighbour_rows), params, inputs)
        param_grads, grad_inputs = pullback(cotangent)
        summed = tuple((a + b for a, b in zip(totals, param_grads)))
        return (summed, (output.astype(jnp.bfloat16), grad_inputs))
    start_grads = tuple((jnp.zeros(weight.shape, jnp.float32) for weight in params))
    totals, (layer_output, input_grad) = lax.scan(one_sequence, start_grads, (layer_input.astype(jnp.float32), neighbour_ids.astype(jnp.int32), out_grad.astype(jnp.float32)))
    return (layer_output, input_grad, totals[0], totals[1], totals[2], totals[3], totals[4], totals[5], totals[6], totals[7], totals[8], totals[9], totals[10], totals[11], totals[12], totals[13], totals[14])
```

```python
import functools
import math

import jax
import jax.numpy as jnp
import numpy as np
from jax import lax
from jax.experimental import pallas as pl
from jax.experimental.pallas import tpu as pltpu
from jax.sharding import PartitionSpec as P

D = 512
H = 8
HD = 64
K = 4
SEG = 512
NB = 32

EPS = 1e-05
HIGH = lax.Precision.HIGHEST
MASKED = -1e30
F32 = jnp.float32
BF16 = jnp.bfloat16
ROWS = 256
SPAN = 2 * SEG + 128
VMEM = 56 << 20


def nn(left, right):
    return lax.dot_general(left, right, (((1,), (0,)), ((), ())), preferred_element_type=F32)


def nt(left, right):
    return lax.dot_general(left, right, (((1,), (1,)), ((), ())), preferred_element_type=F32)


def tn(left, right):
    return lax.dot_general(left, right, (((0,), (0,)), ((), ())), preferred_element_type=F32)


def shape(dims, dtype):
    return jax.ShapeDtypeStruct(tuple(dims), dtype)


def whole(dims):
    zeros = (0,) * len(dims)
    return pl.BlockSpec(tuple(dims), lambda *_: zeros, pipeline_mode=pl.Buffered(1))


def scalars():
    return pl.BlockSpec(memory_space=pltpu.SMEM)


def params(grid_rank):
    return pltpu.CompilerParams(
        dimension_semantics=("arbitrary",) * grid_rank, vmem_limit_bytes=VMEM
    )


def cost(flops, moved, exps=0):
    return pl.CostEstimate(
        flops=int(flops), bytes_accessed=int(moved), transcendentals=int(exps)
    )


def thresholds():
    half_count = NB // 2
    spread_ratio = 2.0 * SEG / half_count
    exact_part = list(range(1, half_count))
    log_part = [
        int(half_count * spread_ratio ** ((bucket_index - half_count) / half_count))
        for bucket_index in range(half_count, NB)
    ]
    return np.array(exact_part + log_part)


def bucket_of(distance):
    return (distance[:, None] >= thresholds()[None, :]).sum(axis=1)


def forward_selector():
    distance = 2 * SEG - np.arange(SPAN)
    bucket = bucket_of(np.maximum(distance, 0))
    return (np.arange(NB)[:, None] == bucket[None, :]).astype(np.float32)


def backward_selector():
    place = np.arange(SPAN)
    offset = np.where(place <= 2 * SEG, place, place - SPAN)
    distance = 2 * SEG - 128 - offset
    bucket = bucket_of(np.maximum(distance, 0))
    chosen = (bucket[:, None] == np.arange(NB)[None, :]) & (distance >= 0)[:, None]
    return chosen.astype(np.float32)


def norm(values):
    average = jnp.mean(values, axis=-1, keepdims=True)
    centred = values - average
    variance = jnp.mean(centred * centred, axis=-1, keepdims=True)
    rstd_value = lax.rsqrt(variance + EPS)
    return centred * rstd_value, rstd_value


def norm_back(grad_result, hat_value, rstd_value, gain):
    scaled = grad_result * gain
    return rstd_value * (
        scaled
        - jnp.mean(scaled, axis=-1, keepdims=True)
        - hat_value * jnp.mean(scaled * hat_value, axis=-1, keepdims=True)
    )


def rows_sum(values):
    return jnp.sum(values, axis=0, keepdims=True)


def pair_mask(head, values):
    lane = lax.broadcasted_iota(jnp.int32, values.shape, 1)
    keep = lane < HD if head == 0 else lane >= HD
    return jnp.where(keep, values, jnp.zeros_like(values))


def prep_kernel(parts, place_ref, small_ref, table_ref, select_ref, vec_ref, own_ref, mem_ref):
    small = small_ref[...].astype(F32)
    devices = small.shape[0]
    vec_ref[...] = jnp.zeros_like(vec_ref)
    start = 0
    for row, width in enumerate(parts):
        pieces = [small[d : d + 1, start : start + width] for d in range(devices)]
        vec_ref[row : row + 1, : width * devices] = jnp.concatenate(pieces, axis=1)
        start += width
    by_distance = lax.dot_general(
        table_ref[...],
        select_ref[...],
        (((1,), (0,)), ((), ())),
        precision=HIGH,
        preferred_element_type=F32,
    )
    lane = lax.broadcasted_iota(jnp.int32, by_distance.shape, 1)
    by_distance = jnp.where(lane > 2 * SEG, MASKED, by_distance)
    hidden = jnp.where(place_ref[1] > 0, 0.0, MASKED)
    for head in range(H):
        line = jnp.broadcast_to(by_distance[head : head + 1, :], (128, SPAN))
        skewed = pltpu.roll(line, 0, 1, stride=1, stride_axis=0)
        tile = skewed[:, 128:].T
        own_ref[head] = tile
        mem_ref[head] = tile + hidden


def prep(place, small, table, parts, ff_width):
    devices, width = small.shape
    tiles = shape((H, 2 * SEG, 128), F32)
    return pl.pallas_call(
        functools.partial(prep_kernel, parts),
        in_specs=[scalars()] + [pl.BlockSpec(memory_space=pltpu.VMEM)] * 3,
        out_specs=[pl.BlockSpec(memory_space=pltpu.VMEM)] * 3,
        out_shape=[shape((8, ff_width), F32), tiles, tiles],
        compiler_params=pltpu.CompilerParams(vmem_limit_bytes=VMEM),
        cost_estimate=cost(0, 9 << 20),
        name="prep",
    )(place, small, table, jnp.asarray(forward_selector()))


def device_of(place_ref, chip_step, core_step):
    index = place_ref[0]
    chip = lax.shift_right_logical(index, 1)
    core = jnp.bitwise_and(index, 1)
    return jnp.bitwise_xor(chip, chip_step) * 2 + jnp.bitwise_xor(core, core_step)


def assemble_kernel(layout, place_ref, near_ref, far_ref, *out_refs):
    steps, rows, _ = near_ref.shape
    for core_step, ref in ((0, near_ref), (1, far_ref)):
        for step in range(steps):
            owner = device_of(place_ref, step, core_step)
            start = 0
            for out_ref, (chunks, width) in zip(out_refs, layout):
                for chunk in range(chunks):
                    target = pl.multiple_of((owner * chunks + chunk) * rows, rows)
                    out_ref[pl.ds(target, rows), :] = ref[step, :, start : start + width]
                    start += width


def assemble(place, near, far, layout):
    steps, rows, columns = near.shape
    total = 2 * steps * rows
    outs = [shape((total * chunks, width), BF16) for chunks, width in layout]
    return pl.pallas_call(
        functools.partial(assemble_kernel, layout),
        in_specs=[scalars()] + [pl.BlockSpec(memory_space=pltpu.VMEM)] * 2,
        out_specs=[pl.BlockSpec(memory_space=pltpu.VMEM)] * len(outs),
        out_shape=outs,
        compiler_params=pltpu.CompilerParams(vmem_limit_bytes=VMEM),
        cost_estimate=cost(0, 4 * total * columns),
        name="assemble",
    )(place, near, far)


def project_kernel(first, x_ref, vec_ref, w_ref, out_ref):
    hat_value, _ = norm(x_ref[0].astype(F32))
    normed = (hat_value * vec_ref[0:1, :D] + vec_ref[1:2, :D]).astype(BF16)
    out_ref[0] = nn(normed, w_ref[:, first:]).astype(BF16)


def project(x, vec, weight, first):
    batch, rows, _ = x.shape
    width = weight.shape[1] - first
    return pl.pallas_call(
        functools.partial(project_kernel, first),
        grid=(batch,),
        in_specs=[
            pl.BlockSpec((1, rows, D), lambda b: (b, 0, 0)),
            whole(vec.shape),
            whole(weight.shape),
        ],
        out_specs=pl.BlockSpec((1, rows, width), lambda b: (b, 0, 0)),
        out_shape=shape((batch, rows, width), BF16),
        compiler_params=params(1),
        cost_estimate=cost(2 * batch * rows * D * width, 2 * batch * rows * (D + width)),
        name="project",
    )(x, vec, weight)


def attend_kernel(q_ref, k_ref, v_ref, km_ref, vm_ref, own_ref, mem_ref, out_ref, prob_ref):
    keys = jnp.concatenate([km_ref[0], k_ref[0]], axis=0)
    values = jnp.concatenate([vm_ref[0], v_ref[0]], axis=0)
    for half in range(SEG // ROWS):
        width = SEG + (half + 1) * ROWS
        span = slice(half * ROWS, (half + 1) * ROWS)
        query = q_ref[0, span, :] * BF16(HD**-0.5)
        total = None
        for head in range(2):
            scores = nt(keys[:width], pair_mask(head, query))
            columns = []
            for part in range(ROWS // 128):
                block = half * (ROWS // 128) + part
                bias = jnp.concatenate(
                    [
                        mem_ref[head, (3 - block) * 128 : (7 - block) * 128, :],
                        own_ref[head, (7 - block) * 128 :, :],
                    ],
                    axis=0,
                )
                used = bias.shape[0]
                piece = scores[:used, part * 128 : (part + 1) * 128] + bias
                top = jnp.max(piece, axis=0, keepdims=True)
                weight = jnp.exp(piece - top)
                weight = (weight * (1.0 / jnp.sum(weight, axis=0, keepdims=True))).astype(BF16)
                if used < width:
                    weight = jnp.concatenate(
                        [weight, jnp.zeros((width - used, 128), BF16)], axis=0
                    )
                columns.append(weight)
            probs = jnp.concatenate(columns, axis=1)
            prob_ref[0, head, :width, span] = probs
            product = tn(probs, pair_mask(head, values)[:width])
            total = product if total is None else total + product
        out_ref[0, span, :] = total.astype(BF16)


def attend(joined, memory, own_bias, mem_bias):
    batch = joined.shape[0]
    pairs = H // 2

    def lanes(offset):
        return pl.BlockSpec((1, SEG, 128), lambda b, h: (b, 0, offset + h))

    bias = pl.BlockSpec((2, 2 * SEG, 128), lambda b, h: (h, 0, 0))
    work = batch * H * SEG * 2 * SEG
    return pl.pallas_call(
        attend_kernel,
        grid=(batch, pairs),
        in_specs=[lanes(0), lanes(pairs), lanes(2 * pairs), lanes(0), lanes(pairs), bias, bias],
        out_specs=[
            lanes(0),
            pl.BlockSpec((1, 2, 2 * SEG, SEG), lambda b, h: (b, h, 0, 0)),
        ],
        out_shape=[shape((batch, SEG, D), BF16), shape((batch, H, 2 * SEG, SEG), BF16)],
        compiler_params=params(2),
        cost_estimate=cost(16 * HD * work, 3 * work, work),
        name="attend",
    )(joined, joined, joined, memory, memory, own_bias, mem_bias)


def attend_back_kernel(
    q_ref, k_ref, v_ref, km_ref, vm_ref, grad_ref, out_ref, prob_ref,
    dq_ref, dk_ref, dv_ref, dkm_ref, dvm_ref, diag_ref, grid_ref,
):
    keys = jnp.concatenate([km_ref[0], k_ref[0]], axis=0)
    values = jnp.concatenate([vm_ref[0], v_ref[0]], axis=0)
    step = pl.program_id(1)

    @pl.when(step == 0)
    def _():
        grid_ref[...] = jnp.zeros_like(grid_ref)

    key_parts = []
    value_parts = []
    for half in range(SEG // ROWS):
        width = SEG + (half + 1) * ROWS
        span = slice(half * ROWS, (half + 1) * ROWS)
        grad = grad_ref[0, span, :]
        query = q_ref[0, span, :] * BF16(HD**-0.5)
        product = (grad.astype(F32) * out_ref[0, span, :].astype(F32)).T
        query_total = key_total = value_total = None
        for head in range(2):
            grad_head = pair_mask(head, grad)
            delta = jnp.sum(product[head * HD : (head + 1) * HD], axis=0, keepdims=True)
            probs = prob_ref[0, head, :width, span]
            scored = probs.astype(F32) * (nt(values[:width], grad_head) - delta)
            for part in range(ROWS // 128):
                block = half * (ROWS // 128) + part
                used = SEG + (block + 1) * 128
                grid_ref[head, (3 - block) * 128 :, :] += scored[
                    :used, part * 128 : (part + 1) * 128
                ]
            scored = scored.astype(BF16)
            for_key = nn(scored, pair_mask(head, query))
            for_value = nn(probs, grad_head)
            for_query = tn(scored, pair_mask(head, keys)[:width])
            key_total = for_key if key_total is None else key_total + for_key
            value_total = for_value if value_total is None else value_total + for_value
            query_total = for_query if query_total is None else query_total + for_query
        dq_ref[0, span, :] = (query_total * HD**-0.5).astype(BF16)
        key_parts.append(key_total)
        value_parts.append(value_total)
    for pieces, mem_ref, own_ref in (
        (key_parts, dkm_ref, dk_ref),
        (value_parts, dvm_ref, dv_ref),
    ):
        both = pieces[0] + pieces[1][: SEG + ROWS]
        mem_ref[0] = both[:SEG].astype(BF16)
        own_ref[0, :ROWS] = both[SEG:].astype(BF16)
        own_ref[0, ROWS:] = pieces[1][SEG + ROWS :].astype(BF16)

    @pl.when(step == pl.num_programs(1) - 1)
    def _():
        for head in range(2):
            line = jnp.concatenate(
                [grid_ref[head].T, jnp.zeros((128, SPAN - 2 * SEG), F32)], axis=1
            )
            row = lax.broadcasted_iota(jnp.int32, line.shape, 0)
            for bit in range(7):
                moved = pltpu.roll(line, SPAN - (1 << bit), 1)
                odd = jnp.bitwise_and(lax.shift_right_logical(row, bit), 1) == 1
                line = jnp.where(odd, moved, line)
            diag_ref[0, head : head + 1, :] = rows_sum(line)


def attend_back(joined, memory, grad, attended, probs):
    batch = joined.shape[0]
    pairs = H // 2

    def lanes(offset):
        return pl.BlockSpec((1, SEG, 128), lambda h, b: (b, 0, offset + h))

    half = shape((batch, SEG, D), BF16)
    work = batch * H * SEG * 2 * SEG
    return pl.pallas_call(
        attend_back_kernel,
        grid=(pairs, batch),
        in_specs=[lanes(0), lanes(pairs), lanes(2 * pairs), lanes(0), lanes(pairs)]
        + [lanes(0)] * 2
        + [pl.BlockSpec((1, 2, 2 * SEG, SEG), lambda h, b: (b, h, 0, 0))],
        out_specs=[lanes(0)] * 5 + [pl.BlockSpec((1, 2, SPAN), lambda h, b: (h, 0, 0))],
        out_shape=[half] * 5 + [shape((pairs, 2, SPAN), F32)],
        scratch_shapes=[pltpu.VMEM((2, 2 * SEG, 128), F32)],
        compiler_params=params(2),
        cost_estimate=cost(32 * HD * work, 3 * work),
        name="attend_back",
    )(joined, joined, joined, memory, memory, grad, attended, probs)


def feed_kernel(
    x_ref, att_ref, vec_ref, merge_ref, expand_ref, reduce_ref, nq_ref,
    after_attn_ref, active_ref, slope_ref, after_ffn_ref, query_ref,
):
    after_attn = x_ref[...].astype(F32) + nn(att_ref[...], merge_ref[...])
    after_attn_ref[...] = after_attn
    hat_value, _ = norm(after_attn)
    normed = (hat_value * vec_ref[2:3, :D] + vec_ref[3:4, :D]).astype(BF16)
    pre = nn(normed, expand_ref[...]) + vec_ref[6:7, :]
    cdf = 0.5 * (1.0 + lax.erf(pre * (1.0 / math.sqrt(2.0))))
    slope = cdf + pre * jnp.exp(-0.5 * pre * pre) * (1.0 / math.sqrt(2.0 * math.pi))
    slope_ref[...] = slope.astype(BF16)
    active = (pre * cdf).astype(BF16)
    active_ref[...] = active
    after_ffn = after_attn + nn(active, reduce_ref[...]) + vec_ref[4:5, :D]
    after_ffn_ref[...] = after_ffn
    query_ref[...] = nn(after_ffn.astype(BF16), nq_ref[...]).astype(BF16)


def feed(x, attended, vec, merge, expand, reduce, near_query):
    count = x.shape[0]
    ff = expand.shape[1]

    def rows(width):
        return pl.BlockSpec((ROWS, width), lambda i: (i, 0))

    return pl.pallas_call(
        feed_kernel,
        grid=(count // ROWS,),
        in_specs=[rows(D), rows(D)]
        + [whole(w.shape) for w in (vec, merge, expand, reduce, near_query)],
        out_specs=[rows(D), rows(ff), rows(ff), rows(D), rows(D)],
        out_shape=[
            shape((count, D), F32),
            shape((count, ff), BF16),
            shape((count, ff), BF16),
            shape((count, D), F32),
            shape((count, D), BF16),
        ],
        compiler_params=params(1),
        cost_estimate=cost(4 * count * D * (ff + D), 12 * count * ff, 2 * count * ff),
        name="feed",
    )(x, attended, vec, merge, expand, reduce, near_query)


def add_rows(ref, row, values):
    ref[row : row + 1, : values.shape[1]] += values


def scatter_rows(place_ref, total_ref, near_ref, far_ref, start, chunks):
    steps, rows = near_ref.shape[0], near_ref.shape[1]
    width = total_ref.shape[1]
    for core_step, ref in ((0, near_ref), (1, far_ref)):
        for step in range(steps):
            owner = device_of(place_ref, step, core_step)
            for chunk in range(chunks):
                source = pl.multiple_of((owner * chunks + chunk) * rows, rows)
                column = start + chunk * width
                ref[step, :, column : column + width] = total_ref[
                    pl.ds(source, rows), :
                ].astype(BF16)
    return start + chunks * width


def feed_back_kernel(
    place_ref, grad_ref, after_ref, active_ref, slope_ref, att_ref, vec_ref,
    merge_ref, expand_ref, reduce_ref,
    after_grad_ref, att_grad_ref, small_ref, near_ref, far_ref,
    expand_total, reduce_total, merge_total,
):
    step = pl.program_id(0)

    @pl.when(step == 0)
    def _():
        expand_total[...] = jnp.zeros_like(expand_total)
        reduce_total[...] = jnp.zeros_like(reduce_total)
        merge_total[...] = jnp.zeros_like(merge_total)
        small_ref[...] = jnp.zeros_like(small_ref)

    grad = grad_ref[...]
    low = grad.astype(BF16)
    add_rows(small_ref, 2, rows_sum(low.astype(F32)))
    reduce_total[...] += tn(active_ref[...], low)
    pre_grad = (nt(low, reduce_ref[...]) * slope_ref[...].astype(F32)).astype(BF16)
    add_rows(small_ref, 3, rows_sum(pre_grad.astype(F32)))
    hat_value, rstd_value = norm(after_ref[...])
    gain = vec_ref[2:3, :D]
    normed = (hat_value * gain + vec_ref[3:4, :D]).astype(BF16)
    expand_total[...] += tn(normed, pre_grad)
    normed_grad = nt(pre_grad, expand_ref[...])
    add_rows(small_ref, 0, rows_sum(normed_grad * hat_value))
    add_rows(small_ref, 1, rows_sum(normed_grad))
    after_grad = grad + norm_back(normed_grad, hat_value, rstd_value, gain)
    after_grad_ref[...] = after_grad
    merge_grad = after_grad.astype(BF16)
    merge_total[...] += tn(att_ref[...], merge_grad)
    att_grad_ref[...] = nt(merge_grad, merge_ref[...]).astype(BF16)

    @pl.when(step == pl.num_programs(0) - 1)
    def _():
        start = scatter_rows(place_ref, expand_total, near_ref, far_ref, 0, 1)
        ratio = reduce_total.shape[0] // D
        start = scatter_rows(place_ref, reduce_total, near_ref, far_ref, start, ratio)
        scatter_rows(place_ref, merge_total, near_ref, far_ref, start, 1)


def feed_back(place, devices, grad, after_attn, active, slope, attended, vec, merge, expand, reduce):
    count = grad.shape[0]
    ff = expand.shape[1]

    def rows(width):
        return pl.BlockSpec((ROWS, width), lambda i: (i, 0))

    packed = (devices // 2, D // devices, 2 * ff + D)
    return pl.pallas_call(
        feed_back_kernel,
        grid=(count // ROWS,),
        in_specs=[scalars(), rows(D), rows(D), rows(ff), rows(ff), rows(D)]
        + [whole(w.shape) for w in (vec, merge, expand, reduce)],
        out_specs=[rows(D), rows(D), whole((8, ff)), whole(packed), whole(packed)],
        out_shape=[
            shape((count, D), F32),
            shape((count, D), BF16),
            shape((8, ff), F32),
            shape(packed, BF16),
            shape(packed, BF16),
        ],
        scratch_shapes=[
            pltpu.VMEM((D, ff), F32),
            pltpu.VMEM((ff, D), F32),
            pltpu.VMEM((D, D), F32),
        ],
        compiler_params=params(1),
        cost_estimate=cost(8 * count * D * (ff + D // 2), 16 * count * ff),
        name="feed_back",
    )(place, grad, after_attn, active, slope, attended, vec, merge, expand, reduce)


def take_kernel(started, place_ref, ids_ref, rows_ref, *refs):
    out_ref = refs[-1]
    base = place_ref[1] * SEG
    ids = ids_ref[0] - base
    place = lax.broadcasted_iota(jnp.int32, (SEG, SEG), 1)
    rows = rows_ref[0]
    for slot in range(K):
        chosen = jnp.where(ids[:, slot : slot + 1] == place, 1.0, 0.0).astype(BF16)
        taken = nn(chosen, rows)
        if started:
            taken = taken + refs[0][0, slot].astype(F32)
        out_ref[0, slot] = taken.astype(BF16)


def take(place, ids, rows, so_far):
    batch = ids.shape[0]
    block = pl.BlockSpec((1, K, SEG, D), lambda b: (b, 0, 0, 0))
    started = so_far is not None
    return pl.pallas_call(
        functools.partial(take_kernel, started),
        grid=(batch,),
        in_specs=[
            scalars(),
            pl.BlockSpec((1, SEG, K), lambda b: (b, 0, 0)),
            pl.BlockSpec((1, SEG, D), lambda b: (b, 0, 0)),
        ]
        + [block] * started,
        out_specs=block,
        out_shape=shape((batch, K, SEG, D), BF16),
        input_output_aliases={3: 0} if started else {},
        compiler_params=params(1),
        cost_estimate=cost(2 * batch * K * SEG * SEG * D, 4 * batch * K * SEG * D),
        name="take",
    )(place, ids, rows, *([so_far] if started else []))


def give_kernel(started, place_ref, ids_ref, grad_ref, *refs):
    out_ref = refs[-1]
    base = place_ref[1] * SEG
    ids = ids_ref[0] - base
    place = lax.broadcasted_iota(jnp.int32, (SEG, SEG), 0)
    total = None
    for slot in range(K):
        chosen = jnp.where(ids[slot : slot + 1, :] == place, 1.0, 0.0).astype(BF16)
        part = nn(chosen, grad_ref[0, slot])
        total = part if total is None else total + part
    if started:
        total = total + refs[0][0].astype(F32)
    out_ref[0] = total.astype(out_ref.dtype)


def give(place, ids, grads, arrived, dtype):
    batch = ids.shape[0]
    block = pl.BlockSpec((1, SEG, D), lambda b: (b, 0, 0))
    started = arrived is not None
    return pl.pallas_call(
        functools.partial(give_kernel, started),
        grid=(batch,),
        in_specs=[
            scalars(),
            pl.BlockSpec((1, K, SEG), lambda b: (b, 0, 0)),
            pl.BlockSpec((1, K, SEG, D), lambda b: (b, 0, 0, 0)),
        ]
        + [block] * started,
        out_specs=block,
        out_shape=shape((batch, SEG, D), dtype),
        compiler_params=params(1),
        cost_estimate=cost(2 * batch * K * SEG * SEG * D, 2 * batch * K * SEG * D),
        name="give",
    )(place, ids, grads, *([arrived] if started else []))


def near_kernel(
    place_ref, rows_ref, query_ref, after_ref, grad_ref, vec_ref, keys_ref, merge_ref, nq_ref,
    out_ref, row_grad_ref, after_grad_ref, small_ref, near_ref, far_ref,
    keys_total, merge_total, query_total,
):
    first = (pl.program_id(0) == 0) & (pl.program_id(1) == 0)
    last = (pl.program_id(0) == pl.num_programs(0) - 1) & (
        pl.program_id(1) == pl.num_programs(1) - 1
    )

    @pl.when(first)
    def _():
        keys_total[...] = jnp.zeros_like(keys_total)
        merge_total[...] = jnp.zeros_like(merge_total)
        query_total[...] = jnp.zeros_like(query_total)
        small_ref[...] = jnp.zeros_like(small_ref)

    row = lax.broadcasted_iota(jnp.int32, (D, D), 0)
    column = lax.broadcasted_iota(jnp.int32, (D, D), 1)
    same_head = jnp.where(
        lax.shift_right_logical(row, 6) == lax.shift_right_logical(column, 6), 1.0, 0.0
    ).astype(BF16)
    scale = HD**-0.5
    query = query_ref[0]
    query_float = query.astype(F32)
    pairs = [nn(rows_ref[0, slot], keys_ref[...]).astype(BF16) for slot in range(K)]
    near_key = [pair[:, :D].astype(F32) for pair in pairs]
    near_value = [pair[:, D:].astype(F32) for pair in pairs]
    scores = [nn((query_float * key).astype(BF16), same_head) * scale for key in near_key]
    top = functools.reduce(jnp.maximum, scores)
    weights = [jnp.exp(score - top) for score in scores]
    inverse = 1.0 / functools.reduce(jnp.add, weights)
    probs = [weight * inverse for weight in weights]
    mixed = functools.reduce(jnp.add, [p * v for p, v in zip(probs, near_value)]).astype(BF16)
    near_out = nn(mixed, merge_ref[...])
    after_ffn = after_ref[0]
    gate_vector = vec_ref[5:6, :D]
    gate = jax.nn.sigmoid(jnp.sum(after_ffn * gate_vector, axis=-1, keepdims=True))
    out_ref[0] = (gate * after_ffn + (1.0 - gate) * near_out).astype(BF16)
    grad = grad_ref[0].astype(F32)
    gate_grad = (
        jnp.sum(grad * (after_ffn - near_out), axis=-1, keepdims=True) * gate * (1.0 - gate)
    )
    add_rows(small_ref, 0, rows_sum(gate_grad * after_ffn))
    near_grad = ((1.0 - gate) * grad).astype(BF16)
    merge_total[...] += tn(mixed, near_grad)
    mixed_grad = nt(near_grad, merge_ref[...]).astype(BF16).astype(F32)
    prob_grads = [nn((mixed_grad * value).astype(BF16), same_head) for value in near_value]
    inner = functools.reduce(jnp.add, [p * g for p, g in zip(probs, prob_grads)])
    query_grad = None
    for slot in range(K):
        score_grad = probs[slot] * (prob_grads[slot] - inner) * scale
        part = score_grad * near_key[slot]
        query_grad = part if query_grad is None else query_grad + part
        pair_grad = jnp.concatenate(
            [(score_grad * query_float).astype(BF16), (probs[slot] * mixed_grad).astype(BF16)],
            axis=1,
        )
        keys_total[...] += tn(rows_ref[0, slot], pair_grad)
        row_grad_ref[0, slot] = nt(pair_grad, keys_ref[...]).astype(BF16)
    query_grad = query_grad.astype(BF16)
    query_total[...] += tn(after_ffn.astype(BF16), query_grad)
    after_grad_ref[0] = gate * grad + gate_grad * gate_vector + nt(query_grad, nq_ref[...])

    @pl.when(last)
    def _():
        start = scatter_rows(place_ref, query_total, near_ref, far_ref, 0, 1)
        start = scatter_rows(place_ref, keys_total, near_ref, far_ref, start, 1)
        scatter_rows(place_ref, merge_total, near_ref, far_ref, start, 1)


def near(place, devices, rows, query, after_ffn, grad, vec, near_keys, near_merge, near_query):
    batch = rows.shape[0]
    row_block = pl.BlockSpec((1, K, ROWS, D), lambda b, i: (b, 0, i, 0))
    block = pl.BlockSpec((1, ROWS, D), lambda b, i: (b, i, 0))
    packed = (devices // 2, D // devices, 4 * D)
    count = batch * SEG
    return pl.pallas_call(
        near_kernel,
        grid=(batch, SEG // ROWS),
        in_specs=[scalars(), row_block, block, block, block]
        + [whole(w.shape) for w in (vec, near_keys, near_merge, near_query)],
        out_specs=[block, row_block, block, whole((8, D)), whole(packed), whole(packed)],
        out_shape=[
            shape((batch, SEG, D), BF16),
            shape((batch, K, SEG, D), BF16),
            shape((batch, SEG, D), F32),
            shape((8, D), F32),
            shape(packed, BF16),
            shape(packed, BF16),
        ],
        scratch_shapes=[
            pltpu.VMEM((D, 2 * D), F32),
            pltpu.VMEM((D, D), F32),
            pltpu.VMEM((D, D), F32),
        ],
        compiler_params=params(2),
        cost_estimate=cost(
            2 * count * D * D * (8 * K + 5), count * D * (4 * K + 12), count * K * D
        ),
        name="near",
    )(place, rows, query, after_ffn, grad, vec, near_keys, near_merge, near_query)


def finish_kernel(
    parts, place_ref, x_ref, before_ref, dq_ref, dk_ref, dv_ref, dkm_ref, dvm_ref, grad_ref,
    own_ref, sent_ref, vec_ref, w_ref, gate_ref, feed_ref, diag_ref, select_ref,
    part_ref, send_ref, near_ref, far_ref,
    w_total, norm_total, small_total,
):
    step = pl.program_id(0)

    @pl.when(step == 0)
    def _():
        w_total[...] = jnp.zeros_like(w_total)
        norm_total[...] = jnp.zeros_like(norm_total)

    gain = vec_ref[0:1, :D]
    shift = vec_ref[1:2, :D]
    hat_value, rstd_value = norm(x_ref[0].astype(F32))
    normed = (hat_value * gain + shift).astype(BF16)
    hat_before, rstd_before = norm(before_ref[0].astype(F32))
    normed_before = (hat_before * gain + shift).astype(BF16)
    w_total[:, :D] += tn(normed, dq_ref[0])
    w_total[:, D : 2 * D] += tn(normed, dk_ref[0]) + tn(normed_before, dkm_ref[0])
    w_total[:, 2 * D :] += tn(normed, dv_ref[0]) + tn(normed_before, dvm_ref[0])
    normed_grad = (
        nt(dq_ref[0], w_ref[:, :D])
        + nt(dk_ref[0], w_ref[:, D : 2 * D])
        + nt(dv_ref[0], w_ref[:, 2 * D :])
    )
    before_grad = nt(dkm_ref[0], w_ref[:, D : 2 * D]) + nt(dvm_ref[0], w_ref[:, 2 * D :])
    add_rows(norm_total, 0, rows_sum(normed_grad * hat_value) + rows_sum(before_grad * hat_before))
    add_rows(norm_total, 1, rows_sum(normed_grad) + rows_sum(before_grad))
    send_ref[0] = (
        sent_ref[0].astype(F32) + norm_back(before_grad, hat_before, rstd_before, gain)
    ).astype(BF16)
    part_ref[0] = (
        grad_ref[0] + own_ref[0] + norm_back(normed_grad, hat_value, rstd_value, gain)
    )

    @pl.when(step == pl.num_programs(0) - 1)
    def _():
        devices = small_total.shape[0]
        rows = w_total.shape[0] // devices
        small_total[...] = jnp.zeros_like(small_total)
        lines = [
            norm_total[0:1, :],
            norm_total[1:2, :],
            feed_ref[0:1, :D],
            feed_ref[1:2, :D],
            feed_ref[2:3, :D],
            gate_ref[0:1, :],
            feed_ref[3:4, :],
        ]
        start = 0
        for line, width in zip(lines, parts):
            for d in range(devices):
                small_total[d : d + 1, start : start + width] = line[
                    :, d * width : (d + 1) * width
                ]
            start += width
        table = lax.dot_general(
            diag_ref[...],
            select_ref[...],
            (((1,), (0,)), ((), ())),
            precision=HIGH,
            preferred_element_type=F32,
        )
        own_buckets = NB // devices
        bucket = lax.broadcasted_iota(jnp.int32, (devices, NB), 1)
        owner = lax.broadcasted_iota(jnp.int32, (devices, NB), 0)
        for place in range(own_buckets):
            chosen = jnp.where(bucket == owner * own_buckets + place, 1.0, 0.0)
            small_total[:, start : start + H] = lax.dot_general(
                chosen,
                table,
                (((1,), (1,)), ((), ())),
                precision=HIGH,
                preferred_element_type=F32,
            )
            start += H
        width = small_total.shape[1]
        for core_step, ref in ((0, near_ref), (1, far_ref)):
            for chip_step in range(ref.shape[0]):
                target = device_of(place_ref, chip_step, core_step)
                source = pl.multiple_of(target * rows, rows)
                ref[chip_step, :rows, :] = w_total[pl.ds(source, rows), :].astype(BF16)
                ref[chip_step, rows:, :] = jnp.zeros((16, ref.shape[2]), BF16)
                line = small_total[pl.ds(target, 1), :]
                ref[chip_step, rows : rows + 16, :width] = jnp.broadcast_to(
                    line, (16, width)
                ).astype(BF16)


def finish(
    place, devices, parts, x, before, pieces, grad, own, sent, vec, weight, gate, feed_small, diag
):
    batch = x.shape[0]
    block = pl.BlockSpec((1, SEG, D), lambda b: (b, 0, 0))
    packed = (devices // 2, D // devices + 16, 3 * D)
    select = jnp.asarray(backward_selector())
    small_width = -(-(sum(parts) + NB * H // devices) // 128) * 128
    return pl.pallas_call(
        functools.partial(finish_kernel, parts),
        grid=(batch,),
        in_specs=[scalars()]
        + [block] * 10
        + [whole(w.shape) for w in (vec, weight, gate, feed_small, diag, select)],
        out_specs=[block, block, whole(packed), whole(packed)],
        out_shape=[
            shape((batch, SEG, D), F32),
            shape((batch, SEG, D), BF16),
            shape(packed, BF16),
            shape(packed, BF16),
        ],
        scratch_shapes=[
            pltpu.VMEM((D, 3 * D), F32),
            pltpu.VMEM((8, D), F32),
            pltpu.VMEM((devices, small_width), F32),
        ],
        compiler_params=params(1),
        cost_estimate=cost(20 * batch * SEG * D * D, 30 * batch * SEG * D),
        name="finish",
    )(
        place, x, before, *pieces, grad, own, sent, vec, weight, gate, feed_small, diag, select
    )


def shift_up(block, distance):
    count = lax.axis_size("seq")
    route = [(i, i + distance) for i in range(count) if 0 <= i + distance < count]
    return lax.ppermute(block, "seq", route)


def swap(block, axis, bits):
    count = lax.axis_size(axis)
    return lax.ppermute(block, axis, [(i, i ^ bits) for i in range(count)])


def gather_weight(place, shard, layout):
    steps = lax.axis_size("fsdp") // 2
    pieces = [shard] + [swap(shard, "fsdp", 2 * step) for step in range(1, steps)]
    near_half = jnp.stack(pieces)
    far_half = swap(near_half, "fsdp", 1)
    return assemble(place, near_half, far_half, layout)


def reduce_weight(near_half, far_half):
    steps = lax.axis_size("fsdp") // 2
    arrived = swap(far_half, "fsdp", 1)
    pieces = [
        (near_half[step].astype(F32) + arrived[step].astype(F32)).astype(BF16)
        for step in range(steps)
    ]
    total = pieces[0].astype(F32)
    for step in range(1, steps):
        total = total + swap(pieces[step], "fsdp", 2 * step).astype(F32)
    bits = 1
    while bits < lax.axis_size("seq"):
        low = total.astype(BF16)
        total = low.astype(F32) + swap(low, "seq", bits).astype(F32)
        bits *= 2
    return total


def on_device(
    layer_input,
    neighbour_ids,
    out_grad,
    attn_norm_gain,
    attn_norm_bias,
    attn_project,
    attn_merge,
    position_bias,
    ffn_norm_gain,
    ffn_norm_bias,
    ffn_expand,
    expand_bias,
    ffn_reduce,
    reduce_bias,
    near_query,
    near_keys,
    near_merge,
    gate_vector,
):
    batch = layer_input.shape[0]
    count = batch * SEG
    devices = lax.axis_size("fsdp")
    segments = lax.axis_size("seq")
    seg_index = lax.axis_index("seq")
    rows = attn_project.shape[0]
    ff = ffn_expand.shape[1]
    ratio = ff // D

    def place_of(segment):
        return jnp.stack([lax.axis_index("fsdp"), segment]).astype(jnp.int32)

    place = place_of(seg_index)
    states = [layer_input]
    for _ in range(1, segments):
        states.append(shift_up(states[-1], 1))
    vectors = [
        attn_norm_gain, attn_norm_bias, ffn_norm_gain, ffn_norm_bias, reduce_bias, gate_vector,
        expand_bias, position_bias,
    ]
    parts = [v.shape[0] for v in vectors[:-1]]
    filled = sum(parts)
    own_bias_width = position_bias.shape[0]
    padding = -(filled + own_bias_width) % 128
    small = jnp.concatenate(vectors + [jnp.zeros((padding,), BF16)])[None]
    small = lax.all_gather(small, "fsdp", axis=0, tiled=True)
    table = small[:, filled : filled + own_bias_width].reshape(NB, H).T.astype(F32)
    (attn_w,) = gather_weight(place, attn_project, ((1, 3 * D),))
    reduce_columns = ffn_reduce.reshape(ratio, rows, D).transpose(1, 0, 2).reshape(rows, ff)
    merge_w, expand_w, reduce_w = gather_weight(
        place,
        jnp.concatenate([attn_merge, ffn_expand, reduce_columns], axis=1),
        ((1, D), (1, ff), (ratio, D)),
    )
    query_w, keys_w, near_merge_w = gather_weight(
        place,
        jnp.concatenate([near_query, near_keys, near_merge], axis=1),
        ((1, D), (1, 2 * D), (1, D)),
    )
    near_rows = None
    for distance in range(segments):
        near_rows = take(
            place_of(seg_index - distance), neighbour_ids, states[distance], near_rows
        )
    vec, own_bias, mem_bias = prep(place, small, table, parts, ff)
    joined = project(layer_input, vec, attn_w, 0)
    before = states[1]
    memory = project(before, vec, attn_w, D)
    attended, probs = attend(joined, memory, own_bias, mem_bias)
    flat_attended = attended.reshape(count, D)
    after_attn, active, slope, after_ffn, queries = feed(
        layer_input.reshape(count, D), flat_attended, vec, merge_w, expand_w, reduce_w, query_w
    )
    output, row_grads, after_grad, gate_small, near_half, far_half = near(
        place, devices, near_rows, queries.reshape(batch, SEG, D),
        after_ffn.reshape(batch, SEG, D), out_grad, vec, keys_w, near_merge_w, query_w,
    )
    near_total = reduce_weight(near_half, far_half)
    ids_across = jnp.swapaxes(neighbour_ids, 1, 2)
    arrived = None
    for distance in range(segments - 1, 0, -1):
        message = give(place_of(seg_index - distance), ids_across, row_grads, arrived, BF16)
        if distance > 1:
            arrived = shift_up(message, -1)
    own = give(place, ids_across, row_grads, None, F32)
    grad_after, att_grad, feed_small, near_half, far_half = feed_back(
        place, devices, after_grad.reshape(count, D), after_attn, active, slope, flat_attended,
        vec, merge_w, expand_w, reduce_w,
    )
    feed_total = reduce_weight(near_half, far_half)
    *pieces, diag = attend_back(
        joined, memory, att_grad.reshape(batch, SEG, D), attended, probs
    )
    partial, message, near_half, far_half = finish(
        place, devices, parts, layer_input, before, pieces, grad_after.reshape(batch, SEG, D),
        own, message, vec, attn_w, gate_small, feed_small, diag.reshape(H, SPAN),
    )
    attn_total = reduce_weight(near_half, far_half)
    input_grad = partial + shift_up(message, -1).astype(F32)
    line = attn_total[rows]
    smalls = []
    start = 0
    for width in parts + [own_bias_width]:
        smalls.append(line[start : start + width])
        start += width
    return (
        output,
        input_grad,
        smalls[0],
        smalls[1],
        attn_total[:rows],
        feed_total[:, 2 * ff :],
        smalls[7],
        smalls[2],
        smalls[3],
        feed_total[:, :ff],
        smalls[6],
        feed_total[:, ff : 2 * ff].reshape(rows, ratio, D).transpose(1, 0, 2).reshape(-1, D),
        smalls[4],
        near_total[:, :D],
        near_total[:, D : 3 * D],
        near_total[:, 3 * D :],
        smalls[5],
    )


def solution(mesh):
    in_specs = (
        P("fsdp", "seq", None),
        P("fsdp", "seq", None),
        P("fsdp", "seq", None),
        P("fsdp"),
        P("fsdp"),
        P("fsdp", None),
        P("fsdp", None),
        P("fsdp"),
        P("fsdp"),
        P("fsdp"),
        P("fsdp", None),
        P("fsdp"),
        P("fsdp", None),
        P("fsdp"),
        P("fsdp", None),
        P("fsdp", None),
        P("fsdp", None),
        P("fsdp"),
    )
    out_specs = (
        P("fsdp", "seq", None),
        P("fsdp", "seq", None),
        P("fsdp"),
        P("fsdp"),
        P("fsdp", None),
        P("fsdp", None),
        P("fsdp"),
        P("fsdp"),
        P("fsdp"),
        P("fsdp", None),
        P("fsdp"),
        P("fsdp", None),
        P("fsdp"),
        P("fsdp", None),
        P("fsdp", None),
        P("fsdp", None),
        P("fsdp"),
    )
    return jax.shard_map(
        on_device, mesh=mesh, in_specs=in_specs, out_specs=out_specs, check_vma=False
    )
```

```python
import functools
import math

import jax
import jax.numpy as jnp
import numpy as np
from jax import lax
from jax.experimental import pallas as pl
from jax.experimental.pallas import tpu as pltpu
from jax.sharding import PartitionSpec as P

D = 512
H = 8
HD = 64
K = 4
SEG = 512
NB = 32

EPS = 1e-05
HIGH = lax.Precision.HIGHEST
MASKED = -1e30
F32 = jnp.float32
BF16 = jnp.bfloat16
ROWS = 256
SPAN = 2 * SEG + 128
VMEM = 56 << 20


def nn(left, right):
    return lax.dot_general(left, right, (((1,), (0,)), ((), ())), preferred_element_type=F32)


def nt(left, right):
    return lax.dot_general(left, right, (((1,), (1,)), ((), ())), preferred_element_type=F32)


def tn(left, right):
    return lax.dot_general(left, right, (((0,), (0,)), ((), ())), preferred_element_type=F32)


def shape(dims, dtype):
    return jax.ShapeDtypeStruct(tuple(dims), dtype)


def whole(dims):
    zeros = (0,) * len(dims)
    return pl.BlockSpec(tuple(dims), lambda *_: zeros, pipeline_mode=pl.Buffered(1))


def scalars():
    return pl.BlockSpec(memory_space=pltpu.SMEM)


def params(grid_rank):
    return pltpu.CompilerParams(
        dimension_semantics=("arbitrary",) * grid_rank, vmem_limit_bytes=VMEM
    )


def cost(flops, moved, exps=0):
    return pl.CostEstimate(
        flops=int(flops / 30), bytes_accessed=int(moved / 30), transcendentals=int(exps / 30)
    )


def thresholds():
    half_count = NB // 2
    spread_ratio = 2.0 * SEG / half_count
    exact_part = list(range(1, half_count))
    log_part = [
        int(half_count * spread_ratio ** ((bucket_index - half_count) / half_count))
        for bucket_index in range(half_count, NB)
    ]
    return np.array(exact_part + log_part)


def bucket_of(distance):
    return (distance[:, None] >= thresholds()[None, :]).sum(axis=1)


def forward_selector():
    distance = np.arange(SPAN) - 128
    bucket = bucket_of(np.maximum(distance, 0))
    return (np.arange(NB)[:, None] == bucket[None, :]).astype(np.float32)


def backward_selector():
    chosen = forward_selector().T.copy()
    chosen[:128] = 0.0
    return chosen


def norm(values):
    average = jnp.mean(values, axis=-1, keepdims=True)
    centred = values - average
    variance = jnp.mean(centred * centred, axis=-1, keepdims=True)
    rstd_value = lax.rsqrt(variance + EPS)
    return centred * rstd_value, rstd_value


def norm_back(grad_result, hat_value, rstd_value, gain):
    scaled = grad_result * gain
    return rstd_value * (
        scaled
        - jnp.mean(scaled, axis=-1, keepdims=True)
        - hat_value * jnp.mean(scaled * hat_value, axis=-1, keepdims=True)
    )


def rows_sum(values):
    return jnp.sum(values, axis=0, keepdims=True)


def pair_mask(head, values):
    lane = lax.broadcasted_iota(jnp.int32, values.shape, 1)
    keep = lane < HD if head == 0 else lane >= HD
    return jnp.where(keep, values, jnp.zeros_like(values))


def pack_first_kernel(*refs):
    weight_ref, *vector_refs, out_ref = refs
    rows = weight_ref.shape[0]
    out_ref[:rows, :] = weight_ref[...]
    out_ref[rows:, :] = jnp.zeros((16, out_ref.shape[1]), BF16)
    for index, ref in enumerate(vector_refs):
        line = ref[...].astype(F32).reshape(1, -1).astype(BF16)
        out_ref[rows + index : rows + index + 1, : ref.shape[0]] = line


def pack_first(weight, vectors):
    rows, columns = weight.shape
    return pl.pallas_call(
        pack_first_kernel,
        out_shape=shape((rows + 16, columns), BF16),
        cost_estimate=cost(0, 4 * rows * columns),
        name="pack_first",
    )(weight, *vectors)


def pack_kernel(rows, *refs):
    out_ref = refs[-1]
    start = 0
    for ref in refs[:-1]:
        for chunk in range(ref.shape[0] // rows):
            out_ref[:, start : start + ref.shape[1]] = ref[chunk * rows : (chunk + 1) * rows, :]
            start += ref.shape[1]


def pack(rows, weights):
    columns = sum(w.size for w in weights) // rows
    return pl.pallas_call(
        functools.partial(pack_kernel, rows),
        out_shape=shape((rows, columns), BF16),
        cost_estimate=cost(0, 4 * rows * columns),
        name="pack",
    )(*weights)


def unpack_kernel(layout, terms, *refs):
    total = functools.reduce(jnp.add, [ref[...].astype(F32) for ref in refs[:terms]])
    refs = refs[terms:]
    rows = refs[0].shape[0]
    start = 0
    for ref, (chunks, width) in zip(refs, layout):
        for chunk in range(chunks):
            ref[chunk * rows : (chunk + 1) * rows, :] = total[:rows, start : start + width]
            start += width
    for index, ref in enumerate(refs[len(layout) :]):
        ref[...] = total[rows + index : rows + index + 1, : ref.shape[0]].reshape(-1)


def unpack(pair, layout, widths=()):
    rows = pair[0].shape[0] - (16 if widths else 0)
    outs = [shape((rows * chunks, width), F32) for chunks, width in layout]
    outs += [shape((width,), F32) for width in widths]
    return pl.pallas_call(
        functools.partial(unpack_kernel, layout, len(pair)),
        out_shape=outs,
        cost_estimate=cost(0, 8 * pair[0].size),
        name="unpack",
    )(*pair)


def device_of(place_ref, chip_step, core_step):
    index = place_ref[0]
    chip = lax.shift_right_logical(index, 1)
    core = jnp.bitwise_and(index, 1)
    return jnp.bitwise_xor(chip, chip_step) * 2 + jnp.bitwise_xor(core, core_step)


def assemble(place_ref, layout, piece_refs, out_refs):
    steps = len(piece_refs) // 2
    for core_step in range(2):
        for step in range(steps):
            ref = piece_refs[core_step * steps + step]
            owner = device_of(place_ref, step, core_step)
            rows = D // (2 * steps)
            start = 0
            for out_ref, (chunks, width) in zip(out_refs, layout):
                for chunk in range(chunks):
                    target = pl.multiple_of((owner * chunks + chunk) * rows, rows)
                    out_ref[pl.ds(target, rows), :] = ref[:rows, start : start + width]
                    start += width


def first_kernel(parts, count, place_ref, x_ref, before_ref, select_ref, *refs):
    piece_refs = refs[:count]
    w_ref, vec_ref, line_ref, joined_ref, memory_ref, small_ref = refs[count:]

    @pl.when(pl.program_id(0) == 0)
    def _():
        assemble(place_ref, ((1, 3 * D),), piece_refs, [w_ref])
        steps = count // 2
        rows = D // count
        for core_step in range(2):
            for step in range(steps):
                owner = device_of(place_ref, step, core_step)
                small_ref[pl.ds(pl.multiple_of(owner * 16, 16), 16), :] = piece_refs[
                    core_step * steps + step
                ][rows:, : small_ref.shape[1]].astype(F32)
        vec_ref[...] = jnp.zeros_like(vec_ref)
        for row, width in enumerate(parts):
            pieces = [small_ref[16 * d + row : 16 * d + row + 1, :width] for d in range(count)]
            vec_ref[row : row + 1, : width * count] = jnp.concatenate(pieces, axis=1)
        row = len(parts)
        table = jnp.concatenate(
            [small_ref[16 * d + row : 16 * d + row + 1, : NB * H // count] for d in range(count)],
            axis=0,
        )
        by_distance = None
        for place in range(NB // count):
            part = lax.dot_general(
                table[:, place * H : (place + 1) * H],
                select_ref[place],
                (((0,), (0,)), ((), ())),
                precision=HIGH,
                preferred_element_type=F32,
            )
            by_distance = part if by_distance is None else by_distance + part
        lane = lax.broadcasted_iota(jnp.int32, by_distance.shape, 1)
        line_ref[...] = jnp.where(lane < 128, MASKED, by_distance)

    for ref, out_ref, first in ((x_ref, joined_ref, 0), (before_ref, memory_ref, D)):
        hat_value, _ = norm(ref[0].astype(F32))
        normed = (hat_value * vec_ref[0:1, :D] + vec_ref[1:2, :D]).astype(BF16)
        out_ref[0] = nn(normed, w_ref[:, first:]).astype(BF16)


def first(place, x, before, pieces, parts, ff):
    batch = x.shape[0]
    count = len(pieces)
    small_width = -(-max(parts) // 128) * 128
    select = forward_selector().reshape(count, NB // count, SPAN).transpose(1, 0, 2)

    def block(width):
        return pl.BlockSpec((1, SEG, width), lambda b: (b, 0, 0))

    return pl.pallas_call(
        functools.partial(first_kernel, parts, count),
        grid=(batch,),
        in_specs=[scalars(), block(D), block(D), whole(select.shape)]
        + [whole(piece.shape) for piece in pieces],
        out_specs=[whole((D, 3 * D)), whole((8, ff)), whole((H, SPAN)), block(3 * D), block(2 * D)],
        out_shape=[
            shape((D, 3 * D), BF16),
            shape((8, ff), F32),
            shape((H, SPAN), F32),
            shape((batch, SEG, 3 * D), BF16),
            shape((batch, SEG, 2 * D), BF16),
        ],
        scratch_shapes=[pltpu.VMEM((16 * count, small_width), F32)],
        compiler_params=params(1),
        cost_estimate=cost(10 * batch * SEG * D * D, 8 * batch * SEG * D),
        name="first",
    )(place, x, before, jnp.asarray(select), *pieces)


def tiles(place_ref, line_ref, first, own_ref, mem_ref):
    hidden = jnp.where(place_ref[1] > 0, 0.0, MASKED)
    for head in range(2):
        index = 2 * (first + pl.program_id(0)) + head
        line = jnp.broadcast_to(line_ref[pl.ds(index, 1), :], (8, SPAN))
        line = pltpu.roll(line, 0, 1, stride=1, stride_axis=0)
        for group in range(16):
            moved = pltpu.roll(line, 8 * group, 1) if group else line
            for tile in range(2 * SEG // 128):
                start = 2 * SEG - 128 * tile
                row = 128 * tile + 8 * group
                piece = moved[:, start : start + 128]
                own_ref[head, row : row + 8, :] = piece
                mem_ref[head, row : row + 8, :] = piece + hidden


def attend_kernel(first, place_ref, q_ref, k_ref, v_ref, km_ref, vm_ref, line_ref, *refs):
    out_ref, prob_ref, own_ref, mem_ref = refs[-4:]

    @pl.when(pl.program_id(1) == 0)
    def _():
        tiles(place_ref, line_ref, first, own_ref, mem_ref)

    keys = jnp.concatenate([km_ref[0], k_ref[0]], axis=0)
    values = jnp.concatenate([vm_ref[0], v_ref[0]], axis=0)
    for half in range(SEG // ROWS):
        width = SEG + (half + 1) * ROWS
        span = slice(half * ROWS, (half + 1) * ROWS)
        query = q_ref[0, span, :] * BF16(HD**-0.5)
        total = None
        for head in range(2):
            scores = nt(keys[:width], pair_mask(head, query))
            columns = []
            for part in range(ROWS // 128):
                block = half * (ROWS // 128) + part
                bias = jnp.concatenate(
                    [
                        mem_ref[head, (3 - block) * 128 : (7 - block) * 128, :],
                        own_ref[head, (7 - block) * 128 :, :],
                    ],
                    axis=0,
                )
                used = bias.shape[0]
                piece = scores[:used, part * 128 : (part + 1) * 128] + bias
                top = jnp.max(piece, axis=0, keepdims=True)
                weight = jnp.exp(piece - top)
                weight = (weight * (1.0 / jnp.sum(weight, axis=0, keepdims=True))).astype(BF16)
                if used < width:
                    weight = jnp.concatenate(
                        [weight, jnp.zeros((width - used, 128), BF16)], axis=0
                    )
                columns.append(weight)
            probs = jnp.concatenate(columns, axis=1)
            prob_ref[0, head, :width, span] = probs
            product = tn(probs, pair_mask(head, values)[:width])
            total = product if total is None else total + product
        out_ref[0, span, :] = total.astype(BF16)


PAIRS = H // 4


def attend(place, joined, memory, line, first, so_far):
    batch = joined.shape[0]

    def lanes(offset):
        return pl.BlockSpec((1, SEG, 128), lambda h, b: (b, 0, offset + first + h))

    work = batch * H * SEG * SEG
    extra = [] if so_far is None else [so_far]
    return pl.pallas_call(
        functools.partial(attend_kernel, first),
        grid=(PAIRS, batch),
        in_specs=[scalars()]
        + [lanes(0), lanes(2 * PAIRS), lanes(4 * PAIRS), lanes(0), lanes(2 * PAIRS)]
        + [whole(line.shape)]
        + [pl.BlockSpec(memory_space=pl.ANY)] * len(extra),
        out_specs=[
            lanes(0),
            pl.BlockSpec((1, 2, 2 * SEG, SEG), lambda h, b: (b, h, 0, 0)),
        ],
        out_shape=[shape((batch, SEG, D), BF16), shape((batch, H // 2, 2 * SEG, SEG), BF16)],
        scratch_shapes=[pltpu.VMEM((2, 2 * SEG, 128), F32)] * 2,
        input_output_aliases={7: 0} if extra else {},
        compiler_params=params(2),
        cost_estimate=cost(16 * HD * work, 3 * work, work),
        name="attend",
    )(place, joined, joined, joined, memory, memory, line, *extra)


def attend_back_kernel(
    q_ref, k_ref, v_ref, km_ref, vm_ref, grad_ref, out_ref, prob_ref, *refs
):
    dq_ref, dk_ref, dv_ref, dkm_ref, dvm_ref, diag_ref, grid_ref = refs[-7:]
    keys = jnp.concatenate([km_ref[0], k_ref[0]], axis=0)
    values = jnp.concatenate([vm_ref[0], v_ref[0]], axis=0)
    step = pl.program_id(1)

    @pl.when(step == 0)
    def _():
        grid_ref[...] = jnp.zeros_like(grid_ref)

    key_parts = []
    value_parts = []
    for half in range(SEG // ROWS):
        width = SEG + (half + 1) * ROWS
        span = slice(half * ROWS, (half + 1) * ROWS)
        grad = grad_ref[0, span, :]
        query = q_ref[0, span, :] * BF16(HD**-0.5)
        product = (grad.astype(F32) * out_ref[0, span, :].astype(F32)).T
        query_total = key_total = value_total = None
        for head in range(2):
            grad_head = pair_mask(head, grad)
            delta = jnp.sum(product[head * HD : (head + 1) * HD], axis=0, keepdims=True)
            probs = prob_ref[0, head, :width, span]
            scored = probs.astype(F32) * (nt(values[:width], grad_head) - delta)
            for part in range(ROWS // 128):
                block = half * (ROWS // 128) + part
                used = SEG + (block + 1) * 128
                grid_ref[head, (3 - block) * 128 :, :] += scored[
                    :used, part * 128 : (part + 1) * 128
                ]
            scored = scored.astype(BF16)
            for_key = nn(scored, pair_mask(head, query))
            for_value = nn(probs, grad_head)
            for_query = tn(scored, pair_mask(head, keys)[:width])
            key_total = for_key if key_total is None else key_total + for_key
            value_total = for_value if value_total is None else value_total + for_value
            query_total = for_query if query_total is None else query_total + for_query
        dq_ref[0, span, :] = (query_total * HD**-0.5).astype(BF16)
        key_parts.append(key_total)
        value_parts.append(value_total)
    for pieces, mem_ref, own_ref in (
        (key_parts, dkm_ref, dk_ref),
        (value_parts, dvm_ref, dv_ref),
    ):
        both = pieces[0] + pieces[1][: SEG + ROWS]
        mem_ref[0] = both[:SEG].astype(BF16)
        own_ref[0, :ROWS] = both[SEG:].astype(BF16)
        own_ref[0, ROWS:] = pieces[1][SEG + ROWS :].astype(BF16)

    @pl.when(step == pl.num_programs(1) - 1)
    def _():
        for head in range(2):
            total = None
            for group in range(16):
                pieces = [
                    grid_ref[head, 128 * tile + 8 * group : 128 * tile + 8 * group + 8, :]
                    for tile in reversed(range(2 * SEG // 128))
                ]
                line = jnp.concatenate([jnp.zeros((8, 128), F32)] + pieces, axis=1)
                if group:
                    line = pltpu.roll(line, SPAN - 8 * group, 1)
                total = line if total is None else total + line
            lines = [total[:1]] + [
                pltpu.roll(total[row : row + 1], SPAN - row, 1) for row in range(1, 8)
            ]
            diag_ref[0, head : head + 1, :] = functools.reduce(jnp.add, lines)


def attend_back(joined, memory, grad, attended, probs, first, so_far):
    batch = joined.shape[0]

    def lanes(offset):
        return pl.BlockSpec((1, SEG, 128), lambda h, b: (b, 0, offset + first + h))

    half = shape((batch, SEG, D), BF16)
    work = batch * H * SEG * SEG
    return pl.pallas_call(
        attend_back_kernel,
        grid=(PAIRS, batch),
        in_specs=[lanes(0), lanes(2 * PAIRS), lanes(4 * PAIRS), lanes(0), lanes(2 * PAIRS)]
        + [lanes(0)] * 2
        + [pl.BlockSpec((1, 2, 2 * SEG, SEG), lambda h, b: (b, h, 0, 0))]
        + [pl.BlockSpec(memory_space=pl.ANY)] * len(so_far),
        out_specs=[lanes(0)] * 5 + [pl.BlockSpec((1, 2, SPAN), lambda h, b: (h, 0, 0))],
        out_shape=[half] * 5 + [shape((PAIRS, 2, SPAN), F32)],
        scratch_shapes=[pltpu.VMEM((2, 2 * SEG, 128), F32)],
        input_output_aliases={8 + i: i for i in range(len(so_far))},
        compiler_params=params(2),
        cost_estimate=cost(32 * HD * work, 3 * work),
        name="attend_back",
    )(joined, joined, joined, memory, memory, grad, attended, probs, *so_far)


def feed_layout(ff):
    return ((1, D), (1, ff), (ff // D, D))


def feed_scratch(ff):
    return [pltpu.VMEM((D, D), BF16), pltpu.VMEM((D, ff), BF16), pltpu.VMEM((ff, D), BF16)]


def feed_kernel(count, place_ref, x_ref, att_ref, vec_ref, *refs):
    piece_refs = refs[:count]
    (
        after_attn_ref, active_ref, slope_ref, after_ffn_ref, merge_ref, expand_ref, reduce_ref,
    ) = refs[count:]

    @pl.when(pl.program_id(0) == 0)
    def _():
        assemble(place_ref, feed_layout(expand_ref.shape[1]), piece_refs, refs[-3:])

    after_attn = x_ref[...].astype(F32) + nn(att_ref[...], merge_ref[...])
    after_attn_ref[...] = after_attn
    hat_value, _ = norm(after_attn)
    normed = (hat_value * vec_ref[2:3, :D] + vec_ref[3:4, :D]).astype(BF16)
    pre = nn(normed, expand_ref[...]) + vec_ref[6:7, :]
    cdf = 0.5 * (1.0 + lax.erf(pre * (1.0 / math.sqrt(2.0))))
    slope = cdf + pre * jnp.exp(-0.5 * pre * pre) * (1.0 / math.sqrt(2.0 * math.pi))
    slope_ref[...] = slope.astype(BF16)
    active = (pre * cdf).astype(BF16)
    active_ref[...] = active
    after_ffn = after_attn + nn(active, reduce_ref[...]) + vec_ref[4:5, :D]
    after_ffn_ref[...] = after_ffn


def feed(place, x, attended, vec, pieces):
    count = x.shape[0]
    ff = vec.shape[1]

    def rows(width):
        return pl.BlockSpec((ROWS, width), lambda i: (i, 0))

    return pl.pallas_call(
        functools.partial(feed_kernel, len(pieces)),
        grid=(count // ROWS,),
        in_specs=[scalars(), rows(D), rows(D), whole(vec.shape)]
        + [whole(piece.shape) for piece in pieces],
        out_specs=[rows(D), rows(ff), rows(ff), rows(D)],
        out_shape=[
            shape((count, D), F32),
            shape((count, ff), BF16),
            shape((count, ff), BF16),
            shape((count, D), F32),
        ],
        scratch_shapes=feed_scratch(ff),
        compiler_params=params(1),
        cost_estimate=cost(4 * count * D * (ff + D), 12 * count * ff, 2 * count * ff),
        name="feed",
    )(place, x, attended, vec, *pieces)


def add_rows(ref, row, values):
    ref[row : row + 1, : values.shape[1]] += values


def scatter_rows(place_ref, total_ref, near_ref, far_ref, start, chunks):
    steps, rows = near_ref.shape[0], near_ref.shape[1]
    width = total_ref.shape[1]
    for core_step, ref in ((0, near_ref), (1, far_ref)):
        for step in range(steps):
            owner = device_of(place_ref, step, core_step)
            for chunk in range(chunks):
                source = pl.multiple_of((owner * chunks + chunk) * rows, rows)
                column = start + chunk * width
                ref[step, :, column : column + width] = total_ref[
                    pl.ds(source, rows), :
                ].astype(BF16)
    return start + chunks * width


def feed_back_kernel(
    count, place_ref, grad_ref, after_ref, slope_ref, att_ref, vec_ref, *refs
):
    piece_refs = refs[:count]
    (
        after_grad_ref, att_grad_ref, small_ref, near_ref, far_ref,
        expand_total, merge_total, merge_ref, expand_ref, reduce_ref,
    ) = refs[count:]
    step = pl.program_id(0)

    @pl.when(step == 0)
    def _():
        assemble(place_ref, feed_layout(expand_ref.shape[1]), piece_refs, refs[-3:])
        expand_total[...] = jnp.zeros_like(expand_total)
        merge_total[...] = jnp.zeros_like(merge_total)
        small_ref[...] = jnp.zeros_like(small_ref)

    grad = grad_ref[...]
    low = grad.astype(BF16)
    add_rows(small_ref, 2, rows_sum(low.astype(F32)))
    pre_grad = (nt(low, reduce_ref[...]) * slope_ref[...].astype(F32)).astype(BF16)
    add_rows(small_ref, 3, rows_sum(pre_grad.astype(F32)))
    hat_value, rstd_value = norm(after_ref[...])
    gain = vec_ref[2:3, :D]
    normed = (hat_value * gain + vec_ref[3:4, :D]).astype(BF16)
    expand_total[...] += tn(normed, pre_grad)
    normed_grad = nt(pre_grad, expand_ref[...])
    add_rows(small_ref, 0, rows_sum(normed_grad * hat_value))
    add_rows(small_ref, 1, rows_sum(normed_grad))
    after_grad = grad + norm_back(normed_grad, hat_value, rstd_value, gain)
    after_grad_ref[...] = after_grad
    merge_grad = after_grad.astype(BF16)
    merge_total[...] += tn(att_ref[...], merge_grad)
    att_grad_ref[...] = nt(merge_grad, merge_ref[...]).astype(BF16)

    @pl.when(step == pl.num_programs(0) - 1)
    def _():
        start = scatter_rows(place_ref, expand_total, near_ref, far_ref, 0, 1)
        scatter_rows(place_ref, merge_total, near_ref, far_ref, start, 1)


def feed_back(place, grad, after_attn, slope, attended, vec, pieces):
    count = grad.shape[0]
    ff = vec.shape[1]
    devices = len(pieces)

    def rows(width):
        return pl.BlockSpec((ROWS, width), lambda i: (i, 0))

    packed = (devices // 2, D // devices, ff + D)
    return pl.pallas_call(
        functools.partial(feed_back_kernel, devices),
        grid=(count // ROWS,),
        in_specs=[scalars(), rows(D), rows(D), rows(ff), rows(D), whole(vec.shape)]
        + [whole(piece.shape) for piece in pieces],
        out_specs=[rows(D), rows(D), whole((8, ff)), whole(packed), whole(packed)],
        out_shape=[
            shape((count, D), F32),
            shape((count, D), BF16),
            shape((8, ff), F32),
            shape(packed, BF16),
            shape(packed, BF16),
        ],
        scratch_shapes=[
            pltpu.VMEM((D, ff), F32),
            pltpu.VMEM((D, D), F32),
        ]
        + feed_scratch(ff),
        compiler_params=params(1),
        cost_estimate=cost(6 * count * D * (ff + D // 2), 12 * count * ff),
        name="feed_back",
    )(place, grad, after_attn, slope, attended, vec, *pieces)


def chosen_rows(ids, slot, rows):
    place = lax.broadcasted_iota(jnp.int32, (ids.shape[0], SEG), 1)
    return nn(jnp.where(ids[:, slot : slot + 1] == place, 1.0, 0.0).astype(BF16), rows)


def ids_down(ids):
    return jnp.concatenate([ids] * 2, axis=0).T


def take_kernel(place_ref, ids_ref, rows_ref, out_ref):
    ids = ids_down(ids_ref[0] - place_ref[1] * SEG)
    rows = rows_ref[0]
    for slot in range(K):
        out_ref[0, slot] = chosen_rows(ids, slot, rows).astype(BF16)


def take(place, ids, rows):
    batch = ids.shape[0]
    return pl.pallas_call(
        take_kernel,
        grid=(batch,),
        in_specs=[
            scalars(),
            pl.BlockSpec((1, K, SEG), lambda b: (b, 0, 0)),
            pl.BlockSpec((1, SEG, D), lambda b: (b, 0, 0)),
        ],
        out_specs=pl.BlockSpec((1, K, SEG, D), lambda b: (b, 0, 0, 0)),
        out_shape=shape((batch, K, SEG, D), BF16),
        compiler_params=params(1),
        cost_estimate=cost(2 * batch * K * SEG * SEG * D, 4 * batch * K * SEG * D),
        name="take",
    )(place, ids, rows)


def give_kernel(distances, started, place_ref, ids_ref, grad_ref, *refs):
    out_refs = refs[started:]
    place = lax.broadcasted_iota(jnp.int32, (SEG, SEG), 0)
    for index, distance in enumerate(distances):
        ids = ids_ref[0] - (place_ref[1] - distance) * SEG
        total = None
        for slot in range(K):
            chosen = jnp.where(ids[slot : slot + 1, :] == place, 1.0, 0.0).astype(BF16)
            part = nn(chosen, grad_ref[0, slot])
            total = part if total is None else total + part
        if started and index == 0:
            total = total + refs[0][0].astype(F32)
        out_refs[index][0] = total.astype(out_refs[index].dtype)


def give(place, ids, grads, arrived, distances):
    batch = ids.shape[0]
    block = pl.BlockSpec((1, SEG, D), lambda b: (b, 0, 0))
    started = arrived is not None
    work = len(distances) * batch * K * SEG * D
    return pl.pallas_call(
        functools.partial(give_kernel, distances, started),
        grid=(batch,),
        in_specs=[
            scalars(),
            pl.BlockSpec((1, K, SEG), lambda b: (b, 0, 0)),
            pl.BlockSpec((1, K, SEG, D), lambda b: (b, 0, 0, 0)),
        ]
        + [block] * started,
        out_specs=[block] * len(distances),
        out_shape=[shape((batch, SEG, D), BF16 if d else F32) for d in distances],
        compiler_params=params(1),
        cost_estimate=cost(2 * work * SEG, 2 * work),
        name="give",
    )(place, ids, grads, *([arrived] if started else []))


def near_kernel(
    hops, count, place_ref, ids_ref, rows_ref, after_ref, grad_ref, vec_ref, *refs
):
    state_refs = refs[:hops]
    piece_refs = refs[hops : hops + count]
    (
        out_ref, row_grad_ref, after_grad_ref, small_ref, near_ref, far_ref,
        keys_total, merge_total, query_total, nq_ref, keys_ref, merge_ref,
    ) = refs[hops + count :]
    first = (pl.program_id(0) == 0) & (pl.program_id(1) == 0)
    last = (pl.program_id(0) == pl.num_programs(0) - 1) & (
        pl.program_id(1) == pl.num_programs(1) - 1
    )

    @pl.when(first)
    def _():
        keys_total[...] = jnp.zeros_like(keys_total)
        merge_total[...] = jnp.zeros_like(merge_total)
        query_total[...] = jnp.zeros_like(query_total)
        assemble(place_ref, ((1, D), (1, 2 * D), (1, D)), piece_refs, refs[-3:])
        small_ref[...] = jnp.zeros_like(small_ref)

    row = lax.broadcasted_iota(jnp.int32, (D, D), 0)
    column = lax.broadcasted_iota(jnp.int32, (D, D), 1)
    same_head = jnp.where(
        lax.shift_right_logical(row, 6) == lax.shift_right_logical(column, 6), 1.0, 0.0
    ).astype(BF16)
    scale = HD**-0.5
    after_ffn = after_ref[0]
    hidden_low = after_ffn.astype(BF16)
    query_float = nn(hidden_low, nq_ref[...]).astype(BF16).astype(F32)
    taken = []
    for slot in range(K):
        total = rows_ref[0, slot].astype(F32)
        for hop in range(hops):
            ids = ids_down(ids_ref[0] - (place_ref[1] - hop - 1) * SEG)
            total = total + chosen_rows(ids, slot, state_refs[hop][0])
        taken.append(total.astype(BF16))
    pairs = [nn(rows, keys_ref[...]).astype(BF16) for rows in taken]
    near_key = [pair[:, :D].astype(F32) for pair in pairs]
    near_value = [pair[:, D:].astype(F32) for pair in pairs]
    scores = [nn((query_float * key).astype(BF16), same_head) * scale for key in near_key]
    top = functools.reduce(jnp.maximum, scores)
    weights = [jnp.exp(score - top) for score in scores]
    inverse = 1.0 / functools.reduce(jnp.add, weights)
    probs = [weight * inverse for weight in weights]
    mixed = functools.reduce(jnp.add, [p * v for p, v in zip(probs, near_value)]).astype(BF16)
    near_out = nn(mixed, merge_ref[...])
    gate_vector = vec_ref[5:6, :D]
    gate = jax.nn.sigmoid(jnp.sum(after_ffn * gate_vector, axis=-1, keepdims=True))
    out_ref[0] = (gate * after_ffn + (1.0 - gate) * near_out).astype(BF16)
    grad = grad_ref[0].astype(F32)
    gate_grad = (
        jnp.sum(grad * (after_ffn - near_out), axis=-1, keepdims=True) * gate * (1.0 - gate)
    )
    add_rows(small_ref, 0, rows_sum(gate_grad * after_ffn))
    near_grad = ((1.0 - gate) * grad).astype(BF16)
    merge_total[...] += tn(mixed, near_grad)
    mixed_grad = nt(near_grad, merge_ref[...]).astype(BF16).astype(F32)
    prob_grads = [nn((mixed_grad * value).astype(BF16), same_head) for value in near_value]
    inner = functools.reduce(jnp.add, [p * g for p, g in zip(probs, prob_grads)])
    query_grad = None
    for slot in range(K):
        score_grad = probs[slot] * (prob_grads[slot] - inner) * scale
        part = score_grad * near_key[slot]
        query_grad = part if query_grad is None else query_grad + part
        pair_grad = jnp.concatenate(
            [(score_grad * query_float).astype(BF16), (probs[slot] * mixed_grad).astype(BF16)],
            axis=1,
        )
        keys_total[...] += tn(taken[slot], pair_grad)
        row_grad_ref[0, slot] = nt(pair_grad, keys_ref[...]).astype(BF16)
    query_grad = query_grad.astype(BF16)
    query_total[...] += tn(hidden_low, query_grad)
    after_grad_ref[0] = gate * grad + gate_grad * gate_vector + nt(query_grad, nq_ref[...])

    @pl.when(last)
    def _():
        start = scatter_rows(place_ref, query_total, near_ref, far_ref, 0, 1)
        start = scatter_rows(place_ref, keys_total, near_ref, far_ref, start, 1)
        scatter_rows(place_ref, merge_total, near_ref, far_ref, start, 1)


def near(place, ids, rows, states, after_ffn, grad, vec, pieces):
    batch = rows.shape[0]
    devices = len(pieces)
    row_block = pl.BlockSpec((1, K, ROWS, D), lambda b, i: (b, 0, i, 0))
    block = pl.BlockSpec((1, ROWS, D), lambda b, i: (b, i, 0))
    packed = (devices // 2, D // devices, 4 * D)
    count = batch * SEG
    return pl.pallas_call(
        functools.partial(near_kernel, len(states), devices),
        grid=(batch, SEG // ROWS),
        in_specs=[scalars(), pl.BlockSpec((1, K, ROWS), lambda b, i: (b, 0, i))]
        + [row_block, block, block, whole(vec.shape)]
        + [pl.BlockSpec((1, SEG, D), lambda b, i: (b, 0, 0))] * len(states)
        + [whole(piece.shape) for piece in pieces],
        out_specs=[block, row_block, block, whole((8, D)), whole(packed), whole(packed)],
        out_shape=[
            shape((batch, SEG, D), BF16),
            shape((batch, K, SEG, D), BF16),
            shape((batch, SEG, D), F32),
            shape((8, D), F32),
            shape(packed, BF16),
            shape(packed, BF16),
        ],
        scratch_shapes=[
            pltpu.VMEM((D, 2 * D), F32),
            pltpu.VMEM((D, D), F32),
            pltpu.VMEM((D, D), F32),
            pltpu.VMEM((D, D), BF16),
            pltpu.VMEM((D, 2 * D), BF16),
            pltpu.VMEM((D, D), BF16),
        ],
        compiler_params=params(2),
        cost_estimate=cost(
            2 * count * D * D * (11 * K + 6), count * D * (4 * K + 12), count * K * D
        ),
        name="near",
    )(place, ids, rows, after_ffn, grad, vec, *states, *pieces)


def reduce_grad_kernel(place_ref, active_ref, grad_ref, near_ref, far_ref, total):
    step = pl.program_id(0)

    @pl.when(step == 0)
    def _():
        total[...] = jnp.zeros_like(total)

    total[...] += tn(active_ref[...], grad_ref[...].astype(BF16))

    @pl.when(step == pl.num_programs(0) - 1)
    def _():
        scatter_rows(place_ref, total, near_ref, far_ref, 0, total.shape[0] // D)


def reduce_grad(place, devices, active, grad):
    count, ff = active.shape
    packed = (devices // 2, D // devices, ff)
    return pl.pallas_call(
        reduce_grad_kernel,
        grid=(count // ROWS,),
        in_specs=[
            scalars(),
            pl.BlockSpec((ROWS, ff), lambda i: (i, 0)),
            pl.BlockSpec((ROWS, D), lambda i: (i, 0)),
        ],
        out_specs=[whole(packed), whole(packed)],
        out_shape=[shape(packed, BF16), shape(packed, BF16)],
        scratch_shapes=[pltpu.VMEM((ff, D), F32)],
        compiler_params=params(1),
        cost_estimate=cost(2 * count * ff * D, 2 * count * ff),
        name="reduce_grad",
    )(place, active, grad)


def finish_kernel(
    parts, place_ref, x_ref, before_ref, dq_ref, dk_ref, dv_ref, dkm_ref, dvm_ref, grad_ref,
    own_ref, sent_ref, arrived_ref, vec_ref, w_ref, gate_ref, feed_ref, diag_ref, select_ref,
    part_ref, send_ref, near_ref, far_ref,
    w_total, norm_total, small_total,
):
    step = pl.program_id(0)

    @pl.when(step == 0)
    def _():
        w_total[...] = jnp.zeros_like(w_total)
        norm_total[...] = jnp.zeros_like(norm_total)

    gain = vec_ref[0:1, :D]
    shift = vec_ref[1:2, :D]
    hat_value, rstd_value = norm(x_ref[0].astype(F32))
    normed = (hat_value * gain + shift).astype(BF16)
    hat_before, rstd_before = norm(before_ref[0].astype(F32))
    normed_before = (hat_before * gain + shift).astype(BF16)
    w_total[:, :D] += tn(normed, dq_ref[0])
    w_total[:, D : 2 * D] += tn(normed, dk_ref[0]) + tn(normed_before, dkm_ref[0])
    w_total[:, 2 * D :] += tn(normed, dv_ref[0]) + tn(normed_before, dvm_ref[0])
    normed_grad = (
        nt(dq_ref[0], w_ref[:, :D])
        + nt(dk_ref[0], w_ref[:, D : 2 * D])
        + nt(dv_ref[0], w_ref[:, 2 * D :])
    )
    before_grad = nt(dkm_ref[0], w_ref[:, D : 2 * D]) + nt(dvm_ref[0], w_ref[:, 2 * D :])
    add_rows(norm_total, 0, rows_sum(normed_grad * hat_value) + rows_sum(before_grad * hat_before))
    add_rows(norm_total, 1, rows_sum(normed_grad) + rows_sum(before_grad))
    send_ref[0] = (
        sent_ref[0].astype(F32)
        + arrived_ref[0].astype(F32)
        + norm_back(before_grad, hat_before, rstd_before, gain)
    ).astype(BF16)
    part_ref[0] = (
        grad_ref[0] + own_ref[0] + norm_back(normed_grad, hat_value, rstd_value, gain)
    )

    @pl.when(step == pl.num_programs(0) - 1)
    def _():
        devices = small_total.shape[0] // 16
        rows = w_total.shape[0] // devices
        small_total[...] = jnp.zeros_like(small_total)
        lines = [
            norm_total[0:1, :],
            norm_total[1:2, :],
            feed_ref[0:1, :D],
            feed_ref[1:2, :D],
            feed_ref[2:3, :D],
            gate_ref[0:1, :],
            feed_ref[3:4, :],
        ]
        for index, (line, width) in enumerate(zip(lines, parts)):
            for d in range(devices):
                row = 16 * d + index
                small_total[row : row + 1, :width] = line[:, d * width : (d + 1) * width]
        table = lax.dot_general(
            diag_ref[...],
            select_ref[...],
            (((1,), (0,)), ((), ())),
            precision=HIGH,
            preferred_element_type=F32,
        )
        own_buckets = NB // devices
        bucket = lax.broadcasted_iota(jnp.int32, (devices, NB), 1)
        owner = lax.broadcasted_iota(jnp.int32, (devices, NB), 0)
        pieces = []
        for place in range(own_buckets):
            chosen = jnp.where(bucket == owner * own_buckets + place, 1.0, 0.0)
            pieces.append(
                lax.dot_general(
                    chosen,
                    table,
                    (((1,), (1,)), ((), ())),
                    precision=HIGH,
                    preferred_element_type=F32,
                )
            )
        buckets = jnp.concatenate(pieces, axis=1)
        for d in range(devices):
            row = 16 * d + len(parts)
            small_total[row : row + 1, : buckets.shape[1]] = buckets[d : d + 1, :]
        width = small_total.shape[1]
        for core_step, ref in ((0, near_ref), (1, far_ref)):
            for chip_step in range(ref.shape[0]):
                target = device_of(place_ref, chip_step, core_step)
                source = pl.multiple_of(target * rows, rows)
                ref[chip_step, :rows, :] = w_total[pl.ds(source, rows), :].astype(BF16)
                ref[chip_step, rows:, :] = jnp.zeros((16, ref.shape[2]), BF16)
                lines = small_total[pl.ds(pl.multiple_of(target * 16, 16), 16), :]
                ref[chip_step, rows:, :width] = lines.astype(BF16)


def finish(
    place, devices, parts, x, before, pieces, grad, own, sent, arrived, vec, weight, gate,
    feed_small, diag,
):
    batch = x.shape[0]
    block = pl.BlockSpec((1, SEG, D), lambda b: (b, 0, 0))
    packed = (devices // 2, D // devices + 16, 3 * D)
    select = jnp.asarray(backward_selector())
    small_width = -(-max(parts) // 128) * 128
    return pl.pallas_call(
        functools.partial(finish_kernel, parts),
        grid=(batch,),
        in_specs=[scalars()]
        + [block] * 11
        + [whole(w.shape) for w in (vec, weight, gate, feed_small, diag, select)],
        out_specs=[block, block, whole(packed), whole(packed)],
        out_shape=[
            shape((batch, SEG, D), F32),
            shape((batch, SEG, D), BF16),
            shape(packed, BF16),
            shape(packed, BF16),
        ],
        scratch_shapes=[
            pltpu.VMEM((D, 3 * D), F32),
            pltpu.VMEM((8, D), F32),
            pltpu.VMEM((16 * devices, small_width), F32),
        ],
        compiler_params=params(1),
        cost_estimate=cost(20 * batch * SEG * D * D, 30 * batch * SEG * D),
        name="finish",
    )(
        place, x, before, *pieces, grad, own, sent, arrived, vec, weight, gate, feed_small, diag,
        select,
    )


def shift(block, distance):
    count = lax.axis_size("seq")
    return lax.ppermute(block, "seq", [(i, (i + distance) % count) for i in range(count)])


def swap(block, axis, bits):
    count = lax.axis_size(axis)
    return lax.ppermute(block, axis, [(i, i ^ bits) for i in range(count)])


def together(*values):
    return lax.optimization_barrier(values)


def chip_steps():
    steps = list(range(1, lax.axis_size("fsdp") // 2))
    cut = (2 * len(steps) + 2) // 3
    return steps[:cut], steps[cut:]


def from_chips(shard, steps):
    return [swap(shard, "fsdp", 2 * step) for step in steps]


def from_core(pieces):
    return [swap(piece, "fsdp", 1) for piece in pieces]


def core_sums(near_half, arrived):
    return [
        (near_half[step].astype(F32) + arrived[step].astype(F32)).astype(BF16)
        for step in range(near_half.shape[0])
    ]


def to_chips(pieces, steps):
    return [swap(pieces[step], "fsdp", 2 * step) for step in steps]


def chip_sum(pieces):
    return functools.reduce(jnp.add, [piece.astype(F32) for piece in pieces]).astype(BF16)


def segment_steps():
    return [1 << bit for bit in range(lax.axis_size("seq").bit_length() - 1)]


def pair_sum(left, right):
    return (left.astype(F32) + right.astype(F32)).astype(BF16)


def on_device(
    layer_input,
    neighbour_ids,
    out_grad,
    attn_norm_gain,
    attn_norm_bias,
    attn_project,
    attn_merge,
    position_bias,
    ffn_norm_gain,
    ffn_norm_bias,
    ffn_expand,
    expand_bias,
    ffn_reduce,
    reduce_bias,
    near_query,
    near_keys,
    near_merge,
    gate_vector,
):
    batch = layer_input.shape[0]
    count = batch * SEG
    devices = lax.axis_size("fsdp")
    segments = lax.axis_size("seq")
    rows = attn_project.shape[0]
    ff = ffn_expand.shape[1]
    ratio = ff // D

    place = jnp.stack([lax.axis_index("fsdp"), lax.axis_index("seq")]).astype(jnp.int32)
    vectors = [
        attn_norm_gain, attn_norm_bias, ffn_norm_gain, ffn_norm_bias, reduce_bias, gate_vector,
        expand_bias, position_bias,
    ]
    parts = [v.shape[0] for v in vectors[:-1]]
    steps = segment_steps()
    near_steps, far_steps = chip_steps()
    chips = near_steps + far_steps

    attn_shard = pack_first(attn_project, vectors)
    attn_pieces = [attn_shard] + from_chips(attn_shard, chips)
    before = shift(layer_input, 1)
    ids = jnp.swapaxes(neighbour_ids, 1, 2)
    feed_shard = pack(rows, [attn_merge, ffn_expand, ffn_reduce])
    near_shard = pack(rows, [near_query, near_keys, near_merge])
    near_rows = take(place, ids, layer_input)
    near_rows, feed_shard, near_shard, attn_pieces = together(
        near_rows, feed_shard, near_shard, attn_pieces
    )
    feed_pieces = [feed_shard] + from_chips(feed_shard, near_steps)
    attn_w, vec, line, joined, memory = first(
        place, layer_input, before, attn_pieces + from_core(attn_pieces), parts, ff
    )
    joined, memory, before, feed_pieces = together(joined, memory, before, feed_pieces)
    feed_pieces += from_chips(feed_shard, far_steps)
    states = [before]
    if segments > 2:
        states.append(shift(before, 1))
    attended = None
    probs = []
    for part in range(2):
        attended, part_probs = attend(place, joined, memory, line, part * PAIRS, attended)
        probs.append(part_probs)
        if part == 0:
            attended, memory, near_shard, feed_pieces, states = together(
                attended, memory, near_shard, feed_pieces, states
            )
            feed_far = from_core(feed_pieces)
            near_pieces = [near_shard] + from_chips(near_shard, chips)
            if len(states) < segments - 1:
                states.append(shift(states[-1], 1))
    attended, feed_far = together(attended, feed_far)
    feed_pieces += feed_far
    flat_attended = attended.reshape(count, D)
    after_attn, active, slope, after_ffn = feed(
        place, layer_input.reshape(count, D), flat_attended, vec, feed_pieces
    )
    after_ffn, near_pieces = together(after_ffn, near_pieces)
    while len(states) < segments - 1:
        states.append(shift(states[-1], 1))
    near_pieces += from_core(near_pieces)
    output, row_grads, after_grad, gate_small, near_half, far_half = near(
        place, ids, near_rows, states, after_ffn.reshape(batch, SEG, D), out_grad, vec,
        near_pieces,
    )

    near_arrived = swap(far_half, "fsdp", 1)
    (message,) = give(place, ids, row_grads, None, (segments - 1,))
    message, after_grad, row_grads = together(message, after_grad, row_grads)
    arrived = shift(message, -1)
    after_grad = after_grad.reshape(count, D)
    reduce_half, reduce_far = reduce_grad(place, devices, active, after_grad)
    reduce_arrived = swap(reduce_far, "fsdp", 1)
    reduce_half, after_grad, near_arrived = together(reduce_half, after_grad, near_arrived)
    grad_after, att_grad, feed_small, feed_half, feed_far = feed_back(
        place, after_grad, after_attn, slope, flat_attended, vec, feed_pieces
    )
    feed_half, feed_far, att_grad, row_grads, arrived, reduce_arrived = together(
        feed_half, feed_far, att_grad, row_grads, arrived, reduce_arrived
    )
    feed_arrived = swap(feed_far, "fsdp", 1)
    near_sums = core_sums(
        jnp.concatenate([near_half, reduce_half], axis=2),
        jnp.concatenate([near_arrived, reduce_arrived], axis=2),
    )
    near_sums, row_grads = together(near_sums, row_grads)
    near_total = [near_sums[0]] + to_chips(near_sums, chips)
    for distance in range(segments - 2, 1, -1):
        (message,) = give(place, ids, row_grads, arrived, (distance,))
        row_grads, message = together(row_grads, message)
        arrived = shift(message, -1)
    row_grads, feed_arrived = together(row_grads, feed_arrived)
    feed_sums = core_sums(feed_half, feed_arrived)
    sent, own = give(place, ids, row_grads, None, (1, 0))
    att_grad, sent, feed_sums = together(att_grad, sent, feed_sums)
    *pieces, first_diag = attend_back(joined, memory, att_grad.reshape(batch, SEG, D), attended, probs[0], 0, [])
    pieces, near_total = together(pieces, near_total)
    near_low = chip_sum(near_total)
    feed_total = [feed_sums[0]] + to_chips(feed_sums, chips)
    near_pair = (near_low, swap(near_low, "seq", steps[0]))
    *pieces, last_diag = attend_back(
        joined, memory, att_grad.reshape(batch, SEG, D), attended, probs[1], PAIRS, pieces
    )
    pieces, arrived, feed_total, near_pair = together(pieces, arrived, feed_total, near_pair)
    for step in steps[1:]:
        near_low = pair_sum(*near_pair)
        near_pair = (near_low, swap(near_low, "seq", step))
    feed_low = chip_sum(feed_total)
    diag = jnp.concatenate([first_diag.reshape(-1, SPAN), last_diag.reshape(-1, SPAN)], axis=0)
    partial, message, attn_half, attn_far = finish(
        place, devices, parts, layer_input, before, pieces, grad_after.reshape(batch, SEG, D),
        own, sent, arrived, vec, attn_w, gate_small, feed_small, diag,
    )
    partial, message, attn_half, attn_far, near_pair, feed_low = together(
        partial, message, attn_half, attn_far, near_pair, feed_low
    )
    attn_arrived = swap(attn_far, "fsdp", 1)
    last = shift(message, -1)
    feed_pair = (feed_low, swap(feed_low, "seq", steps[0]))
    attn_sums = core_sums(attn_half, attn_arrived)
    attn_total = [attn_sums[0]] + to_chips(attn_sums, chips)
    near_grads = unpack(near_pair, ((1, D), (1, 2 * D), (1, D), (ratio, D)))
    near_grads, attn_total, feed_pair = together(near_grads, attn_total, feed_pair)
    attn_low = chip_sum(attn_total)
    for step in steps[1:]:
        feed_low = pair_sum(*feed_pair)
        feed_pair = (feed_low, swap(feed_low, "seq", step))
    for step in steps[:-1]:
        attn_low = pair_sum(attn_low, swap(attn_low, "seq", step))
    attn_low, last = together(attn_low, last)
    attn_pair = (attn_low, swap(attn_low, "seq", steps[-1]))
    input_grad = partial + last.astype(F32)
    feed_grads = unpack(feed_pair, ((1, ff), (1, D)))
    input_grad, feed_grads, attn_pair = together(input_grad, feed_grads, attn_pair)
    project_grad, *smalls = unpack(attn_pair, ((1, 3 * D),), parts + [position_bias.shape[0]])
    return (
        output,
        input_grad,
        smalls[0],
        smalls[1],
        project_grad,
        feed_grads[1],
        smalls[7],
        smalls[2],
        smalls[3],
        feed_grads[0],
        smalls[6],
        near_grads[3],
        smalls[4],
        *near_grads[:3],
        smalls[5],
    )


def solution(mesh):
    in_specs = (
        P("fsdp", "seq", None),
        P("fsdp", "seq", None),
        P("fsdp", "seq", None),
        P("fsdp"),
        P("fsdp"),
        P("fsdp", None),
        P("fsdp", None),
        P("fsdp"),
        P("fsdp"),
        P("fsdp"),
        P("fsdp", None),
        P("fsdp"),
        P("fsdp", None),
        P("fsdp"),
        P("fsdp", None),
        P("fsdp", None),
        P("fsdp", None),
        P("fsdp"),
    )
    out_specs = (
        P("fsdp", "seq", None),
        P("fsdp", "seq", None),
        P("fsdp"),
        P("fsdp"),
        P("fsdp", None),
        P("fsdp", None),
        P("fsdp"),
        P("fsdp"),
        P("fsdp"),
        P("fsdp", None),
        P("fsdp"),
        P("fsdp", None),
        P("fsdp"),
        P("fsdp", None),
        P("fsdp", None),
        P("fsdp", None),
        P("fsdp"),
    )
    return jax.shard_map(
        on_device, mesh=mesh, in_specs=in_specs, out_specs=out_specs, check_vma=False
    )
```

```python
import functools
import math

import jax
import jax.numpy as jnp
import numpy as np
from jax import lax
from jax.experimental import pallas as pl
from jax.experimental.pallas import tpu as pltpu
from jax.sharding import PartitionSpec as P

D = 512
H = 8
HD = 64
K = 4
SEG = 512
NB = 32

EPS = 1e-05
HIGH = lax.Precision.HIGHEST
MASKED = -1e30
F32 = jnp.float32
BF16 = jnp.bfloat16
ROWS = 256
SPAN = 2 * SEG + 128
VMEM = 56 << 20


def nn(left, right):
    return lax.dot_general(left, right, (((1,), (0,)), ((), ())), preferred_element_type=F32)


def nt(left, right):
    return lax.dot_general(left, right, (((1,), (1,)), ((), ())), preferred_element_type=F32)


def tn(left, right):
    return lax.dot_general(left, right, (((0,), (0,)), ((), ())), preferred_element_type=F32)


def shape(dims, dtype):
    return jax.ShapeDtypeStruct(tuple(dims), dtype)


def whole(dims):
    zeros = (0,) * len(dims)
    return pl.BlockSpec(tuple(dims), lambda *_: zeros, pipeline_mode=pl.Buffered(1))


def scalars():
    return pl.BlockSpec(memory_space=pltpu.SMEM)


def params(grid_rank):
    return pltpu.CompilerParams(
        dimension_semantics=("arbitrary",) * grid_rank, vmem_limit_bytes=VMEM
    )


def cost(flops, moved, exps=0):
    return pl.CostEstimate(
        flops=int(flops / 30), bytes_accessed=int(moved / 30), transcendentals=int(exps / 30)
    )


def thresholds():
    half_count = NB // 2
    spread_ratio = 2.0 * SEG / half_count
    exact_part = list(range(1, half_count))
    log_part = [
        int(half_count * spread_ratio ** ((bucket_index - half_count) / half_count))
        for bucket_index in range(half_count, NB)
    ]
    return np.array(exact_part + log_part)


def bucket_of(distance):
    return (distance[:, None] >= thresholds()[None, :]).sum(axis=1)


def forward_selector():
    distance = np.arange(SPAN) - 128
    bucket = bucket_of(np.maximum(distance, 0))
    return (np.arange(NB)[:, None] == bucket[None, :]).astype(np.float32)


def backward_selector():
    chosen = forward_selector().T.copy()
    chosen[:128] = 0.0
    return chosen


def norm(values):
    average = jnp.mean(values, axis=-1, keepdims=True)
    centred = values - average
    variance = jnp.mean(centred * centred, axis=-1, keepdims=True)
    rstd_value = lax.rsqrt(variance + EPS)
    return centred * rstd_value, rstd_value


def norm_back(grad_result, hat_value, rstd_value, gain):
    scaled = grad_result * gain
    return rstd_value * (
        scaled
        - jnp.mean(scaled, axis=-1, keepdims=True)
        - hat_value * jnp.mean(scaled * hat_value, axis=-1, keepdims=True)
    )


def rows_sum(values):
    return jnp.sum(values, axis=0, keepdims=True)


def pair_mask(head, values):
    lane = lax.broadcasted_iota(jnp.int32, values.shape, 1)
    keep = lane < HD if head == 0 else lane >= HD
    return jnp.where(keep, values, jnp.zeros_like(values))


def pack_first_kernel(*refs):
    weight_ref, *vector_refs, out_ref = refs
    rows = weight_ref.shape[0]
    out_ref[:rows, :] = weight_ref[...]
    out_ref[rows:, :] = jnp.zeros((16, out_ref.shape[1]), BF16)
    for index, ref in enumerate(vector_refs):
        line = ref[...].astype(F32).reshape(1, -1).astype(BF16)
        out_ref[rows + index : rows + index + 1, : ref.shape[0]] = line


def pack_first(weight, vectors):
    rows, columns = weight.shape
    return pl.pallas_call(
        pack_first_kernel,
        out_shape=shape((rows + 16, columns), BF16),
        cost_estimate=cost(0, 4 * rows * columns),
        name="pack_first",
    )(weight, *vectors)


def pack_kernel(rows, *refs):
    out_ref = refs[-1]
    start = 0
    for ref in refs[:-1]:
        for chunk in range(ref.shape[0] // rows):
            out_ref[:, start : start + ref.shape[1]] = ref[chunk * rows : (chunk + 1) * rows, :]
            start += ref.shape[1]


def pack(rows, weights):
    columns = sum(w.size for w in weights) // rows
    return pl.pallas_call(
        functools.partial(pack_kernel, rows),
        out_shape=shape((rows, columns), BF16),
        cost_estimate=cost(0, 4 * rows * columns),
        name="pack",
    )(*weights)


def unpack_kernel(layout, terms, *refs):
    total = functools.reduce(jnp.add, [ref[...].astype(F32) for ref in refs[:terms]])
    refs = refs[terms:]
    rows = refs[0].shape[0]
    start = 0
    for ref, (chunks, width) in zip(refs, layout):
        for chunk in range(chunks):
            ref[chunk * rows : (chunk + 1) * rows, :] = total[:rows, start : start + width]
            start += width
    for index, ref in enumerate(refs[len(layout) :]):
        ref[...] = total[rows + index : rows + index + 1, : ref.shape[0]].reshape(-1)


def unpack(pair, layout, widths=()):
    rows = pair[0].shape[0] - (16 if widths else 0)
    outs = [shape((rows * chunks, width), F32) for chunks, width in layout]
    outs += [shape((width,), F32) for width in widths]
    return pl.pallas_call(
        functools.partial(unpack_kernel, layout, len(pair)),
        out_shape=outs,
        cost_estimate=cost(0, 8 * pair[0].size),
        name="unpack",
    )(*pair)


def device_of(place_ref, chip_step, core_step):
    index = place_ref[0]
    chip = lax.shift_right_logical(index, 1)
    core = jnp.bitwise_and(index, 1)
    return jnp.bitwise_xor(chip, chip_step) * 2 + jnp.bitwise_xor(core, core_step)


def assemble(place_ref, layout, piece_refs, out_refs):
    steps = len(piece_refs) // 2
    for core_step in range(2):
        for step in range(steps):
            ref = piece_refs[core_step * steps + step]
            owner = device_of(place_ref, step, core_step)
            rows = D // (2 * steps)
            start = 0
            for out_ref, (chunks, width) in zip(out_refs, layout):
                for chunk in range(chunks):
                    target = pl.multiple_of((owner * chunks + chunk) * rows, rows)
                    out_ref[pl.ds(target, rows), :] = ref[:rows, start : start + width]
                    start += width


def first_kernel(parts, count, place_ref, x_ref, select_ref, *refs):
    piece_refs = refs[:count]
    w_ref, vec_ref, line_ref, joined_ref, small_ref = refs[count:]

    @pl.when(pl.program_id(0) == 0)
    def _():
        assemble(place_ref, ((1, 3 * D),), piece_refs, [w_ref])
        steps = count // 2
        rows = D // count
        for core_step in range(2):
            for step in range(steps):
                owner = device_of(place_ref, step, core_step)
                small_ref[pl.ds(pl.multiple_of(owner * 16, 16), 16), :] = piece_refs[
                    core_step * steps + step
                ][rows:, : small_ref.shape[1]].astype(F32)
        vec_ref[...] = jnp.zeros_like(vec_ref)
        for row, width in enumerate(parts):
            pieces = [small_ref[16 * d + row : 16 * d + row + 1, :width] for d in range(count)]
            vec_ref[row : row + 1, : width * count] = jnp.concatenate(pieces, axis=1)
        row = len(parts)
        table = jnp.concatenate(
            [small_ref[16 * d + row : 16 * d + row + 1, : NB * H // count] for d in range(count)],
            axis=0,
        )
        by_distance = None
        for place in range(NB // count):
            part = lax.dot_general(
                table[:, place * H : (place + 1) * H],
                select_ref[place],
                (((0,), (0,)), ((), ())),
                precision=HIGH,
                preferred_element_type=F32,
            )
            by_distance = part if by_distance is None else by_distance + part
        lane = lax.broadcasted_iota(jnp.int32, by_distance.shape, 1)
        line_ref[...] = jnp.where(lane < 128, MASKED, by_distance)

    hat_value, _ = norm(x_ref[0].astype(F32))
    normed = (hat_value * vec_ref[0:1, :D] + vec_ref[1:2, :D]).astype(BF16)
    joined_ref[0] = nn(normed, w_ref[...]).astype(BF16)


def remember_kernel(x_ref, vec_ref, w_ref, out_ref):
    hat_value, _ = norm(x_ref[0].astype(F32))
    normed = (hat_value * vec_ref[0:1, :D] + vec_ref[1:2, :D]).astype(BF16)
    out_ref[0] = nn(normed, w_ref[:, D:]).astype(BF16)


def remember(before, vec, weight):
    batch = before.shape[0]

    def block(width):
        return pl.BlockSpec((1, SEG, width), lambda b: (b, 0, 0))

    return pl.pallas_call(
        remember_kernel,
        grid=(batch,),
        in_specs=[block(D), whole(vec.shape), whole(weight.shape)],
        out_specs=block(2 * D),
        out_shape=shape((batch, SEG, 2 * D), BF16),
        compiler_params=params(1),
        cost_estimate=cost(4 * batch * SEG * D * D, 6 * batch * SEG * D),
        name="remember",
    )(before, vec, weight)


def first(place, x, pieces, parts, ff):
    batch = x.shape[0]
    count = len(pieces)
    small_width = -(-max(parts) // 128) * 128
    select = forward_selector().reshape(count, NB // count, SPAN).transpose(1, 0, 2)

    def block(width):
        return pl.BlockSpec((1, SEG, width), lambda b: (b, 0, 0))

    return pl.pallas_call(
        functools.partial(first_kernel, parts, count),
        grid=(batch,),
        in_specs=[scalars(), block(D), whole(select.shape)]
        + [whole(piece.shape) for piece in pieces],
        out_specs=[whole((D, 3 * D)), whole((8, ff)), whole((H, SPAN)), block(3 * D)],
        out_shape=[
            shape((D, 3 * D), BF16),
            shape((8, ff), F32),
            shape((H, SPAN), F32),
            shape((batch, SEG, 3 * D), BF16),
        ],
        scratch_shapes=[pltpu.VMEM((16 * count, small_width), F32)],
        compiler_params=params(1),
        cost_estimate=cost(6 * batch * SEG * D * D, 8 * batch * SEG * D),
        name="first",
    )(place, x, jnp.asarray(select), *pieces)


def tiles(place_ref, line_ref, first, own_ref, mem_ref):
    hidden = jnp.where(place_ref[1] > 0, 0.0, MASKED)
    for head in range(2):
        index = 2 * (first + pl.program_id(0)) + head
        line = jnp.broadcast_to(line_ref[pl.ds(index, 1), :], (8, SPAN))
        line = pltpu.roll(line, 0, 1, stride=1, stride_axis=0)
        for group in range(16):
            moved = pltpu.roll(line, 8 * group, 1) if group else line
            for tile in range(2 * SEG // 128):
                start = 2 * SEG - 128 * tile
                row = 128 * tile + 8 * group
                piece = moved[:, start : start + 128]
                own_ref[head, row : row + 8, :] = piece
                mem_ref[head, row : row + 8, :] = piece + hidden


def attend_kernel(first, place_ref, q_ref, k_ref, v_ref, km_ref, vm_ref, line_ref, *refs):
    out_ref, prob_ref, own_ref, mem_ref = refs[-4:]

    @pl.when(pl.program_id(1) == 0)
    def _():
        tiles(place_ref, line_ref, first, own_ref, mem_ref)

    keys = jnp.concatenate([km_ref[0], k_ref[0]], axis=0)
    values = jnp.concatenate([vm_ref[0], v_ref[0]], axis=0)
    for half in range(SEG // ROWS):
        width = SEG + (half + 1) * ROWS
        span = slice(half * ROWS, (half + 1) * ROWS)
        query = q_ref[0, span, :] * BF16(HD**-0.5)
        total = None
        for head in range(2):
            scores = nt(keys[:width], pair_mask(head, query))
            columns = []
            for part in range(ROWS // 128):
                block = half * (ROWS // 128) + part
                bias = jnp.concatenate(
                    [
                        mem_ref[head, (3 - block) * 128 : (7 - block) * 128, :],
                        own_ref[head, (7 - block) * 128 :, :],
                    ],
                    axis=0,
                )
                used = bias.shape[0]
                piece = scores[:used, part * 128 : (part + 1) * 128] + bias
                top = jnp.max(piece, axis=0, keepdims=True)
                weight = jnp.exp(piece - top)
                weight = (weight * (1.0 / jnp.sum(weight, axis=0, keepdims=True))).astype(BF16)
                if used < width:
                    weight = jnp.concatenate(
                        [weight, jnp.zeros((width - used, 128), BF16)], axis=0
                    )
                columns.append(weight)
            probs = jnp.concatenate(columns, axis=1)
            prob_ref[0, head, :width, span] = probs
            product = tn(probs, pair_mask(head, values)[:width])
            total = product if total is None else total + product
        out_ref[0, span, :] = total.astype(BF16)


PAIRS = H // 4


def attend(place, joined, memory, line, first, so_far):
    batch = joined.shape[0]

    def lanes(offset):
        return pl.BlockSpec((1, SEG, 128), lambda h, b: (b, 0, offset + first + h))

    work = batch * H * SEG * SEG
    extra = [] if so_far is None else [so_far]
    return pl.pallas_call(
        functools.partial(attend_kernel, first),
        grid=(PAIRS, batch),
        in_specs=[scalars()]
        + [lanes(0), lanes(2 * PAIRS), lanes(4 * PAIRS), lanes(0), lanes(2 * PAIRS)]
        + [whole(line.shape)]
        + [pl.BlockSpec(memory_space=pl.ANY)] * len(extra),
        out_specs=[
            lanes(0),
            pl.BlockSpec((1, 2, 2 * SEG, SEG), lambda h, b: (b, h, 0, 0)),
        ],
        out_shape=[shape((batch, SEG, D), BF16), shape((batch, H // 2, 2 * SEG, SEG), BF16)],
        scratch_shapes=[pltpu.VMEM((2, 2 * SEG, 128), F32)] * 2,
        input_output_aliases={7: 0} if extra else {},
        compiler_params=params(2),
        cost_estimate=cost(16 * HD * work, 3 * work, work),
        name="attend",
    )(place, joined, joined, joined, memory, memory, line, *extra)


def attend_back_kernel(
    q_ref, k_ref, v_ref, km_ref, vm_ref, grad_ref, out_ref, prob_ref, *refs
):
    dq_ref, dk_ref, dv_ref, dkm_ref, dvm_ref, diag_ref, grid_ref = refs[-7:]
    keys = jnp.concatenate([km_ref[0], k_ref[0]], axis=0)
    values = jnp.concatenate([vm_ref[0], v_ref[0]], axis=0)
    step = pl.program_id(1)

    @pl.when(step == 0)
    def _():
        grid_ref[...] = jnp.zeros_like(grid_ref)

    key_parts = []
    value_parts = []
    for half in range(SEG // ROWS):
        width = SEG + (half + 1) * ROWS
        span = slice(half * ROWS, (half + 1) * ROWS)
        grad = grad_ref[0, span, :]
        query = q_ref[0, span, :] * BF16(HD**-0.5)
        product = (grad.astype(F32) * out_ref[0, span, :].astype(F32)).T
        query_total = key_total = value_total = None
        for head in range(2):
            grad_head = pair_mask(head, grad)
            delta = jnp.sum(product[head * HD : (head + 1) * HD], axis=0, keepdims=True)
            probs = prob_ref[0, head, :width, span]
            scored = probs.astype(F32) * (nt(values[:width], grad_head) - delta)
            for part in range(ROWS // 128):
                block = half * (ROWS // 128) + part
                used = SEG + (block + 1) * 128
                grid_ref[head, (3 - block) * 128 :, :] += scored[
                    :used, part * 128 : (part + 1) * 128
                ]
            scored = scored.astype(BF16)
            for_key = nn(scored, pair_mask(head, query))
            for_value = nn(probs, grad_head)
            for_query = tn(scored, pair_mask(head, keys)[:width])
            key_total = for_key if key_total is None else key_total + for_key
            value_total = for_value if value_total is None else value_total + for_value
            query_total = for_query if query_total is None else query_total + for_query
        dq_ref[0, span, :] = (query_total * HD**-0.5).astype(BF16)
        key_parts.append(key_total)
        value_parts.append(value_total)
    for pieces, mem_ref, own_ref in (
        (key_parts, dkm_ref, dk_ref),
        (value_parts, dvm_ref, dv_ref),
    ):
        both = pieces[0] + pieces[1][: SEG + ROWS]
        mem_ref[0] = both[:SEG].astype(BF16)
        own_ref[0, :ROWS] = both[SEG:].astype(BF16)
        own_ref[0, ROWS:] = pieces[1][SEG + ROWS :].astype(BF16)

    @pl.when(step == pl.num_programs(1) - 1)
    def _():
        for head in range(2):
            total = None
            for group in range(16):
                pieces = [
                    grid_ref[head, 128 * tile + 8 * group : 128 * tile + 8 * group + 8, :]
                    for tile in reversed(range(2 * SEG // 128))
                ]
                line = jnp.concatenate([jnp.zeros((8, 128), F32)] + pieces, axis=1)
                if group:
                    line = pltpu.roll(line, SPAN - 8 * group, 1)
                total = line if total is None else total + line
            lines = [total[:1]] + [
                pltpu.roll(total[row : row + 1], SPAN - row, 1) for row in range(1, 8)
            ]
            diag_ref[0, head : head + 1, :] = functools.reduce(jnp.add, lines)


def attend_back(joined, memory, grad, attended, probs, first, so_far):
    batch = joined.shape[0]

    def lanes(offset):
        return pl.BlockSpec((1, SEG, 128), lambda h, b: (b, 0, offset + first + h))

    half = shape((batch, SEG, D), BF16)
    work = batch * H * SEG * SEG
    return pl.pallas_call(
        attend_back_kernel,
        grid=(PAIRS, batch),
        in_specs=[lanes(0), lanes(2 * PAIRS), lanes(4 * PAIRS), lanes(0), lanes(2 * PAIRS)]
        + [lanes(0)] * 2
        + [pl.BlockSpec((1, 2, 2 * SEG, SEG), lambda h, b: (b, h, 0, 0))]
        + [pl.BlockSpec(memory_space=pl.ANY)] * len(so_far),
        out_specs=[lanes(0)] * 5 + [pl.BlockSpec((1, 2, SPAN), lambda h, b: (h, 0, 0))],
        out_shape=[half] * 5 + [shape((PAIRS, 2, SPAN), F32)],
        scratch_shapes=[pltpu.VMEM((2, 2 * SEG, 128), F32)],
        input_output_aliases={8 + i: i for i in range(len(so_far))},
        compiler_params=params(2),
        cost_estimate=cost(32 * HD * work, 3 * work),
        name="attend_back",
    )(joined, joined, joined, memory, memory, grad, attended, probs, *so_far)


def feed_layout(ff):
    return ((1, D), (1, ff), (ff // D, D))


def feed_scratch(ff):
    return [pltpu.VMEM((D, D), BF16), pltpu.VMEM((D, ff), BF16), pltpu.VMEM((ff, D), BF16)]


def feed_kernel(count, place_ref, x_ref, att_ref, vec_ref, *refs):
    piece_refs = refs[:count]
    (
        after_attn_ref, active_ref, slope_ref, after_ffn_ref, merge_ref, expand_ref, reduce_ref,
    ) = refs[count:]

    @pl.when(pl.program_id(0) == 0)
    def _():
        assemble(place_ref, feed_layout(expand_ref.shape[1]), piece_refs, refs[-3:])

    after_attn = x_ref[...].astype(F32) + nn(att_ref[...], merge_ref[...])
    after_attn_ref[...] = after_attn
    hat_value, _ = norm(after_attn)
    normed = (hat_value * vec_ref[2:3, :D] + vec_ref[3:4, :D]).astype(BF16)
    pre = nn(normed, expand_ref[...]) + vec_ref[6:7, :]
    cdf = 0.5 * (1.0 + lax.erf(pre * (1.0 / math.sqrt(2.0))))
    slope = cdf + pre * jnp.exp(-0.5 * pre * pre) * (1.0 / math.sqrt(2.0 * math.pi))
    slope_ref[...] = slope.astype(BF16)
    active = (pre * cdf).astype(BF16)
    active_ref[...] = active
    after_ffn = after_attn + nn(active, reduce_ref[...]) + vec_ref[4:5, :D]
    after_ffn_ref[...] = after_ffn


def feed(place, x, attended, vec, pieces):
    count = x.shape[0]
    ff = vec.shape[1]

    def rows(width):
        return pl.BlockSpec((ROWS, width), lambda i: (i, 0))

    return pl.pallas_call(
        functools.partial(feed_kernel, len(pieces)),
        grid=(count // ROWS,),
        in_specs=[scalars(), rows(D), rows(D), whole(vec.shape)]
        + [whole(piece.shape) for piece in pieces],
        out_specs=[rows(D), rows(ff), rows(ff), rows(D)],
        out_shape=[
            shape((count, D), F32),
            shape((count, ff), BF16),
            shape((count, ff), BF16),
            shape((count, D), F32),
        ],
        scratch_shapes=feed_scratch(ff),
        compiler_params=params(1),
        cost_estimate=cost(4 * count * D * (ff + D), 12 * count * ff, 2 * count * ff),
        name="feed",
    )(place, x, attended, vec, *pieces)


def add_rows(ref, row, values):
    ref[row : row + 1, : values.shape[1]] += values


def scatter_rows(place_ref, total_ref, near_ref, far_ref, start, chunks):
    steps, rows = near_ref.shape[0], near_ref.shape[1]
    width = total_ref.shape[1]
    for core_step, ref in ((0, near_ref), (1, far_ref)):
        for step in range(steps):
            owner = device_of(place_ref, step, core_step)
            for chunk in range(chunks):
                source = pl.multiple_of((owner * chunks + chunk) * rows, rows)
                column = start + chunk * width
                ref[step, :, column : column + width] = total_ref[
                    pl.ds(source, rows), :
                ].astype(BF16)
    return start + chunks * width


def feed_back_kernel(
    count, place_ref, grad_ref, after_ref, slope_ref, att_ref, vec_ref, *refs
):
    piece_refs = refs[:count]
    (
        after_grad_ref, att_grad_ref, small_ref, near_ref, far_ref,
        expand_total, merge_total, merge_ref, expand_ref, reduce_ref,
    ) = refs[count:]
    step = pl.program_id(0)

    @pl.when(step == 0)
    def _():
        assemble(place_ref, feed_layout(expand_ref.shape[1]), piece_refs, refs[-3:])
        expand_total[...] = jnp.zeros_like(expand_total)
        merge_total[...] = jnp.zeros_like(merge_total)
        small_ref[...] = jnp.zeros_like(small_ref)

    grad = grad_ref[...]
    low = grad.astype(BF16)
    add_rows(small_ref, 2, rows_sum(low.astype(F32)))
    pre_grad = (nt(low, reduce_ref[...]) * slope_ref[...].astype(F32)).astype(BF16)
    add_rows(small_ref, 3, rows_sum(pre_grad.astype(F32)))
    hat_value, rstd_value = norm(after_ref[...])
    gain = vec_ref[2:3, :D]
    normed = (hat_value * gain + vec_ref[3:4, :D]).astype(BF16)
    expand_total[...] += tn(normed, pre_grad)
    normed_grad = nt(pre_grad, expand_ref[...])
    add_rows(small_ref, 0, rows_sum(normed_grad * hat_value))
    add_rows(small_ref, 1, rows_sum(normed_grad))
    after_grad = grad + norm_back(normed_grad, hat_value, rstd_value, gain)
    after_grad_ref[...] = after_grad
    merge_grad = after_grad.astype(BF16)
    merge_total[...] += tn(att_ref[...], merge_grad)
    att_grad_ref[...] = nt(merge_grad, merge_ref[...]).astype(BF16)

    @pl.when(step == pl.num_programs(0) - 1)
    def _():
        start = scatter_rows(place_ref, expand_total, near_ref, far_ref, 0, 1)
        scatter_rows(place_ref, merge_total, near_ref, far_ref, start, 1)


def feed_back(place, grad, after_attn, slope, attended, vec, pieces):
    count = grad.shape[0]
    ff = vec.shape[1]
    devices = len(pieces)

    def rows(width):
        return pl.BlockSpec((ROWS, width), lambda i: (i, 0))

    packed = (devices // 2, D // devices, ff + D)
    return pl.pallas_call(
        functools.partial(feed_back_kernel, devices),
        grid=(count // ROWS,),
        in_specs=[scalars(), rows(D), rows(D), rows(ff), rows(D), whole(vec.shape)]
        + [whole(piece.shape) for piece in pieces],
        out_specs=[rows(D), rows(D), whole((8, ff)), whole(packed), whole(packed)],
        out_shape=[
            shape((count, D), F32),
            shape((count, D), BF16),
            shape((8, ff), F32),
            shape(packed, BF16),
            shape(packed, BF16),
        ],
        scratch_shapes=[
            pltpu.VMEM((D, ff), F32),
            pltpu.VMEM((D, D), F32),
        ]
        + feed_scratch(ff),
        compiler_params=params(1),
        cost_estimate=cost(6 * count * D * (ff + D // 2), 12 * count * ff),
        name="feed_back",
    )(place, grad, after_attn, slope, attended, vec, *pieces)


def chosen_rows(ids, slot, rows):
    place = lax.broadcasted_iota(jnp.int32, (ids.shape[0], SEG), 1)
    return nn(jnp.where(ids[:, slot : slot + 1] == place, 1.0, 0.0).astype(BF16), rows)


def ids_down(ids):
    return jnp.concatenate([ids] * 2, axis=0).T


def take_kernel(place_ref, ids_ref, rows_ref, out_ref):
    ids = ids_down(ids_ref[0] - place_ref[1] * SEG)
    rows = rows_ref[0]
    for slot in range(K):
        out_ref[0, slot] = chosen_rows(ids, slot, rows).astype(BF16)


def take(place, ids, rows):
    batch = ids.shape[0]
    return pl.pallas_call(
        take_kernel,
        grid=(batch,),
        in_specs=[
            scalars(),
            pl.BlockSpec((1, K, SEG), lambda b: (b, 0, 0)),
            pl.BlockSpec((1, SEG, D), lambda b: (b, 0, 0)),
        ],
        out_specs=pl.BlockSpec((1, K, SEG, D), lambda b: (b, 0, 0, 0)),
        out_shape=shape((batch, K, SEG, D), BF16),
        compiler_params=params(1),
        cost_estimate=cost(2 * batch * K * SEG * SEG * D, 4 * batch * K * SEG * D),
        name="take",
    )(place, ids, rows)


def give_kernel(distances, started, place_ref, ids_ref, grad_ref, *refs):
    out_refs = refs[started:]
    place = lax.broadcasted_iota(jnp.int32, (SEG, SEG), 0)
    for index, distance in enumerate(distances):
        ids = ids_ref[0] - (place_ref[1] - distance) * SEG
        total = None
        for slot in range(K):
            chosen = jnp.where(ids[slot : slot + 1, :] == place, 1.0, 0.0).astype(BF16)
            part = nn(chosen, grad_ref[0, slot])
            total = part if total is None else total + part
        if started and index == 0:
            total = total + refs[0][0].astype(F32)
        out_refs[index][0] = total.astype(out_refs[index].dtype)


def give(place, ids, grads, arrived, distances):
    batch = ids.shape[0]
    block = pl.BlockSpec((1, SEG, D), lambda b: (b, 0, 0))
    started = arrived is not None
    work = len(distances) * batch * K * SEG * D
    return pl.pallas_call(
        functools.partial(give_kernel, distances, started),
        grid=(batch,),
        in_specs=[
            scalars(),
            pl.BlockSpec((1, K, SEG), lambda b: (b, 0, 0)),
            pl.BlockSpec((1, K, SEG, D), lambda b: (b, 0, 0, 0)),
        ]
        + [block] * started,
        out_specs=[block] * len(distances),
        out_shape=[shape((batch, SEG, D), BF16 if d else F32) for d in distances],
        compiler_params=params(1),
        cost_estimate=cost(2 * work * SEG, 2 * work),
        name="give",
    )(place, ids, grads, *([arrived] if started else []))


def near_kernel(
    hops, count, place_ref, ids_ref, rows_ref, after_ref, grad_ref, active_ref, vec_ref, *refs
):
    state_refs = refs[:hops]
    piece_refs = refs[hops : hops + count]
    (
        out_ref, row_grad_ref, after_grad_ref, small_ref, near_ref, far_ref,
        keys_total, merge_total, query_total, reduce_total, nq_ref, keys_ref, merge_ref,
    ) = refs[hops + count :]
    first = (pl.program_id(0) == 0) & (pl.program_id(1) == 0)
    last = (pl.program_id(0) == pl.num_programs(0) - 1) & (
        pl.program_id(1) == pl.num_programs(1) - 1
    )

    @pl.when(first)
    def _():
        keys_total[...] = jnp.zeros_like(keys_total)
        merge_total[...] = jnp.zeros_like(merge_total)
        query_total[...] = jnp.zeros_like(query_total)
        reduce_total[...] = jnp.zeros_like(reduce_total)
        assemble(place_ref, ((1, D), (1, 2 * D), (1, D)), piece_refs, refs[-3:])
        small_ref[...] = jnp.zeros_like(small_ref)

    scale = HD**-0.5
    place = lax.broadcasted_iota(jnp.int32, (K * D, 128), 0)
    lane = lax.broadcasted_iota(jnp.int32, (K * D, 128), 1)
    group = lax.shift_right_logical(place, 9) * H + jnp.bitwise_and(
        lax.shift_right_logical(place, 6), H - 1
    )
    gather = jnp.where(jnp.bitwise_and(lane, K * H - 1) == group, 1.0, 0.0).astype(BF16)
    lane = lax.broadcasted_iota(jnp.int32, (128, K * D), 0)
    place = lax.broadcasted_iota(jnp.int32, (128, K * D), 1)
    group = lax.shift_right_logical(place, 9) * H + jnp.bitwise_and(
        lax.shift_right_logical(place, 6), H - 1
    )
    spread = jnp.where(
        (jnp.bitwise_and(lane, K * H - 1) == group) & (lane < 2 * K * H), 1.0, 0.0
    ).astype(BF16)

    def over_slots(combine, values):
        values = combine(values, pltpu.roll(values, 2 * H, 1))
        return combine(values, pltpu.roll(values, H, 1))

    def to_rows(values):
        high = values.astype(BF16)
        low = (values - high.astype(F32)).astype(BF16)
        lane = lax.broadcasted_iota(jnp.int32, values.shape, 1)
        return nn(jnp.where(lane < K * H, high, low), spread)

    def slot_of(values, slot):
        return values[:, slot * D : (slot + 1) * D]

    after_ffn = after_ref[0]
    hidden_low = after_ffn.astype(BF16)
    query = nn(hidden_low, nq_ref[...]).astype(BF16)
    query_float = query.astype(F32)
    ids = ids_down(ids_ref[0])
    states = jnp.concatenate([ref[0] for ref in state_refs], axis=0) if hops else None
    taken = []
    for slot in range(K):
        total = rows_ref[0, slot]
        if hops:
            chosen = []
            for hop in range(hops):
                column = ids[:, slot : slot + 1] - (place_ref[1] - hop - 1) * SEG
                here = lax.broadcasted_iota(jnp.int32, (ids.shape[0], SEG), 1)
                chosen.append(jnp.where(column == here, 1.0, 0.0).astype(BF16))
            moved = nn(jnp.concatenate(chosen, axis=1), states)
            total = total + moved.astype(BF16)
        taken.append(total)
    pairs = [nn(rows, keys_ref[...]).astype(BF16) for rows in taken]
    near_key = [pair[:, :D] for pair in pairs]
    near_value = [pair[:, D:] for pair in pairs]
    products = jnp.concatenate([query * key for key in near_key], axis=1)
    scores = nn(products, gather) * scale
    weights = jnp.exp(scores - over_slots(jnp.maximum, scores))
    probs = weights / over_slots(jnp.add, weights)
    prob_rows = to_rows(probs)
    mixed = functools.reduce(
        jnp.add, [slot_of(prob_rows, i) * v.astype(F32) for i, v in enumerate(near_value)]
    ).astype(BF16)
    near_out = nn(mixed, merge_ref[...])
    gate_vector = vec_ref[5:6, :D]
    gate = jax.nn.sigmoid(jnp.sum(after_ffn * gate_vector, axis=-1, keepdims=True))
    out_ref[0] = (gate * after_ffn + (1.0 - gate) * near_out).astype(BF16)
    grad = grad_ref[0].astype(F32)
    gate_grad = (
        jnp.sum(grad * (after_ffn - near_out), axis=-1, keepdims=True) * gate * (1.0 - gate)
    )
    add_rows(small_ref, 0, rows_sum(gate_grad * after_ffn))
    near_grad = ((1.0 - gate) * grad).astype(BF16)
    merge_total[...] += tn(mixed, near_grad)
    mixed_low = nt(near_grad, merge_ref[...]).astype(BF16)
    mixed_grad = mixed_low.astype(F32)
    products = jnp.concatenate([mixed_low * value for value in near_value], axis=1)
    prob_grads = nn(products, gather)
    inner = over_slots(jnp.add, probs * prob_grads)
    score_rows = to_rows(probs * (prob_grads - inner) * scale)
    query_grad = None
    for slot in range(K):
        score_grad = slot_of(score_rows, slot)
        part = score_grad * near_key[slot].astype(F32)
        query_grad = part if query_grad is None else query_grad + part
        pair_grad = jnp.concatenate(
            [
                (score_grad * query_float).astype(BF16),
                (slot_of(prob_rows, slot) * mixed_grad).astype(BF16),
            ],
            axis=1,
        )
        keys_total[...] += tn(taken[slot], pair_grad)
        row_grad_ref[0, slot] = nt(pair_grad, keys_ref[...]).astype(BF16)
    query_grad = query_grad.astype(BF16)
    query_total[...] += tn(hidden_low, query_grad)
    after_grad = gate * grad + gate_grad * gate_vector + nt(query_grad, nq_ref[...])
    after_grad_ref[0] = after_grad
    reduce_total[...] += tn(active_ref[...], after_grad.astype(BF16))

    @pl.when(last)
    def _():
        start = scatter_rows(place_ref, query_total, near_ref, far_ref, 0, 1)
        start = scatter_rows(place_ref, keys_total, near_ref, far_ref, start, 1)
        start = scatter_rows(place_ref, merge_total, near_ref, far_ref, start, 1)
        ratio = reduce_total.shape[0] // D
        scatter_rows(place_ref, reduce_total, near_ref, far_ref, start, ratio)


def near(place, ids, rows, states, after_ffn, grad, active, vec, pieces):
    batch = rows.shape[0]
    devices = len(pieces)
    row_block = pl.BlockSpec((1, K, ROWS, D), lambda b, i: (b, 0, i, 0))
    block = pl.BlockSpec((1, ROWS, D), lambda b, i: (b, i, 0))
    ff = active.shape[1]
    packed = (devices // 2, D // devices, 4 * D + ff)
    count = batch * SEG
    blocks = SEG // ROWS
    return pl.pallas_call(
        functools.partial(near_kernel, len(states), devices),
        grid=(batch, SEG // ROWS),
        in_specs=[scalars(), pl.BlockSpec((1, K, ROWS), lambda b, i: (b, 0, i))]
        + [row_block, block, block]
        + [pl.BlockSpec((ROWS, ff), lambda b, i: (b * blocks + i, 0)), whole(vec.shape)]
        + [pl.BlockSpec((1, SEG, D), lambda b, i: (b, 0, 0))] * len(states)
        + [whole(piece.shape) for piece in pieces],
        out_specs=[block, row_block, block, whole((8, D)), whole(packed), whole(packed)],
        out_shape=[
            shape((batch, SEG, D), BF16),
            shape((batch, K, SEG, D), BF16),
            shape((batch, SEG, D), F32),
            shape((8, D), F32),
            shape(packed, BF16),
            shape(packed, BF16),
        ],
        scratch_shapes=[
            pltpu.VMEM((D, 2 * D), F32),
            pltpu.VMEM((D, D), F32),
            pltpu.VMEM((D, D), F32),
            pltpu.VMEM((ff, D), F32),
            pltpu.VMEM((D, D), BF16),
            pltpu.VMEM((D, 2 * D), BF16),
            pltpu.VMEM((D, D), BF16),
        ],
        compiler_params=params(2),
        cost_estimate=cost(
            2 * count * D * D * (11 * K + 6), count * D * (4 * K + 12), count * K * D
        ),
        name="near",
    )(place, ids, rows, after_ffn, grad, active, vec, *states, *pieces)


def finish_kernel(
    parts, place_ref, x_ref, before_ref, dq_ref, dk_ref, dv_ref, dkm_ref, dvm_ref, grad_ref,
    own_ref, sent_ref, arrived_ref, vec_ref, w_ref, gate_ref, feed_ref, diag_ref, select_ref,
    part_ref, send_ref, near_ref, far_ref,
    w_total, norm_total, small_total,
):
    step = pl.program_id(0)

    @pl.when(step == 0)
    def _():
        w_total[...] = jnp.zeros_like(w_total)
        norm_total[...] = jnp.zeros_like(norm_total)

    gain = vec_ref[0:1, :D]
    shift = vec_ref[1:2, :D]
    hat_value, rstd_value = norm(x_ref[0].astype(F32))
    normed = (hat_value * gain + shift).astype(BF16)
    hat_before, rstd_before = norm(before_ref[0].astype(F32))
    normed_before = (hat_before * gain + shift).astype(BF16)
    w_total[:, :D] += tn(normed, dq_ref[0])
    w_total[:, D : 2 * D] += tn(normed, dk_ref[0]) + tn(normed_before, dkm_ref[0])
    w_total[:, 2 * D :] += tn(normed, dv_ref[0]) + tn(normed_before, dvm_ref[0])
    normed_grad = (
        nt(dq_ref[0], w_ref[:, :D])
        + nt(dk_ref[0], w_ref[:, D : 2 * D])
        + nt(dv_ref[0], w_ref[:, 2 * D :])
    )
    before_grad = nt(dkm_ref[0], w_ref[:, D : 2 * D]) + nt(dvm_ref[0], w_ref[:, 2 * D :])
    add_rows(norm_total, 0, rows_sum(normed_grad * hat_value) + rows_sum(before_grad * hat_before))
    add_rows(norm_total, 1, rows_sum(normed_grad) + rows_sum(before_grad))
    send_ref[0] = (
        sent_ref[0].astype(F32)
        + arrived_ref[0].astype(F32)
        + norm_back(before_grad, hat_before, rstd_before, gain)
    ).astype(BF16)
    part_ref[0] = (
        grad_ref[0] + own_ref[0] + norm_back(normed_grad, hat_value, rstd_value, gain)
    )

    @pl.when(step == pl.num_programs(0) - 1)
    def _():
        devices = small_total.shape[0] // 16
        rows = w_total.shape[0] // devices
        small_total[...] = jnp.zeros_like(small_total)
        lines = [
            norm_total[0:1, :],
            norm_total[1:2, :],
            feed_ref[0:1, :D],
            feed_ref[1:2, :D],
            feed_ref[2:3, :D],
            gate_ref[0:1, :],
            feed_ref[3:4, :],
        ]
        for index, (line, width) in enumerate(zip(lines, parts)):
            for d in range(devices):
                row = 16 * d + index
                small_total[row : row + 1, :width] = line[:, d * width : (d + 1) * width]
        table = lax.dot_general(
            diag_ref[...],
            select_ref[...],
            (((1,), (0,)), ((), ())),
            precision=HIGH,
            preferred_element_type=F32,
        )
        own_buckets = NB // devices
        bucket = lax.broadcasted_iota(jnp.int32, (devices, NB), 1)
        owner = lax.broadcasted_iota(jnp.int32, (devices, NB), 0)
        pieces = []
        for place in range(own_buckets):
            chosen = jnp.where(bucket == owner * own_buckets + place, 1.0, 0.0)
            pieces.append(
                lax.dot_general(
                    chosen,
                    table,
                    (((1,), (1,)), ((), ())),
                    precision=HIGH,
                    preferred_element_type=F32,
                )
            )
        buckets = jnp.concatenate(pieces, axis=1)
        for d in range(devices):
            row = 16 * d + len(parts)
            small_total[row : row + 1, : buckets.shape[1]] = buckets[d : d + 1, :]
        width = small_total.shape[1]
        for core_step, ref in ((0, near_ref), (1, far_ref)):
            for chip_step in range(ref.shape[0]):
                target = device_of(place_ref, chip_step, core_step)
                source = pl.multiple_of(target * rows, rows)
                ref[chip_step, :rows, :] = w_total[pl.ds(source, rows), :].astype(BF16)
                ref[chip_step, rows:, :] = jnp.zeros((16, ref.shape[2]), BF16)
                lines = small_total[pl.ds(pl.multiple_of(target * 16, 16), 16), :]
                ref[chip_step, rows:, :width] = lines.astype(BF16)


def finish(
    place, devices, parts, x, before, pieces, grad, own, sent, arrived, vec, weight, gate,
    feed_small, diag,
):
    batch = x.shape[0]
    block = pl.BlockSpec((1, SEG, D), lambda b: (b, 0, 0))
    packed = (devices // 2, D // devices + 16, 3 * D)
    select = jnp.asarray(backward_selector())
    small_width = -(-max(parts) // 128) * 128
    return pl.pallas_call(
        functools.partial(finish_kernel, parts),
        grid=(batch,),
        in_specs=[scalars()]
        + [block] * 11
        + [whole(w.shape) for w in (vec, weight, gate, feed_small, diag, select)],
        out_specs=[block, block, whole(packed), whole(packed)],
        out_shape=[
            shape((batch, SEG, D), F32),
            shape((batch, SEG, D), BF16),
            shape(packed, BF16),
            shape(packed, BF16),
        ],
        scratch_shapes=[
            pltpu.VMEM((D, 3 * D), F32),
            pltpu.VMEM((8, D), F32),
            pltpu.VMEM((16 * devices, small_width), F32),
        ],
        compiler_params=params(1),
        cost_estimate=cost(20 * batch * SEG * D * D, 30 * batch * SEG * D),
        name="finish",
    )(
        place, x, before, *pieces, grad, own, sent, arrived, vec, weight, gate, feed_small, diag,
        select,
    )


def shift(block, distance):
    count = lax.axis_size("seq")
    return lax.ppermute(block, "seq", [(i, (i + distance) % count) for i in range(count)])


def swap(block, axis, bits):
    count = lax.axis_size(axis)
    return lax.ppermute(block, axis, [(i, i ^ bits) for i in range(count)])


def together(*values):
    return lax.optimization_barrier(values)


def chip_steps():
    steps = list(range(1, lax.axis_size("fsdp") // 2))
    cut = (2 * len(steps) + 2) // 3
    return steps[:cut], steps[cut:]


def from_chips(shard, steps):
    return [swap(shard, "fsdp", 2 * step) for step in steps]


def from_core(pieces):
    return [swap(piece, "fsdp", 1) for piece in pieces]


def core_sums(near_half, arrived):
    return [
        (near_half[step].astype(F32) + arrived[step].astype(F32)).astype(BF16)
        for step in range(near_half.shape[0])
    ]


def to_chips(pieces, steps):
    return [swap(pieces[step], "fsdp", 2 * step) for step in steps]


def chip_sum(pieces):
    return functools.reduce(jnp.add, [piece.astype(F32) for piece in pieces]).astype(BF16)


def segment_steps():
    return [1 << bit for bit in range(lax.axis_size("seq").bit_length() - 1)]


def pair_sum(left, right):
    return (left.astype(F32) + right.astype(F32)).astype(BF16)


def on_device(
    layer_input,
    neighbour_ids,
    out_grad,
    attn_norm_gain,
    attn_norm_bias,
    attn_project,
    attn_merge,
    position_bias,
    ffn_norm_gain,
    ffn_norm_bias,
    ffn_expand,
    expand_bias,
    ffn_reduce,
    reduce_bias,
    near_query,
    near_keys,
    near_merge,
    gate_vector,
):
    batch = layer_input.shape[0]
    count = batch * SEG
    devices = lax.axis_size("fsdp")
    segments = lax.axis_size("seq")
    rows = attn_project.shape[0]
    ff = ffn_expand.shape[1]
    ratio = ff // D

    place = jnp.stack([lax.axis_index("fsdp"), lax.axis_index("seq")]).astype(jnp.int32)
    vectors = [
        attn_norm_gain, attn_norm_bias, ffn_norm_gain, ffn_norm_bias, reduce_bias, gate_vector,
        expand_bias, position_bias,
    ]
    parts = [v.shape[0] for v in vectors[:-1]]
    steps = segment_steps()
    near_steps, far_steps = chip_steps()
    chips = near_steps + far_steps

    attn_shard = pack_first(attn_project, vectors)
    attn_pieces = [attn_shard] + from_chips(attn_shard, chips)
    before = shift(layer_input, 1)
    ids = jnp.swapaxes(neighbour_ids, 1, 2)
    feed_shard = pack(rows, [attn_merge, ffn_expand, ffn_reduce])
    near_shard = pack(rows, [near_query, near_keys, near_merge])
    near_rows = take(place, ids, layer_input)
    near_rows, feed_shard, near_shard, attn_pieces = together(
        near_rows, feed_shard, near_shard, attn_pieces
    )
    feed_pieces = [feed_shard] + from_chips(feed_shard, near_steps)
    attn_w, vec, line, joined = first(
        place, layer_input, attn_pieces + from_core(attn_pieces), parts, ff
    )
    joined, before = together(joined, before)
    states = [before]
    if segments > 2:
        states.append(shift(before, 1))
    memory = remember(before, vec, attn_w)
    attended = None
    probs = []
    for part in range(2):
        attended, part_probs = attend(place, joined, memory, line, part * PAIRS, attended)
        probs.append(part_probs)
        if part == 0:
            attended, memory, feed_pieces, states = together(
                attended, memory, feed_pieces, states
            )
            feed_far = from_core(feed_pieces)
            feed_rest = from_chips(feed_pieces[0], far_steps)
            if len(states) < segments - 1:
                states.append(shift(states[-1], 1))
    attended, feed_far, feed_rest, near_shard = together(
        attended, feed_far, feed_rest, near_shard
    )
    feed_pieces += feed_rest + feed_far + from_core(feed_rest)
    near_pieces = [near_shard] + from_chips(near_shard, chips)
    flat_attended = attended.reshape(count, D)
    after_attn, active, slope, after_ffn = feed(
        place, layer_input.reshape(count, D), flat_attended, vec, feed_pieces
    )
    after_ffn, near_pieces = together(after_ffn, near_pieces)
    while len(states) < segments - 1:
        states.append(shift(states[-1], 1))
    near_pieces += from_core(near_pieces)
    output, row_grads, after_grad, gate_small, near_half, far_half = near(
        place, ids, near_rows, states, after_ffn.reshape(batch, SEG, D), out_grad, active, vec,
        near_pieces,
    )

    near_arrived = swap(far_half, "fsdp", 1)
    (message,) = give(place, ids, row_grads, None, (segments - 1,))
    message, near_arrived, after_grad, row_grads = together(
        message, near_arrived, after_grad, row_grads
    )
    arrived = shift(message, -1)
    near_sums = core_sums(near_half, near_arrived)
    near_sums, after_grad = together(near_sums, after_grad)
    near_total = [near_sums[0]] + to_chips(near_sums, chips)
    grad_after, att_grad, feed_small, feed_half, feed_far = feed_back(
        place, after_grad.reshape(count, D), after_attn, slope, flat_attended, vec, feed_pieces
    )
    feed_half, feed_far, att_grad, row_grads, arrived, near_total = together(
        feed_half, feed_far, att_grad, row_grads, arrived, near_total
    )
    near_low = chip_sum(near_total)
    feed_arrived = swap(feed_far, "fsdp", 1)
    near_pair = (near_low, swap(near_low, "seq", steps[0]))
    row_grads, near_low = together(row_grads, near_low)
    for distance in range(segments - 2, 1, -1):
        (message,) = give(place, ids, row_grads, arrived, (distance,))
        if distance > 2:
            arrived = shift(message, -1)
        row_grads, message, feed_arrived = together(row_grads, message, feed_arrived)
    feed_sums = core_sums(feed_half, feed_arrived)
    feed_sums, row_grads = together(feed_sums, row_grads)
    feed_total = [feed_sums[0]] + to_chips(feed_sums, chips)
    sent, own = give(place, ids, row_grads, None, (1, 0))
    if segments > 3:
        sent, own, message = together(sent, own, message)
        arrived = shift(message, -1)
    att_grad, sent, near_pair = together(att_grad, sent, near_pair)
    *pieces, first_diag = attend_back(
        joined, memory, att_grad.reshape(batch, SEG, D), attended, probs[0], 0, []
    )
    pieces, feed_total, arrived = together(pieces, feed_total, arrived)
    feed_low = chip_sum(feed_total)
    for step in steps[1:]:
        near_low = pair_sum(*near_pair)
        near_low, feed_low = together(near_low, feed_low)
        near_pair = (near_low, swap(near_low, "seq", step))
    feed_pair = (feed_low, swap(feed_low, "seq", steps[0]))
    *pieces, last_diag = attend_back(
        joined, memory, att_grad.reshape(batch, SEG, D), attended, probs[1], PAIRS, pieces
    )
    pieces, feed_pair = together(pieces, feed_pair)
    diag = jnp.concatenate([first_diag.reshape(-1, SPAN), last_diag.reshape(-1, SPAN)], axis=0)
    partial, message, attn_half, attn_far = finish(
        place, devices, parts, layer_input, before, pieces, grad_after.reshape(batch, SEG, D),
        own, sent, arrived, vec, attn_w, gate_small, feed_small, diag,
    )
    partial, message, attn_half, attn_far, near_pair = together(
        partial, message, attn_half, attn_far, near_pair
    )
    last = shift(message, -1)
    attn_arrived = swap(attn_far, "fsdp", 1)
    for step in steps[1:]:
        feed_low = pair_sum(*feed_pair)
        feed_pair = (feed_low, swap(feed_low, "seq", step))
    attn_sums = core_sums(attn_half, attn_arrived)
    attn_total = [attn_sums[0]] + to_chips(attn_sums, chips)
    near_grads = unpack(near_pair, ((1, D), (1, 2 * D), (1, D), (ratio, D)))
    near_grads, attn_total, last = together(near_grads, attn_total, last)
    attn_low = chip_sum(attn_total)
    for step in steps[:-1]:
        attn_low = pair_sum(attn_low, swap(attn_low, "seq", step))
    attn_pair = (attn_low, swap(attn_low, "seq", steps[-1]))
    input_grad = partial + last.astype(F32)
    feed_grads = unpack(feed_pair, ((1, ff), (1, D)))
    input_grad, feed_grads, attn_pair = together(input_grad, feed_grads, attn_pair)
    project_grad, *smalls = unpack(attn_pair, ((1, 3 * D),), parts + [position_bias.shape[0]])
    return (
        output,
        input_grad,
        smalls[0],
        smalls[1],
        project_grad,
        feed_grads[1],
        smalls[7],
        smalls[2],
        smalls[3],
        feed_grads[0],
        smalls[6],
        near_grads[3],
        smalls[4],
        *near_grads[:3],
        smalls[5],
    )


def solution(mesh):
    in_specs = (
        P("fsdp", "seq", None),
        P("fsdp", "seq", None),
        P("fsdp", "seq", None),
        P("fsdp"),
        P("fsdp"),
        P("fsdp", None),
        P("fsdp", None),
        P("fsdp"),
        P("fsdp"),
        P("fsdp"),
        P("fsdp", None),
        P("fsdp"),
        P("fsdp", None),
        P("fsdp"),
        P("fsdp", None),
        P("fsdp", None),
        P("fsdp", None),
        P("fsdp"),
    )
    out_specs = (
        P("fsdp", "seq", None),
        P("fsdp", "seq", None),
        P("fsdp"),
        P("fsdp"),
        P("fsdp", None),
        P("fsdp", None),
        P("fsdp"),
        P("fsdp"),
        P("fsdp"),
        P("fsdp", None),
        P("fsdp"),
        P("fsdp", None),
        P("fsdp"),
        P("fsdp", None),
        P("fsdp", None),
        P("fsdp", None),
        P("fsdp"),
    )
    return jax.shard_map(
        on_device, mesh=mesh, in_specs=in_specs, out_specs=out_specs, check_vma=False
    )
```

```python
import functools
import math

import jax
import jax.numpy as jnp
import numpy as np
from jax import lax
from jax.experimental import pallas as pl
from jax.experimental.pallas import tpu as pltpu
from jax.sharding import PartitionSpec as P

D = 512
H = 8
HD = 64
K = 4
SEG = 512
NB = 32

EPS = 1e-05
HIGH = lax.Precision.HIGHEST
MASKED = -1e30
F32 = jnp.float32
BF16 = jnp.bfloat16
ROWS = 256
SPAN = 2 * SEG + 128
VMEM = 56 << 20


def nn(left, right):
    return lax.dot_general(left, right, (((1,), (0,)), ((), ())), preferred_element_type=F32)


def nt(left, right):
    return lax.dot_general(left, right, (((1,), (1,)), ((), ())), preferred_element_type=F32)


def tn(left, right):
    return lax.dot_general(left, right, (((0,), (0,)), ((), ())), preferred_element_type=F32)


def shape(dims, dtype):
    return jax.ShapeDtypeStruct(tuple(dims), dtype)


def whole(dims):
    zeros = (0,) * len(dims)
    return pl.BlockSpec(tuple(dims), lambda *_: zeros, pipeline_mode=pl.Buffered(1))


def scalars():
    return pl.BlockSpec(memory_space=pltpu.SMEM)


def params(grid_rank):
    return pltpu.CompilerParams(
        dimension_semantics=("arbitrary",) * grid_rank, vmem_limit_bytes=VMEM
    )


def cost(flops, moved, exps=0):
    return pl.CostEstimate(
        flops=int(flops / 30), bytes_accessed=int(moved / 30), transcendentals=int(exps / 30)
    )


def thresholds():
    half_count = NB // 2
    spread_ratio = 2.0 * SEG / half_count
    exact_part = list(range(1, half_count))
    log_part = [
        int(half_count * spread_ratio ** ((bucket_index - half_count) / half_count))
        for bucket_index in range(half_count, NB)
    ]
    return np.array(exact_part + log_part)


def bucket_of(distance):
    return (distance[:, None] >= thresholds()[None, :]).sum(axis=1)


def forward_selector():
    distance = np.arange(SPAN) - 128
    bucket = bucket_of(np.maximum(distance, 0))
    return (np.arange(NB)[:, None] == bucket[None, :]).astype(np.float32)


def backward_selector():
    chosen = forward_selector().T.copy()
    chosen[:128] = 0.0
    return chosen


def norm(values):
    average = jnp.mean(values, axis=-1, keepdims=True)
    centred = values - average
    variance = jnp.mean(centred * centred, axis=-1, keepdims=True)
    rstd_value = lax.rsqrt(variance + EPS)
    return centred * rstd_value, rstd_value


def norm_back(grad_result, hat_value, rstd_value, gain):
    scaled = grad_result * gain
    return rstd_value * (
        scaled
        - jnp.mean(scaled, axis=-1, keepdims=True)
        - hat_value * jnp.mean(scaled * hat_value, axis=-1, keepdims=True)
    )


def rows_sum(values):
    return jnp.sum(values, axis=0, keepdims=True)


def pair_mask(head, values):
    lane = lax.broadcasted_iota(jnp.int32, values.shape, 1)
    keep = lane < HD if head == 0 else lane >= HD
    return jnp.where(keep, values, jnp.zeros_like(values))


def pack_first_kernel(*refs):
    weight_ref, *vector_refs, out_ref = refs
    rows = weight_ref.shape[0]
    out_ref[:rows, :] = weight_ref[...]
    out_ref[rows:, :] = jnp.zeros((16, out_ref.shape[1]), BF16)
    for index, ref in enumerate(vector_refs):
        line = ref[...].astype(F32).reshape(1, -1).astype(BF16)
        out_ref[rows + index : rows + index + 1, : ref.shape[0]] = line


def pack_first(weight, vectors):
    rows, columns = weight.shape
    return pl.pallas_call(
        pack_first_kernel,
        out_shape=shape((rows + 16, columns), BF16),
        cost_estimate=cost(0, 4 * rows * columns),
        name="pack_first",
    )(weight, *vectors)


def pack_kernel(rows, *refs):
    out_ref = refs[-1]
    start = 0
    for ref in refs[:-1]:
        for chunk in range(ref.shape[0] // rows):
            out_ref[:, start : start + ref.shape[1]] = ref[chunk * rows : (chunk + 1) * rows, :]
            start += ref.shape[1]


def pack(rows, weights):
    columns = sum(w.size for w in weights) // rows
    return pl.pallas_call(
        functools.partial(pack_kernel, rows),
        out_shape=shape((rows, columns), BF16),
        cost_estimate=cost(0, 4 * rows * columns),
        name="pack",
    )(*weights)


def unpack_kernel(layout, terms, *refs):
    total = functools.reduce(jnp.add, [ref[...].astype(F32) for ref in refs[:terms]])
    refs = refs[terms:]
    rows = refs[0].shape[0]
    start = 0
    for ref, (chunks, width) in zip(refs, layout):
        for chunk in range(chunks):
            ref[chunk * rows : (chunk + 1) * rows, :] = total[:rows, start : start + width]
            start += width
    for index, ref in enumerate(refs[len(layout) :]):
        ref[...] = total[rows + index : rows + index + 1, : ref.shape[0]].reshape(-1)


def unpack(pair, layout, widths=()):
    rows = pair[0].shape[0] - (16 if widths else 0)
    outs = [shape((rows * chunks, width), F32) for chunks, width in layout]
    outs += [shape((width,), F32) for width in widths]
    return pl.pallas_call(
        functools.partial(unpack_kernel, layout, len(pair)),
        out_shape=outs,
        cost_estimate=cost(0, 8 * pair[0].size),
        name="unpack",
    )(*pair)


def device_of(place_ref, chip_step, core_step):
    index = place_ref[0]
    chip = lax.shift_right_logical(index, 1)
    core = jnp.bitwise_and(index, 1)
    return jnp.bitwise_xor(chip, chip_step) * 2 + jnp.bitwise_xor(core, core_step)


def assemble(place_ref, layout, piece_refs, out_refs):
    steps = len(piece_refs) // 2
    for core_step in range(2):
        for step in range(steps):
            ref = piece_refs[core_step * steps + step]
            owner = device_of(place_ref, step, core_step)
            rows = D // (2 * steps)
            start = 0
            for out_ref, (chunks, width) in zip(out_refs, layout):
                for chunk in range(chunks):
                    target = pl.multiple_of((owner * chunks + chunk) * rows, rows)
                    out_ref[pl.ds(target, rows), :] = ref[:rows, start : start + width]
                    start += width


def first_kernel(parts, count, place_ref, x_ref, select_ref, *refs):
    piece_refs = refs[:count]
    w_ref, vec_ref, line_ref, joined_ref, small_ref = refs[count:]

    @pl.when(pl.program_id(0) == 0)
    def _():
        assemble(place_ref, ((1, 3 * D),), piece_refs, [w_ref])
        steps = count // 2
        rows = D // count
        for core_step in range(2):
            for step in range(steps):
                owner = device_of(place_ref, step, core_step)
                small_ref[pl.ds(pl.multiple_of(owner * 16, 16), 16), :] = piece_refs[
                    core_step * steps + step
                ][rows:, : small_ref.shape[1]].astype(F32)
        vec_ref[...] = jnp.zeros_like(vec_ref)
        for row, width in enumerate(parts):
            pieces = [small_ref[16 * d + row : 16 * d + row + 1, :width] for d in range(count)]
            vec_ref[row : row + 1, : width * count] = jnp.concatenate(pieces, axis=1)
        row = len(parts)
        table = jnp.concatenate(
            [small_ref[16 * d + row : 16 * d + row + 1, : NB * H // count] for d in range(count)],
            axis=0,
        )
        by_distance = None
        for place in range(NB // count):
            part = lax.dot_general(
                table[:, place * H : (place + 1) * H],
                select_ref[place],
                (((0,), (0,)), ((), ())),
                precision=HIGH,
                preferred_element_type=F32,
            )
            by_distance = part if by_distance is None else by_distance + part
        lane = lax.broadcasted_iota(jnp.int32, by_distance.shape, 1)
        line_ref[...] = jnp.where(lane < 128, MASKED, by_distance)

    hat_value, _ = norm(x_ref[0].astype(F32))
    normed = (hat_value * vec_ref[0:1, :D] + vec_ref[1:2, :D]).astype(BF16)
    joined_ref[0] = nn(normed, w_ref[...]).astype(BF16)


def remember_kernel(x_ref, vec_ref, w_ref, out_ref):
    hat_value, _ = norm(x_ref[0].astype(F32))
    normed = (hat_value * vec_ref[0:1, :D] + vec_ref[1:2, :D]).astype(BF16)
    out_ref[0] = nn(normed, w_ref[:, D:]).astype(BF16)


def remember(before, vec, weight):
    batch = before.shape[0]

    def block(width):
        return pl.BlockSpec((1, SEG, width), lambda b: (b, 0, 0))

    return pl.pallas_call(
        remember_kernel,
        grid=(batch,),
        in_specs=[block(D), whole(vec.shape), whole(weight.shape)],
        out_specs=block(2 * D),
        out_shape=shape((batch, SEG, 2 * D), BF16),
        compiler_params=params(1),
        cost_estimate=cost(4 * batch * SEG * D * D, 6 * batch * SEG * D),
        name="remember",
    )(before, vec, weight)


def first(place, x, pieces, parts, ff):
    batch = x.shape[0]
    count = len(pieces)
    small_width = -(-max(parts) // 128) * 128
    select = forward_selector().reshape(count, NB // count, SPAN).transpose(1, 0, 2)

    def block(width):
        return pl.BlockSpec((1, SEG, width), lambda b: (b, 0, 0))

    return pl.pallas_call(
        functools.partial(first_kernel, parts, count),
        grid=(batch,),
        in_specs=[scalars(), block(D), whole(select.shape)]
        + [whole(piece.shape) for piece in pieces],
        out_specs=[whole((D, 3 * D)), whole((8, ff)), whole((H, SPAN)), block(3 * D)],
        out_shape=[
            shape((D, 3 * D), BF16),
            shape((8, ff), F32),
            shape((H, SPAN), F32),
            shape((batch, SEG, 3 * D), BF16),
        ],
        scratch_shapes=[pltpu.VMEM((16 * count, small_width), F32)],
        compiler_params=params(1),
        cost_estimate=cost(6 * batch * SEG * D * D, 8 * batch * SEG * D),
        name="first",
    )(place, x, jnp.asarray(select), *pieces)


def tiles(place_ref, line_ref, first, own_ref, mem_ref):
    hidden = jnp.where(place_ref[1] > 0, 0.0, MASKED)
    for head in range(2):
        index = 2 * (first + pl.program_id(0)) + head
        line = jnp.broadcast_to(line_ref[pl.ds(index, 1), :], (8, SPAN))
        line = pltpu.roll(line, 0, 1, stride=1, stride_axis=0)
        for group in range(16):
            moved = pltpu.roll(line, 8 * group, 1) if group else line
            for tile in range(2 * SEG // 128):
                start = 2 * SEG - 128 * tile
                row = 128 * tile + 8 * group
                piece = moved[:, start : start + 128]
                own_ref[head, row : row + 8, :] = piece
                mem_ref[head, row : row + 8, :] = piece + hidden


def attend_kernel(first, place_ref, q_ref, k_ref, v_ref, km_ref, vm_ref, line_ref, *refs):
    out_ref, prob_ref, own_ref, mem_ref = refs[-4:]

    @pl.when(pl.program_id(1) == 0)
    def _():
        tiles(place_ref, line_ref, first, own_ref, mem_ref)

    keys = jnp.concatenate([km_ref[0], k_ref[0]], axis=0)
    values = jnp.concatenate([vm_ref[0], v_ref[0]], axis=0)
    for half in range(SEG // ROWS):
        width = SEG + (half + 1) * ROWS
        span = slice(half * ROWS, (half + 1) * ROWS)
        query = q_ref[0, span, :] * BF16(HD**-0.5)
        total = None
        for head in range(2):
            scores = nt(keys[:width], pair_mask(head, query))
            columns = []
            for part in range(ROWS // 128):
                block = half * (ROWS // 128) + part
                bias = jnp.concatenate(
                    [
                        mem_ref[head, (3 - block) * 128 : (7 - block) * 128, :],
                        own_ref[head, (7 - block) * 128 :, :],
                    ],
                    axis=0,
                )
                used = bias.shape[0]
                piece = scores[:used, part * 128 : (part + 1) * 128] + bias
                top = jnp.max(piece, axis=0, keepdims=True)
                weight = jnp.exp(piece - top)
                weight = (weight * (1.0 / jnp.sum(weight, axis=0, keepdims=True))).astype(BF16)
                if used < width:
                    weight = jnp.concatenate(
                        [weight, jnp.zeros((width - used, 128), BF16)], axis=0
                    )
                columns.append(weight)
            probs = jnp.concatenate(columns, axis=1)
            prob_ref[0, head, :width, span] = probs
            product = tn(probs, pair_mask(head, values)[:width])
            total = product if total is None else total + product
        out_ref[0, span, :] = total.astype(BF16)


PAIRS = H // 4


def attend(place, joined, memory, line, first, so_far):
    batch = joined.shape[0]

    def lanes(offset):
        return pl.BlockSpec((1, SEG, 128), lambda h, b: (b, 0, offset + first + h))

    work = batch * H * SEG * SEG
    extra = [] if so_far is None else [so_far]
    return pl.pallas_call(
        functools.partial(attend_kernel, first),
        grid=(PAIRS, batch),
        in_specs=[scalars()]
        + [lanes(0), lanes(2 * PAIRS), lanes(4 * PAIRS), lanes(0), lanes(2 * PAIRS)]
        + [whole(line.shape)]
        + [pl.BlockSpec(memory_space=pl.ANY)] * len(extra),
        out_specs=[
            lanes(0),
            pl.BlockSpec((1, 2, 2 * SEG, SEG), lambda h, b: (b, h, 0, 0)),
        ],
        out_shape=[shape((batch, SEG, D), BF16), shape((batch, H // 2, 2 * SEG, SEG), BF16)],
        scratch_shapes=[pltpu.VMEM((2, 2 * SEG, 128), F32)] * 2,
        input_output_aliases={7: 0} if extra else {},
        compiler_params=params(2),
        cost_estimate=cost(16 * HD * work, 3 * work, work),
        name="attend",
    )(place, joined, joined, joined, memory, memory, line, *extra)


def attend_back_kernel(
    q_ref, k_ref, v_ref, km_ref, vm_ref, grad_ref, out_ref, prob_ref, *refs
):
    dq_ref, dk_ref, dv_ref, dkm_ref, dvm_ref, diag_ref, grid_ref = refs[-7:]
    keys = jnp.concatenate([km_ref[0], k_ref[0]], axis=0)
    values = jnp.concatenate([vm_ref[0], v_ref[0]], axis=0)
    step = pl.program_id(1)

    @pl.when(step == 0)
    def _():
        grid_ref[...] = jnp.zeros_like(grid_ref)

    key_parts = []
    value_parts = []
    for half in range(SEG // ROWS):
        width = SEG + (half + 1) * ROWS
        span = slice(half * ROWS, (half + 1) * ROWS)
        grad = grad_ref[0, span, :]
        query = q_ref[0, span, :] * BF16(HD**-0.5)
        product = (grad.astype(F32) * out_ref[0, span, :].astype(F32)).T
        query_total = key_total = value_total = None
        for head in range(2):
            grad_head = pair_mask(head, grad)
            delta = jnp.sum(product[head * HD : (head + 1) * HD], axis=0, keepdims=True)
            probs = prob_ref[0, head, :width, span]
            scored = probs.astype(F32) * (nt(values[:width], grad_head) - delta)
            for part in range(ROWS // 128):
                block = half * (ROWS // 128) + part
                used = SEG + (block + 1) * 128
                grid_ref[head, (3 - block) * 128 :, :] += scored[
                    :used, part * 128 : (part + 1) * 128
                ]
            scored = scored.astype(BF16)
            for_key = nn(scored, pair_mask(head, query))
            for_value = nn(probs, grad_head)
            for_query = tn(scored, pair_mask(head, keys)[:width])
            key_total = for_key if key_total is None else key_total + for_key
            value_total = for_value if value_total is None else value_total + for_value
            query_total = for_query if query_total is None else query_total + for_query
        dq_ref[0, span, :] = (query_total * HD**-0.5).astype(BF16)
        key_parts.append(key_total)
        value_parts.append(value_total)
    for pieces, mem_ref, own_ref in (
        (key_parts, dkm_ref, dk_ref),
        (value_parts, dvm_ref, dv_ref),
    ):
        both = pieces[0] + pieces[1][: SEG + ROWS]
        mem_ref[0] = both[:SEG].astype(BF16)
        own_ref[0, :ROWS] = both[SEG:].astype(BF16)
        own_ref[0, ROWS:] = pieces[1][SEG + ROWS :].astype(BF16)

    @pl.when(step == pl.num_programs(1) - 1)
    def _():
        for head in range(2):
            total = None
            for group in range(16):
                pieces = [
                    grid_ref[head, 128 * tile + 8 * group : 128 * tile + 8 * group + 8, :]
                    for tile in reversed(range(2 * SEG // 128))
                ]
                line = jnp.concatenate([jnp.zeros((8, 128), F32)] + pieces, axis=1)
                if group:
                    line = pltpu.roll(line, SPAN - 8 * group, 1)
                total = line if total is None else total + line
            lines = [total[:1]] + [
                pltpu.roll(total[row : row + 1], SPAN - row, 1) for row in range(1, 8)
            ]
            diag_ref[0, head : head + 1, :] = functools.reduce(jnp.add, lines)


def attend_back(joined, memory, grad, attended, probs, first, so_far):
    batch = joined.shape[0]

    def lanes(offset):
        return pl.BlockSpec((1, SEG, 128), lambda h, b: (b, 0, offset + first + h))

    half = shape((batch, SEG, D), BF16)
    work = batch * H * SEG * SEG
    return pl.pallas_call(
        attend_back_kernel,
        grid=(PAIRS, batch),
        in_specs=[lanes(0), lanes(2 * PAIRS), lanes(4 * PAIRS), lanes(0), lanes(2 * PAIRS)]
        + [lanes(0)] * 2
        + [pl.BlockSpec((1, 2, 2 * SEG, SEG), lambda h, b: (b, h, 0, 0))]
        + [pl.BlockSpec(memory_space=pl.ANY)] * len(so_far),
        out_specs=[lanes(0)] * 5 + [pl.BlockSpec((1, 2, SPAN), lambda h, b: (h, 0, 0))],
        out_shape=[half] * 5 + [shape((PAIRS, 2, SPAN), F32)],
        scratch_shapes=[pltpu.VMEM((2, 2 * SEG, 128), F32)],
        input_output_aliases={8 + i: i for i in range(len(so_far))},
        compiler_params=params(2),
        cost_estimate=cost(32 * HD * work, 3 * work),
        name="attend_back",
    )(joined, joined, joined, memory, memory, grad, attended, probs, *so_far)


def feed_layout(ff):
    return ((1, D), (1, ff), (ff // D, D))


def feed_scratch(ff):
    return [pltpu.VMEM((D, D), BF16), pltpu.VMEM((D, ff), BF16), pltpu.VMEM((ff, D), BF16)]


def feed_kernel(count, place_ref, x_ref, att_ref, vec_ref, *refs):
    piece_refs = refs[:count]
    (
        after_attn_ref, active_ref, slope_ref, after_ffn_ref, merge_ref, expand_ref, reduce_ref,
    ) = refs[count:]

    @pl.when(pl.program_id(0) == 0)
    def _():
        assemble(place_ref, feed_layout(expand_ref.shape[1]), piece_refs, refs[-3:])

    after_attn = x_ref[...].astype(F32) + nn(att_ref[...], merge_ref[...])
    after_attn_ref[...] = after_attn
    hat_value, _ = norm(after_attn)
    normed = (hat_value * vec_ref[2:3, :D] + vec_ref[3:4, :D]).astype(BF16)
    pre = nn(normed, expand_ref[...]) + vec_ref[6:7, :]
    cdf = 0.5 * (1.0 + lax.erf(pre * (1.0 / math.sqrt(2.0))))
    slope = cdf + pre * jnp.exp(-0.5 * pre * pre) * (1.0 / math.sqrt(2.0 * math.pi))
    slope_ref[...] = slope.astype(BF16)
    active = (pre * cdf).astype(BF16)
    active_ref[...] = active
    after_ffn = after_attn + nn(active, reduce_ref[...]) + vec_ref[4:5, :D]
    after_ffn_ref[...] = after_ffn


def feed(place, x, attended, vec, pieces):
    count = x.shape[0]
    ff = vec.shape[1]

    def rows(width):
        return pl.BlockSpec((ROWS, width), lambda i: (i, 0))

    return pl.pallas_call(
        functools.partial(feed_kernel, len(pieces)),
        grid=(count // ROWS,),
        in_specs=[scalars(), rows(D), rows(D), whole(vec.shape)]
        + [whole(piece.shape) for piece in pieces],
        out_specs=[rows(D), rows(ff), rows(ff), rows(D)],
        out_shape=[
            shape((count, D), F32),
            shape((count, ff), BF16),
            shape((count, ff), BF16),
            shape((count, D), F32),
        ],
        scratch_shapes=feed_scratch(ff),
        compiler_params=params(1),
        cost_estimate=cost(4 * count * D * (ff + D), 12 * count * ff, 2 * count * ff),
        name="feed",
    )(place, x, attended, vec, *pieces)


def add_rows(ref, row, values):
    ref[row : row + 1, : values.shape[1]] += values


def scatter_rows(place_ref, total_ref, near_ref, far_ref, start, chunks):
    steps, rows = near_ref.shape[0], near_ref.shape[1]
    width = total_ref.shape[1]
    for core_step, ref in ((0, near_ref), (1, far_ref)):
        for step in range(steps):
            owner = device_of(place_ref, step, core_step)
            for chunk in range(chunks):
                source = pl.multiple_of((owner * chunks + chunk) * rows, rows)
                column = start + chunk * width
                ref[step, :, column : column + width] = total_ref[
                    pl.ds(source, rows), :
                ].astype(BF16)
    return start + chunks * width


def feed_back_kernel(
    count, place_ref, grad_ref, after_ref, active_ref, slope_ref, att_ref, vec_ref, *refs
):
    piece_refs = refs[:count]
    (
        after_grad_ref, att_grad_ref, small_ref, near_ref, far_ref,
        expand_total, reduce_total, merge_total, merge_ref, expand_ref, reduce_ref,
    ) = refs[count:]
    step = pl.program_id(0)

    @pl.when(step == 0)
    def _():
        assemble(place_ref, feed_layout(expand_ref.shape[1]), piece_refs, refs[-3:])
        expand_total[...] = jnp.zeros_like(expand_total)
        merge_total[...] = jnp.zeros_like(merge_total)
        reduce_total[...] = jnp.zeros_like(reduce_total)
        small_ref[...] = jnp.zeros_like(small_ref)

    grad = grad_ref[...]
    low = grad.astype(BF16)
    add_rows(small_ref, 2, rows_sum(low.astype(F32)))
    reduce_total[...] += tn(active_ref[...], low)
    pre_grad = (nt(low, reduce_ref[...]) * slope_ref[...].astype(F32)).astype(BF16)
    add_rows(small_ref, 3, rows_sum(pre_grad.astype(F32)))
    hat_value, rstd_value = norm(after_ref[...])
    gain = vec_ref[2:3, :D]
    normed = (hat_value * gain + vec_ref[3:4, :D]).astype(BF16)
    expand_total[...] += tn(normed, pre_grad)
    normed_grad = nt(pre_grad, expand_ref[...])
    add_rows(small_ref, 0, rows_sum(normed_grad * hat_value))
    add_rows(small_ref, 1, rows_sum(normed_grad))
    after_grad = grad + norm_back(normed_grad, hat_value, rstd_value, gain)
    after_grad_ref[...] = after_grad
    merge_grad = after_grad.astype(BF16)
    merge_total[...] += tn(att_ref[...], merge_grad)
    att_grad_ref[...] = nt(merge_grad, merge_ref[...]).astype(BF16)

    @pl.when(step == pl.num_programs(0) - 1)
    def _():
        start = scatter_rows(place_ref, expand_total, near_ref, far_ref, 0, 1)
        ratio = reduce_total.shape[0] // D
        start = scatter_rows(place_ref, reduce_total, near_ref, far_ref, start, ratio)
        scatter_rows(place_ref, merge_total, near_ref, far_ref, start, 1)


def feed_back(place, grad, after_attn, active, slope, attended, vec, pieces):
    count = grad.shape[0]
    ff = vec.shape[1]
    devices = len(pieces)

    def rows(width):
        return pl.BlockSpec((ROWS, width), lambda i: (i, 0))

    packed = (devices // 2, D // devices, 2 * ff + D)
    return pl.pallas_call(
        functools.partial(feed_back_kernel, devices),
        grid=(count // ROWS,),
        in_specs=[scalars(), rows(D), rows(D), rows(ff), rows(ff), rows(D), whole(vec.shape)]
        + [whole(piece.shape) for piece in pieces],
        out_specs=[rows(D), rows(D), whole((8, ff)), whole(packed), whole(packed)],
        out_shape=[
            shape((count, D), F32),
            shape((count, D), BF16),
            shape((8, ff), F32),
            shape(packed, BF16),
            shape(packed, BF16),
        ],
        scratch_shapes=[
            pltpu.VMEM((D, ff), F32),
            pltpu.VMEM((ff, D), F32),
            pltpu.VMEM((D, D), F32),
        ]
        + feed_scratch(ff),
        compiler_params=params(1),
        cost_estimate=cost(8 * count * D * (ff + D // 2), 12 * count * ff),
        name="feed_back",
    )(place, grad, after_attn, active, slope, attended, vec, *pieces)


def chosen_rows(ids, slot, rows):
    place = lax.broadcasted_iota(jnp.int32, (ids.shape[0], SEG), 1)
    return nn(jnp.where(ids[:, slot : slot + 1] == place, 1.0, 0.0).astype(BF16), rows)


def ids_down(ids):
    return jnp.concatenate([ids] * 2, axis=0).T


def take_kernel(place_ref, ids_ref, rows_ref, out_ref):
    ids = ids_down(ids_ref[0] - place_ref[1] * SEG)
    rows = rows_ref[0]
    for slot in range(K):
        out_ref[0, slot] = chosen_rows(ids, slot, rows).astype(BF16)


def take(place, ids, rows):
    batch = ids.shape[0]
    return pl.pallas_call(
        take_kernel,
        grid=(batch,),
        in_specs=[
            scalars(),
            pl.BlockSpec((1, K, SEG), lambda b: (b, 0, 0)),
            pl.BlockSpec((1, SEG, D), lambda b: (b, 0, 0)),
        ],
        out_specs=pl.BlockSpec((1, K, SEG, D), lambda b: (b, 0, 0, 0)),
        out_shape=shape((batch, K, SEG, D), BF16),
        compiler_params=params(1),
        cost_estimate=cost(2 * batch * K * SEG * SEG * D, 4 * batch * K * SEG * D),
        name="take",
    )(place, ids, rows)


def give_kernel(distances, started, place_ref, ids_ref, grad_ref, *refs):
    out_refs = refs[started:]
    place = lax.broadcasted_iota(jnp.int32, (SEG, SEG), 0)
    for index, distance in enumerate(distances):
        ids = ids_ref[0] - (place_ref[1] - distance) * SEG
        total = None
        for slot in range(K):
            chosen = jnp.where(ids[slot : slot + 1, :] == place, 1.0, 0.0).astype(BF16)
            part = nn(chosen, grad_ref[0, slot])
            total = part if total is None else total + part
        if started and index == 0:
            total = total + refs[0][0].astype(F32)
        out_refs[index][0] = total.astype(out_refs[index].dtype)


def give(place, ids, grads, arrived, distances):
    batch = ids.shape[0]
    block = pl.BlockSpec((1, SEG, D), lambda b: (b, 0, 0))
    started = arrived is not None
    work = len(distances) * batch * K * SEG * D
    return pl.pallas_call(
        functools.partial(give_kernel, distances, started),
        grid=(batch,),
        in_specs=[
            scalars(),
            pl.BlockSpec((1, K, SEG), lambda b: (b, 0, 0)),
            pl.BlockSpec((1, K, SEG, D), lambda b: (b, 0, 0, 0)),
        ]
        + [block] * started,
        out_specs=[block] * len(distances),
        out_shape=[shape((batch, SEG, D), BF16 if d else F32) for d in distances],
        compiler_params=params(1),
        cost_estimate=cost(2 * work * SEG, 2 * work),
        name="give",
    )(place, ids, grads, *([arrived] if started else []))


def near_kernel(
    hops, count, place_ref, ids_ref, rows_ref, after_ref, grad_ref, vec_ref, *refs
):
    state_refs = refs[:hops]
    piece_refs = refs[hops : hops + count]
    (
        out_ref, row_grad_ref, after_grad_ref, small_ref, near_ref, far_ref,
        keys_total, merge_total, query_total, nq_ref, keys_ref, merge_ref,
    ) = refs[hops + count :]
    first = (pl.program_id(0) == 0) & (pl.program_id(1) == 0)
    last = (pl.program_id(0) == pl.num_programs(0) - 1) & (
        pl.program_id(1) == pl.num_programs(1) - 1
    )

    @pl.when(first)
    def _():
        keys_total[...] = jnp.zeros_like(keys_total)
        merge_total[...] = jnp.zeros_like(merge_total)
        query_total[...] = jnp.zeros_like(query_total)
        assemble(place_ref, ((1, D), (1, 2 * D), (1, D)), piece_refs, refs[-3:])
        small_ref[...] = jnp.zeros_like(small_ref)

    scale = HD**-0.5
    place = lax.broadcasted_iota(jnp.int32, (K * D, 128), 0)
    lane = lax.broadcasted_iota(jnp.int32, (K * D, 128), 1)
    group = lax.shift_right_logical(place, 9) * H + jnp.bitwise_and(
        lax.shift_right_logical(place, 6), H - 1
    )
    gather = jnp.where(jnp.bitwise_and(lane, K * H - 1) == group, 1.0, 0.0).astype(BF16)
    lane = lax.broadcasted_iota(jnp.int32, (128, K * D), 0)
    place = lax.broadcasted_iota(jnp.int32, (128, K * D), 1)
    group = lax.shift_right_logical(place, 9) * H + jnp.bitwise_and(
        lax.shift_right_logical(place, 6), H - 1
    )
    spread = jnp.where(
        (jnp.bitwise_and(lane, K * H - 1) == group) & (lane < 2 * K * H), 1.0, 0.0
    ).astype(BF16)

    def over_slots(combine, values):
        values = combine(values, pltpu.roll(values, 2 * H, 1))
        return combine(values, pltpu.roll(values, H, 1))

    def to_rows(values):
        high = values.astype(BF16)
        low = (values - high.astype(F32)).astype(BF16)
        lane = lax.broadcasted_iota(jnp.int32, values.shape, 1)
        return nn(jnp.where(lane < K * H, high, low), spread)

    def slot_of(values, slot):
        return values[:, slot * D : (slot + 1) * D]

    after_ffn = after_ref[0]
    hidden_low = after_ffn.astype(BF16)
    query = nn(hidden_low, nq_ref[...]).astype(BF16)
    query_float = query.astype(F32)
    ids = ids_down(ids_ref[0])
    states = jnp.concatenate([ref[0] for ref in state_refs], axis=0) if hops else None
    taken = []
    for slot in range(K):
        total = rows_ref[0, slot]
        if hops:
            chosen = []
            for hop in range(hops):
                column = ids[:, slot : slot + 1] - (place_ref[1] - hop - 1) * SEG
                here = lax.broadcasted_iota(jnp.int32, (ids.shape[0], SEG), 1)
                chosen.append(jnp.where(column == here, 1.0, 0.0).astype(BF16))
            moved = nn(jnp.concatenate(chosen, axis=1), states)
            total = total + moved.astype(BF16)
        taken.append(total)
    pairs = [nn(rows, keys_ref[...]).astype(BF16) for rows in taken]
    near_key = [pair[:, :D] for pair in pairs]
    near_value = [pair[:, D:] for pair in pairs]
    products = jnp.concatenate([query * key for key in near_key], axis=1)
    scores = nn(products, gather) * scale
    weights = jnp.exp(scores - over_slots(jnp.maximum, scores))
    probs = weights / over_slots(jnp.add, weights)
    prob_rows = to_rows(probs)
    mixed = functools.reduce(
        jnp.add, [slot_of(prob_rows, i) * v.astype(F32) for i, v in enumerate(near_value)]
    ).astype(BF16)
    near_out = nn(mixed, merge_ref[...])
    gate_vector = vec_ref[5:6, :D]
    gate = jax.nn.sigmoid(jnp.sum(after_ffn * gate_vector, axis=-1, keepdims=True))
    out_ref[0] = (gate * after_ffn + (1.0 - gate) * near_out).astype(BF16)
    grad = grad_ref[0].astype(F32)
    gate_grad = (
        jnp.sum(grad * (after_ffn - near_out), axis=-1, keepdims=True) * gate * (1.0 - gate)
    )
    add_rows(small_ref, 0, rows_sum(gate_grad * after_ffn))
    near_grad = ((1.0 - gate) * grad).astype(BF16)
    merge_total[...] += tn(mixed, near_grad)
    mixed_low = nt(near_grad, merge_ref[...]).astype(BF16)
    mixed_grad = mixed_low.astype(F32)
    products = jnp.concatenate([mixed_low * value for value in near_value], axis=1)
    prob_grads = nn(products, gather)
    inner = over_slots(jnp.add, probs * prob_grads)
    score_rows = to_rows(probs * (prob_grads - inner) * scale)
    query_grad = None
    for slot in range(K):
        score_grad = slot_of(score_rows, slot)
        part = score_grad * near_key[slot].astype(F32)
        query_grad = part if query_grad is None else query_grad + part
        pair_grad = jnp.concatenate(
            [
                (score_grad * query_float).astype(BF16),
                (slot_of(prob_rows, slot) * mixed_grad).astype(BF16),
            ],
            axis=1,
        )
        keys_total[...] += tn(taken[slot], pair_grad)
        row_grad_ref[0, slot] = nt(pair_grad, keys_ref[...]).astype(BF16)
    query_grad = query_grad.astype(BF16)
    query_total[...] += tn(hidden_low, query_grad)
    after_grad_ref[0] = gate * grad + gate_grad * gate_vector + nt(query_grad, nq_ref[...])

    @pl.when(last)
    def _():
        start = scatter_rows(place_ref, query_total, near_ref, far_ref, 0, 1)
        start = scatter_rows(place_ref, keys_total, near_ref, far_ref, start, 1)
        scatter_rows(place_ref, merge_total, near_ref, far_ref, start, 1)


def near(place, ids, rows, states, after_ffn, grad, vec, pieces):
    batch = rows.shape[0]
    devices = len(pieces)
    row_block = pl.BlockSpec((1, K, ROWS, D), lambda b, i: (b, 0, i, 0))
    block = pl.BlockSpec((1, ROWS, D), lambda b, i: (b, i, 0))
    packed = (devices // 2, D // devices, 4 * D)
    count = batch * SEG
    return pl.pallas_call(
        functools.partial(near_kernel, len(states), devices),
        grid=(batch, SEG // ROWS),
        in_specs=[scalars(), pl.BlockSpec((1, K, ROWS), lambda b, i: (b, 0, i))]
        + [row_block, block, block, whole(vec.shape)]
        + [pl.BlockSpec((1, SEG, D), lambda b, i: (b, 0, 0))] * len(states)
        + [whole(piece.shape) for piece in pieces],
        out_specs=[block, row_block, block, whole((8, D)), whole(packed), whole(packed)],
        out_shape=[
            shape((batch, SEG, D), BF16),
            shape((batch, K, SEG, D), BF16),
            shape((batch, SEG, D), F32),
            shape((8, D), F32),
            shape(packed, BF16),
            shape(packed, BF16),
        ],
        scratch_shapes=[
            pltpu.VMEM((D, 2 * D), F32),
            pltpu.VMEM((D, D), F32),
            pltpu.VMEM((D, D), F32),
            pltpu.VMEM((D, D), BF16),
            pltpu.VMEM((D, 2 * D), BF16),
            pltpu.VMEM((D, D), BF16),
        ],
        compiler_params=params(2),
        cost_estimate=cost(
            2 * count * D * D * (11 * K + 6), count * D * (4 * K + 12), count * K * D
        ),
        name="near",
    )(place, ids, rows, after_ffn, grad, vec, *states, *pieces)


def finish_kernel(
    x_ref, before_ref, dq_ref, dk_ref, dv_ref, dkm_ref, dvm_ref, grad_ref, own_ref, sent_ref,
    arrived_ref, vec_ref, w_ref,
    part_ref, send_ref, normed_ref, normed_before_ref, small_ref,
):
    @pl.when(pl.program_id(0) == 0)
    def _():
        small_ref[...] = jnp.zeros_like(small_ref)

    gain = vec_ref[0:1, :D]
    shift_by = vec_ref[1:2, :D]
    hat_before, rstd_before = norm(before_ref[0].astype(F32))
    normed_before_ref[0] = (hat_before * gain + shift_by).astype(BF16)
    before_grad = nt(dkm_ref[0], w_ref[:, D : 2 * D]) + nt(dvm_ref[0], w_ref[:, 2 * D :])
    send_ref[0] = (
        sent_ref[0].astype(F32)
        + arrived_ref[0].astype(F32)
        + norm_back(before_grad, hat_before, rstd_before, gain)
    ).astype(BF16)
    hat_value, rstd_value = norm(x_ref[0].astype(F32))
    normed_ref[0] = (hat_value * gain + shift_by).astype(BF16)
    normed_grad = (
        nt(dq_ref[0], w_ref[:, :D])
        + nt(dk_ref[0], w_ref[:, D : 2 * D])
        + nt(dv_ref[0], w_ref[:, 2 * D :])
    )
    add_rows(small_ref, 0, rows_sum(normed_grad * hat_value) + rows_sum(before_grad * hat_before))
    add_rows(small_ref, 1, rows_sum(normed_grad) + rows_sum(before_grad))
    part_ref[0] = (
        grad_ref[0] + own_ref[0] + norm_back(normed_grad, hat_value, rstd_value, gain)
    )


def finish(x, before, pieces, grad, own, sent, arrived, vec, weight):
    batch = x.shape[0]
    block = pl.BlockSpec((1, SEG, D), lambda b: (b, 0, 0))
    low = shape((batch, SEG, D), BF16)
    return pl.pallas_call(
        finish_kernel,
        grid=(batch,),
        in_specs=[block] * 11 + [whole(w.shape) for w in (vec, weight)],
        out_specs=[block] * 4 + [whole((8, D))],
        out_shape=[shape((batch, SEG, D), F32), low, low, low, shape((8, D), F32)],
        compiler_params=params(1),
        cost_estimate=cost(10 * batch * SEG * D * D, 34 * batch * SEG * D),
        name="finish",
    )(x, before, *pieces, grad, own, sent, arrived, vec, weight)


def project_grad_kernel(
    parts, place_ref, normed_ref, normed_before_ref, dq_ref, dk_ref, dv_ref, dkm_ref, dvm_ref,
    norm_ref, gate_ref, feed_ref, select_ref, first_ref, last_ref,
    near_ref, far_ref, w_total, small_total,
):
    step = pl.program_id(0)

    @pl.when(step == 0)
    def _():
        w_total[...] = jnp.zeros_like(w_total)

    normed = normed_ref[0]
    normed_before = normed_before_ref[0]
    w_total[:, :D] += tn(normed, dq_ref[0])
    w_total[:, D : 2 * D] += tn(normed, dk_ref[0]) + tn(normed_before, dkm_ref[0])
    w_total[:, 2 * D :] += tn(normed, dv_ref[0]) + tn(normed_before, dvm_ref[0])

    @pl.when(step == pl.num_programs(0) - 1)
    def _():
        devices = small_total.shape[0] // 16
        rows = w_total.shape[0] // devices
        small_total[...] = jnp.zeros_like(small_total)
        lines = [
            norm_ref[0:1, :],
            norm_ref[1:2, :],
            feed_ref[0:1, :D],
            feed_ref[1:2, :D],
            feed_ref[2:3, :D],
            gate_ref[0:1, :],
            feed_ref[3:4, :],
        ]
        for index, (line, width) in enumerate(zip(lines, parts)):
            for d in range(devices):
                row = 16 * d + index
                small_total[row : row + 1, :width] = line[:, d * width : (d + 1) * width]
        table = lax.dot_general(
            jnp.concatenate([ref[i] for ref in (first_ref, last_ref) for i in range(PAIRS)], axis=0),
            select_ref[...],
            (((1,), (0,)), ((), ())),
            precision=HIGH,
            preferred_element_type=F32,
        )
        own_buckets = NB // devices
        bucket = lax.broadcasted_iota(jnp.int32, (devices, NB), 1)
        owner = lax.broadcasted_iota(jnp.int32, (devices, NB), 0)
        pieces = []
        for place in range(own_buckets):
            chosen = jnp.where(bucket == owner * own_buckets + place, 1.0, 0.0)
            pieces.append(
                lax.dot_general(
                    chosen,
                    table,
                    (((1,), (1,)), ((), ())),
                    precision=HIGH,
                    preferred_element_type=F32,
                )
            )
        buckets = jnp.concatenate(pieces, axis=1)
        for d in range(devices):
            row = 16 * d + len(parts)
            small_total[row : row + 1, : buckets.shape[1]] = buckets[d : d + 1, :]
        width = small_total.shape[1]
        for core_step, ref in ((0, near_ref), (1, far_ref)):
            for chip_step in range(ref.shape[0]):
                target = device_of(place_ref, chip_step, core_step)
                source = pl.multiple_of(target * rows, rows)
                ref[chip_step, :rows, :] = w_total[pl.ds(source, rows), :].astype(BF16)
                ref[chip_step, rows:, :] = jnp.zeros((16, ref.shape[2]), BF16)
                lines = small_total[pl.ds(pl.multiple_of(target * 16, 16), 16), :]
                ref[chip_step, rows:, :width] = lines.astype(BF16)


def project_grad(place, devices, parts, normed, normed_before, pieces, norm_small, gate, feed_small, diags):
    batch = normed.shape[0]
    block = pl.BlockSpec((1, SEG, D), lambda b: (b, 0, 0))
    packed = (devices // 2, D // devices + 16, 3 * D)
    select = jnp.asarray(backward_selector())
    small_width = -(-max(parts) // 128) * 128
    return pl.pallas_call(
        functools.partial(project_grad_kernel, parts),
        grid=(batch,),
        in_specs=[scalars()]
        + [block] * 7
        + [whole(w.shape) for w in (norm_small, gate, feed_small, select, *diags)],
        out_specs=[whole(packed)] * 2,
        out_shape=[shape(packed, BF16)] * 2,
        scratch_shapes=[
            pltpu.VMEM((D, 3 * D), F32),
            pltpu.VMEM((16 * devices, small_width), F32),
        ],
        compiler_params=params(1),
        cost_estimate=cost(10 * batch * SEG * D * D, 20 * batch * SEG * D),
        name="project_grad",
    )(
        place, normed, normed_before, *pieces, norm_small, gate, feed_small, select, *diags,
    )


def shift(block, distance):
    count = lax.axis_size("seq")
    return lax.ppermute(block, "seq", [(i, (i + distance) % count) for i in range(count)])


def swap(block, axis, bits):
    count = lax.axis_size(axis)
    return lax.ppermute(block, axis, [(i, i ^ bits) for i in range(count)])


def together(*values):
    return lax.optimization_barrier(values)


def chip_steps():
    steps = list(range(1, lax.axis_size("fsdp") // 2))
    cut = (2 * len(steps) + 2) // 3
    return steps[:cut], steps[cut:]


def from_chips(shard, steps):
    return [swap(shard, "fsdp", 2 * step) for step in steps]


def from_core(pieces):
    return [swap(piece, "fsdp", 1) for piece in pieces]


def core_sums(near_half, arrived):
    return [
        (near_half[step].astype(F32) + arrived[step].astype(F32)).astype(BF16)
        for step in range(near_half.shape[0])
    ]


def to_chips(pieces, steps):
    return [swap(pieces[step], "fsdp", 2 * step) for step in steps]


def chip_sum(pieces):
    return functools.reduce(jnp.add, [piece.astype(F32) for piece in pieces]).astype(BF16)


def segment_steps():
    return [1 << bit for bit in range(lax.axis_size("seq").bit_length() - 1)]


def halves(values, bit):
    half = values.shape[1] // 2
    high = jnp.bitwise_and(lax.axis_index("seq"), bit) > 0
    left, right = values[:, :half], values[:, half:]
    return jnp.where(high, right, left), jnp.where(high, left, right)


def joined_halves(mine, other, bit):
    high = jnp.bitwise_and(lax.axis_index("seq"), bit) > 0
    return jnp.concatenate([jnp.where(high, other, mine), jnp.where(high, mine, other)], axis=1)


def pair_sum(left, right):
    return (left.astype(F32) + right.astype(F32)).astype(BF16)


def on_device(
    layer_input,
    neighbour_ids,
    out_grad,
    attn_norm_gain,
    attn_norm_bias,
    attn_project,
    attn_merge,
    position_bias,
    ffn_norm_gain,
    ffn_norm_bias,
    ffn_expand,
    expand_bias,
    ffn_reduce,
    reduce_bias,
    near_query,
    near_keys,
    near_merge,
    gate_vector,
):
    batch = layer_input.shape[0]
    count = batch * SEG
    devices = lax.axis_size("fsdp")
    segments = lax.axis_size("seq")
    rows = attn_project.shape[0]
    ff = ffn_expand.shape[1]
    ratio = ff // D

    place = jnp.stack([lax.axis_index("fsdp"), lax.axis_index("seq")]).astype(jnp.int32)
    vectors = [
        attn_norm_gain, attn_norm_bias, ffn_norm_gain, ffn_norm_bias, reduce_bias, gate_vector,
        expand_bias, position_bias,
    ]
    parts = [v.shape[0] for v in vectors[:-1]]
    steps = segment_steps()
    near_steps, far_steps = chip_steps()
    chips = near_steps + far_steps

    attn_shard = pack_first(attn_project, vectors)
    attn_pieces = [attn_shard] + from_chips(attn_shard, chips)
    before = shift(layer_input, 1)
    ids = jnp.swapaxes(neighbour_ids, 1, 2)
    feed_shard = pack(rows, [attn_merge, ffn_expand, ffn_reduce])
    near_shard = pack(rows, [near_query, near_keys, near_merge])
    near_rows = take(place, ids, layer_input)
    near_rows, feed_shard, near_shard, attn_pieces = together(
        near_rows, feed_shard, near_shard, attn_pieces
    )
    feed_pieces = [feed_shard] + from_chips(feed_shard, near_steps)
    attn_w, vec, line, joined = first(
        place, layer_input, attn_pieces + from_core(attn_pieces), parts, ff
    )
    joined, before = together(joined, before)
    states = [before]
    if segments > 2:
        states.append(shift(before, 1))
    memory = remember(before, vec, attn_w)
    attended = None
    probs = []
    for part in range(2):
        attended, part_probs = attend(place, joined, memory, line, part * PAIRS, attended)
        probs.append(part_probs)
        if part == 0:
            attended, memory, feed_pieces = together(attended, memory, feed_pieces)
            feed_far = from_core(feed_pieces)
            feed_rest = from_chips(feed_pieces[0], far_steps)
    attended, states = together(attended, states)
    if len(states) < segments - 1:
        states.append(shift(states[-1], 1))
    attended, feed_far, feed_rest, near_shard = together(
        attended, feed_far, feed_rest, near_shard
    )
    feed_pieces += feed_rest + feed_far + from_core(feed_rest)
    near_pieces = [near_shard] + from_chips(near_shard, chips)
    flat_attended = attended.reshape(count, D)
    after_attn, active, slope, after_ffn = feed(
        place, layer_input.reshape(count, D), flat_attended, vec, feed_pieces
    )
    after_ffn, near_pieces = together(after_ffn, near_pieces)
    while len(states) < segments - 1:
        states.append(shift(states[-1], 1))
    near_pieces += from_core(near_pieces)
    output, row_grads, after_grad, gate_small, near_half, far_half = near(
        place, ids, near_rows, states, after_ffn.reshape(batch, SEG, D), out_grad, vec,
        near_pieces,
    )

    near_arrived = swap(far_half, "fsdp", 1)
    (message,) = give(place, ids, row_grads, None, (segments - 1,))
    message, near_arrived, after_grad, row_grads = together(
        message, near_arrived, after_grad, row_grads
    )
    arrived = shift(message, -1)
    near_sums = core_sums(near_half, near_arrived)
    near_sums, after_grad = together(near_sums, after_grad)
    near_total = [near_sums[0]] + to_chips(near_sums, chips)
    grad_after, att_grad, feed_small, feed_half, feed_far = feed_back(
        place, after_grad.reshape(count, D), after_attn, active, slope, flat_attended, vec,
        feed_pieces,
    )
    feed_half, feed_far, att_grad, row_grads, arrived, near_total = together(
        feed_half, feed_far, att_grad, row_grads, arrived, near_total
    )
    near_low = chip_sum(near_total)
    feed_arrived = swap(feed_far, "fsdp", 1)
    near_pair = (near_low, swap(near_low, "seq", steps[0]))
    row_grads, near_low = together(row_grads, near_low)
    for distance in range(segments - 2, 1, -1):
        (message,) = give(place, ids, row_grads, arrived, (distance,))
        row_grads, message, feed_arrived, near_pair = together(
            row_grads, message, feed_arrived, near_pair
        )
        arrived = shift(message, -1)
    feed_sums = core_sums(feed_half, feed_arrived)
    feed_sums, row_grads = together(feed_sums, row_grads)
    feed_total = [feed_sums[0]] + to_chips(feed_sums, chips)
    sent, own = give(place, ids, row_grads, None, (1, 0))
    att_grad, sent = together(att_grad, sent)
    *pieces, first_diag = attend_back(
        joined, memory, att_grad.reshape(batch, SEG, D), attended, probs[0], 0, []
    )
    pieces, feed_total, arrived = together(pieces, feed_total, arrived)
    feed_low = chip_sum(feed_total)
    for step in steps[1:]:
        near_low = pair_sum(*near_pair)
        near_low, feed_low = together(near_low, feed_low)
        near_pair = (near_low, swap(near_low, "seq", step))
    kept, passed = halves(feed_low, steps[0])
    feed_pair = (kept, swap(passed, "seq", steps[0]))
    *pieces, last_diag = attend_back(
        joined, memory, att_grad.reshape(batch, SEG, D), attended, probs[1], PAIRS, pieces
    )
    pieces, feed_pair, near_pair = together(pieces, feed_pair, near_pair)
    for step in steps[1:]:
        kept, passed = halves(pair_sum(*feed_pair), step)
        feed_pair = (kept, swap(passed, "seq", step))
    partial, message, normed, normed_before, norm_small = finish(
        layer_input, before, pieces, grad_after.reshape(batch, SEG, D), own, sent, arrived, vec,
        attn_w,
    )
    partial, message, norm_small, feed_pair = together(partial, message, norm_small, feed_pair)
    feed_low = pair_sum(*feed_pair)
    last = [shift(message[0], -1)]
    attn_half, attn_far = project_grad(
        place, devices, parts, normed, normed_before, pieces, norm_small, gate_small, feed_small,
        [first_diag, last_diag],
    )
    attn_half, attn_far, message, last, feed_low = together(
        attn_half, attn_far, message, last, feed_low
    )
    attn_arrived = swap(attn_far, "fsdp", 1)
    last += [shift(message[sequence], -1) for sequence in range(1, batch)]
    feed_pair = (feed_low, swap(feed_low, "seq", steps[-1]))
    attn_sums = core_sums(attn_half, attn_arrived)
    attn_total = [attn_sums[0]] + to_chips(attn_sums, chips)
    near_grads = unpack(near_pair, ((1, D), (1, 2 * D), (1, D)))
    near_grads, attn_total, last, feed_pair = together(near_grads, attn_total, last, feed_pair)
    attn_low = chip_sum(attn_total)
    for step in reversed(steps[:-1]):
        feed_low = joined_halves(*feed_pair, 2 * step)
        feed_pair = (feed_low, swap(feed_low, "seq", step))
    for step in steps[:-1]:
        attn_low = pair_sum(attn_low, swap(attn_low, "seq", step))
    attn_pair = (attn_low, swap(attn_low, "seq", steps[-1]))
    input_grad = partial + jnp.stack(last).astype(F32)
    feed_pair = together(feed_pair, input_grad, attn_low)[0]
    feed_grads = unpack(
        (joined_halves(*feed_pair, steps[0]),), ((1, ff), (ratio, D), (1, D))
    )
    feed_grads, attn_pair = together(feed_grads, attn_pair)
    project_out, *smalls = unpack(attn_pair, ((1, 3 * D),), parts + [position_bias.shape[0]])
    return (
        output,
        input_grad,
        smalls[0],
        smalls[1],
        project_out,
        feed_grads[2],
        smalls[7],
        smalls[2],
        smalls[3],
        feed_grads[0],
        smalls[6],
        feed_grads[1],
        smalls[4],
        *near_grads,
        smalls[5],
    )


def solution(mesh):
    in_specs = (
        P("fsdp", "seq", None),
        P("fsdp", "seq", None),
        P("fsdp", "seq", None),
        P("fsdp"),
        P("fsdp"),
        P("fsdp", None),
        P("fsdp", None),
        P("fsdp"),
        P("fsdp"),
        P("fsdp"),
        P("fsdp", None),
        P("fsdp"),
        P("fsdp", None),
        P("fsdp"),
        P("fsdp", None),
        P("fsdp", None),
        P("fsdp", None),
        P("fsdp"),
    )
    out_specs = (
        P("fsdp", "seq", None),
        P("fsdp", "seq", None),
        P("fsdp"),
        P("fsdp"),
        P("fsdp", None),
        P("fsdp", None),
        P("fsdp"),
        P("fsdp"),
        P("fsdp"),
        P("fsdp", None),
        P("fsdp"),
        P("fsdp", None),
        P("fsdp"),
        P("fsdp", None),
        P("fsdp", None),
        P("fsdp", None),
        P("fsdp"),
    )
    return jax.shard_map(
        on_device, mesh=mesh, in_specs=in_specs, out_specs=out_specs, check_vma=False
    )
```

```python
import functools
import math

import jax
import jax.numpy as jnp
import numpy as np
from jax import lax
from jax.experimental import pallas as pl
from jax.experimental.pallas import tpu as pltpu
from jax.sharding import PartitionSpec as P

D = 512
H = 8
HD = 64
K = 4
SEG = 512
NB = 32

EPS = 1e-05
HIGH = lax.Precision.HIGHEST
MASKED = -1e30
F32 = jnp.float32
BF16 = jnp.bfloat16
ROWS = 256
SPAN = 2 * SEG + 128
VMEM = 56 << 20


def nn(left, right):
    return lax.dot_general(left, right, (((1,), (0,)), ((), ())), preferred_element_type=F32)


def nt(left, right):
    return lax.dot_general(left, right, (((1,), (1,)), ((), ())), preferred_element_type=F32)


def tn(left, right):
    return lax.dot_general(left, right, (((0,), (0,)), ((), ())), preferred_element_type=F32)


def shape(dims, dtype):
    return jax.ShapeDtypeStruct(tuple(dims), dtype)


def whole(dims):
    zeros = (0,) * len(dims)
    return pl.BlockSpec(tuple(dims), lambda *_: zeros, pipeline_mode=pl.Buffered(1))


def scalars():
    return pl.BlockSpec(memory_space=pltpu.SMEM)


def params(grid_rank):
    return pltpu.CompilerParams(
        dimension_semantics=("arbitrary",) * grid_rank, vmem_limit_bytes=VMEM
    )


def cost(flops, moved, exps=0):
    return pl.CostEstimate(
        flops=int(flops / 30), bytes_accessed=int(moved / 30), transcendentals=int(exps / 30)
    )


def thresholds():
    half_count = NB // 2
    spread_ratio = 2.0 * SEG / half_count
    exact_part = list(range(1, half_count))
    log_part = [
        int(half_count * spread_ratio ** ((bucket_index - half_count) / half_count))
        for bucket_index in range(half_count, NB)
    ]
    return np.array(exact_part + log_part)


def bucket_of(distance):
    return (distance[:, None] >= thresholds()[None, :]).sum(axis=1)


def forward_selector():
    distance = np.arange(SPAN) - 128
    bucket = bucket_of(np.maximum(distance, 0))
    return (np.arange(NB)[:, None] == bucket[None, :]).astype(np.float32)


def backward_selector():
    chosen = forward_selector().T.copy()
    chosen[:128] = 0.0
    return chosen


def norm(values):
    average = jnp.mean(values, axis=-1, keepdims=True)
    centred = values - average
    variance = jnp.mean(centred * centred, axis=-1, keepdims=True)
    rstd_value = lax.rsqrt(variance + EPS)
    return centred * rstd_value, rstd_value


def norm_back(grad_result, hat_value, rstd_value, gain):
    scaled = grad_result * gain
    return rstd_value * (
        scaled
        - jnp.mean(scaled, axis=-1, keepdims=True)
        - hat_value * jnp.mean(scaled * hat_value, axis=-1, keepdims=True)
    )


def rows_sum(values):
    return jnp.sum(values, axis=0, keepdims=True)


def pair_mask(head, values):
    lane = lax.broadcasted_iota(jnp.int32, values.shape, 1)
    keep = lane < HD if head == 0 else lane >= HD
    return jnp.where(keep, values, jnp.zeros_like(values))


def pack_first_kernel(*refs):
    weight_ref, *vector_refs, out_ref = refs
    rows = weight_ref.shape[0]
    out_ref[:rows, :] = weight_ref[...]
    out_ref[rows:, :] = jnp.zeros((16, out_ref.shape[1]), BF16)
    for index, ref in enumerate(vector_refs):
        line = ref[...].astype(F32).reshape(1, -1).astype(BF16)
        out_ref[rows + index : rows + index + 1, : ref.shape[0]] = line


def pack_first(weight, vectors):
    rows, columns = weight.shape
    return pl.pallas_call(
        pack_first_kernel,
        out_shape=shape((rows + 16, columns), BF16),
        cost_estimate=cost(0, 4 * rows * columns),
        name="pack_first",
    )(weight, *vectors)


def pack_kernel(rows, *refs):
    out_ref = refs[-1]
    start = 0
    for ref in refs[:-1]:
        for chunk in range(ref.shape[0] // rows):
            out_ref[:, start : start + ref.shape[1]] = ref[chunk * rows : (chunk + 1) * rows, :]
            start += ref.shape[1]


def pack(rows, weights):
    columns = sum(w.size for w in weights) // rows
    return pl.pallas_call(
        functools.partial(pack_kernel, rows),
        out_shape=shape((rows, columns), BF16),
        cost_estimate=cost(0, 4 * rows * columns),
        name="pack",
    )(*weights)


def unpack_kernel(layout, terms, bit, place_ref, *refs):
    total = [ref[...].astype(F32) for ref in refs[:terms]]
    if bit:
        high = jnp.bitwise_and(place_ref[1], bit) > 0
        mine, other = total
        total = jnp.concatenate(
            [jnp.where(high, other, mine), jnp.where(high, mine, other)], axis=1
        )
    else:
        total = functools.reduce(jnp.add, total)
    refs = refs[terms:]
    rows = refs[0].shape[0]
    start = 0
    for ref, (chunks, width) in zip(refs, layout):
        for chunk in range(chunks):
            ref[chunk * rows : (chunk + 1) * rows, :] = total[:rows, start : start + width]
            start += width
    for index, ref in enumerate(refs[len(layout) :]):
        ref[...] = total[rows + index : rows + index + 1, : ref.shape[0]].reshape(-1)


def unpack(place, pair, layout, widths=(), bit=0):
    rows = pair[0].shape[0] - (16 if widths else 0)
    outs = [shape((rows * chunks, width), F32) for chunks, width in layout]
    outs += [shape((width,), F32) for width in widths]
    return pl.pallas_call(
        functools.partial(unpack_kernel, layout, len(pair), bit),
        in_specs=[scalars()] + [pl.BlockSpec(memory_space=pltpu.VMEM)] * len(pair),
        out_shape=outs,
        compiler_params=pltpu.CompilerParams(vmem_limit_bytes=VMEM),
        cost_estimate=cost(0, 8 * pair[0].size),
        name="unpack",
    )(place, *pair)


def device_of(place_ref, chip_step, core_step):
    index = place_ref[0]
    chip = lax.shift_right_logical(index, 1)
    core = jnp.bitwise_and(index, 1)
    return jnp.bitwise_xor(chip, chip_step) * 2 + jnp.bitwise_xor(core, core_step)


def assemble(place_ref, layout, piece_refs, out_refs):
    steps = len(piece_refs) // 2
    for core_step in range(2):
        for step in range(steps):
            ref = piece_refs[core_step * steps + step]
            owner = device_of(place_ref, step, core_step)
            rows = D // (2 * steps)
            start = 0
            for out_ref, (chunks, width) in zip(out_refs, layout):
                for chunk in range(chunks):
                    target = pl.multiple_of((owner * chunks + chunk) * rows, rows)
                    out_ref[pl.ds(target, rows), :] = ref[:rows, start : start + width]
                    start += width


def first_kernel(parts, count, place_ref, x_ref, select_ref, *refs):
    piece_refs = refs[:count]
    w_ref, vec_ref, line_ref, joined_ref, small_ref = refs[count:]

    @pl.when(pl.program_id(0) == 0)
    def _():
        assemble(place_ref, ((1, 3 * D),), piece_refs, [w_ref])
        steps = count // 2
        rows = D // count
        for core_step in range(2):
            for step in range(steps):
                owner = device_of(place_ref, step, core_step)
                small_ref[pl.ds(pl.multiple_of(owner * 16, 16), 16), :] = piece_refs[
                    core_step * steps + step
                ][rows:, : small_ref.shape[1]].astype(F32)
        vec_ref[...] = jnp.zeros_like(vec_ref)
        for row, width in enumerate(parts):
            pieces = [small_ref[16 * d + row : 16 * d + row + 1, :width] for d in range(count)]
            vec_ref[row : row + 1, : width * count] = jnp.concatenate(pieces, axis=1)
        row = len(parts)
        table = jnp.concatenate(
            [small_ref[16 * d + row : 16 * d + row + 1, : NB * H // count] for d in range(count)],
            axis=0,
        )
        by_distance = None
        for place in range(NB // count):
            part = lax.dot_general(
                table[:, place * H : (place + 1) * H],
                select_ref[place],
                (((0,), (0,)), ((), ())),
                precision=HIGH,
                preferred_element_type=F32,
            )
            by_distance = part if by_distance is None else by_distance + part
        lane = lax.broadcasted_iota(jnp.int32, by_distance.shape, 1)
        line_ref[...] = jnp.where(lane < 128, MASKED, by_distance)

    hat_value, _ = norm(x_ref[0].astype(F32))
    normed = (hat_value * vec_ref[0:1, :D] + vec_ref[1:2, :D]).astype(BF16)
    joined_ref[0] = nn(normed, w_ref[...]).astype(BF16)


def remember_kernel(x_ref, vec_ref, w_ref, out_ref):
    hat_value, _ = norm(x_ref[0].astype(F32))
    normed = (hat_value * vec_ref[0:1, :D] + vec_ref[1:2, :D]).astype(BF16)
    out_ref[0] = nn(normed, w_ref[:, D:]).astype(BF16)


def remember(before, vec, weight):
    batch = before.shape[0]

    def block(width):
        return pl.BlockSpec((1, SEG, width), lambda b: (b, 0, 0))

    return pl.pallas_call(
        remember_kernel,
        grid=(batch,),
        in_specs=[block(D), whole(vec.shape), whole(weight.shape)],
        out_specs=block(2 * D),
        out_shape=shape((batch, SEG, 2 * D), BF16),
        compiler_params=params(1),
        cost_estimate=cost(4 * batch * SEG * D * D, 6 * batch * SEG * D),
        name="remember",
    )(before, vec, weight)


def first(place, x, pieces, parts, ff):
    batch = x.shape[0]
    count = len(pieces)
    small_width = -(-max(parts) // 128) * 128
    select = forward_selector().reshape(count, NB // count, SPAN).transpose(1, 0, 2)

    def block(width):
        return pl.BlockSpec((1, SEG, width), lambda b: (b, 0, 0))

    return pl.pallas_call(
        functools.partial(first_kernel, parts, count),
        grid=(batch,),
        in_specs=[scalars(), block(D), whole(select.shape)]
        + [whole(piece.shape) for piece in pieces],
        out_specs=[whole((D, 3 * D)), whole((8, ff)), whole((H, SPAN)), block(3 * D)],
        out_shape=[
            shape((D, 3 * D), BF16),
            shape((8, ff), F32),
            shape((H, SPAN), F32),
            shape((batch, SEG, 3 * D), BF16),
        ],
        scratch_shapes=[pltpu.VMEM((16 * count, small_width), F32)],
        compiler_params=params(1),
        cost_estimate=cost(6 * batch * SEG * D * D, 8 * batch * SEG * D),
        name="first",
    )(place, x, jnp.asarray(select), *pieces)


def tiles(place_ref, line_ref, first, own_ref, mem_ref):
    hidden = jnp.where(place_ref[1] > 0, 0.0, MASKED)
    for head in range(2):
        index = 2 * (first + pl.program_id(0)) + head
        line = jnp.broadcast_to(line_ref[pl.ds(index, 1), :], (8, SPAN))
        line = pltpu.roll(line, 0, 1, stride=1, stride_axis=0)
        for group in range(16):
            moved = pltpu.roll(line, 8 * group, 1) if group else line
            for tile in range(2 * SEG // 128):
                start = 2 * SEG - 128 * tile
                row = 128 * tile + 8 * group
                piece = moved[:, start : start + 128]
                own_ref[head, row : row + 8, :] = piece
                mem_ref[head, row : row + 8, :] = piece + hidden


def attend_kernel(first, place_ref, q_ref, k_ref, v_ref, km_ref, vm_ref, line_ref, *refs):
    out_ref, prob_ref, own_ref, mem_ref = refs[-4:]

    @pl.when(pl.program_id(1) == 0)
    def _():
        tiles(place_ref, line_ref, first, own_ref, mem_ref)

    keys = jnp.concatenate([km_ref[0], k_ref[0]], axis=0)
    values = jnp.concatenate([vm_ref[0], v_ref[0]], axis=0)
    for half in range(SEG // ROWS):
        width = SEG + (half + 1) * ROWS
        span = slice(half * ROWS, (half + 1) * ROWS)
        query = q_ref[0, span, :] * BF16(HD**-0.5)
        total = None
        for head in range(2):
            scores = nt(keys[:width], pair_mask(head, query))
            columns = []
            for part in range(ROWS // 128):
                block = half * (ROWS // 128) + part
                bias = jnp.concatenate(
                    [
                        mem_ref[head, (3 - block) * 128 : (7 - block) * 128, :],
                        own_ref[head, (7 - block) * 128 :, :],
                    ],
                    axis=0,
                )
                used = bias.shape[0]
                piece = scores[:used, part * 128 : (part + 1) * 128] + bias
                top = jnp.max(piece, axis=0, keepdims=True)
                weight = jnp.exp(piece - top)
                weight = (weight * (1.0 / jnp.sum(weight, axis=0, keepdims=True))).astype(BF16)
                if used < width:
                    weight = jnp.concatenate(
                        [weight, jnp.zeros((width - used, 128), BF16)], axis=0
                    )
                columns.append(weight)
            probs = jnp.concatenate(columns, axis=1)
            prob_ref[0, head, :width, span] = probs
            product = tn(probs, pair_mask(head, values)[:width])
            total = product if total is None else total + product
        out_ref[0, span, :] = total.astype(BF16)


PAIRS = H // 4


def attend(place, joined, memory, line, first, so_far):
    batch = joined.shape[0]

    def lanes(offset):
        return pl.BlockSpec((1, SEG, 128), lambda h, b: (b, 0, offset + first + h))

    work = batch * H * SEG * SEG
    extra = [] if so_far is None else [so_far]
    return pl.pallas_call(
        functools.partial(attend_kernel, first),
        grid=(PAIRS, batch),
        in_specs=[scalars()]
        + [lanes(0), lanes(2 * PAIRS), lanes(4 * PAIRS), lanes(0), lanes(2 * PAIRS)]
        + [whole(line.shape)]
        + [pl.BlockSpec(memory_space=pl.ANY)] * len(extra),
        out_specs=[
            lanes(0),
            pl.BlockSpec((1, 2, 2 * SEG, SEG), lambda h, b: (b, h, 0, 0)),
        ],
        out_shape=[shape((batch, SEG, D), BF16), shape((batch, H // 2, 2 * SEG, SEG), BF16)],
        scratch_shapes=[pltpu.VMEM((2, 2 * SEG, 128), F32)] * 2,
        input_output_aliases={7: 0} if extra else {},
        compiler_params=params(2),
        cost_estimate=cost(16 * HD * work, 3 * work, work),
        name="attend",
    )(place, joined, joined, joined, memory, memory, line, *extra)


def attend_back_kernel(
    q_ref, k_ref, v_ref, km_ref, vm_ref, grad_ref, out_ref, prob_ref, *refs
):
    dq_ref, dk_ref, dv_ref, dkm_ref, dvm_ref, diag_ref, grid_ref = refs[-7:]
    keys = jnp.concatenate([km_ref[0], k_ref[0]], axis=0)
    values = jnp.concatenate([vm_ref[0], v_ref[0]], axis=0)
    step = pl.program_id(1)

    @pl.when(step == 0)
    def _():
        grid_ref[...] = jnp.zeros_like(grid_ref)

    key_parts = []
    value_parts = []
    for half in range(SEG // ROWS):
        width = SEG + (half + 1) * ROWS
        span = slice(half * ROWS, (half + 1) * ROWS)
        grad = grad_ref[0, span, :]
        query = q_ref[0, span, :] * BF16(HD**-0.5)
        product = (grad.astype(F32) * out_ref[0, span, :].astype(F32)).T
        query_total = key_total = value_total = None
        for head in range(2):
            grad_head = pair_mask(head, grad)
            delta = jnp.sum(product[head * HD : (head + 1) * HD], axis=0, keepdims=True)
            probs = prob_ref[0, head, :width, span]
            scored = probs.astype(F32) * (nt(values[:width], grad_head) - delta)
            for part in range(ROWS // 128):
                block = half * (ROWS // 128) + part
                used = SEG + (block + 1) * 128
                grid_ref[head, (3 - block) * 128 :, :] += scored[
                    :used, part * 128 : (part + 1) * 128
                ]
            scored = scored.astype(BF16)
            for_key = nn(scored, pair_mask(head, query))
            for_value = nn(probs, grad_head)
            for_query = tn(scored, pair_mask(head, keys)[:width])
            key_total = for_key if key_total is None else key_total + for_key
            value_total = for_value if value_total is None else value_total + for_value
            query_total = for_query if query_total is None else query_total + for_query
        dq_ref[0, span, :] = (query_total * HD**-0.5).astype(BF16)
        key_parts.append(key_total)
        value_parts.append(value_total)
    for pieces, mem_ref, own_ref in (
        (key_parts, dkm_ref, dk_ref),
        (value_parts, dvm_ref, dv_ref),
    ):
        both = pieces[0] + pieces[1][: SEG + ROWS]
        mem_ref[0] = both[:SEG].astype(BF16)
        own_ref[0, :ROWS] = both[SEG:].astype(BF16)
        own_ref[0, ROWS:] = pieces[1][SEG + ROWS :].astype(BF16)

    @pl.when(step == pl.num_programs(1) - 1)
    def _():
        for head in range(2):
            total = None
            for group in range(16):
                pieces = [
                    grid_ref[head, 128 * tile + 8 * group : 128 * tile + 8 * group + 8, :]
                    for tile in reversed(range(2 * SEG // 128))
                ]
                line = jnp.concatenate([jnp.zeros((8, 128), F32)] + pieces, axis=1)
                if group:
                    line = pltpu.roll(line, SPAN - 8 * group, 1)
                total = line if total is None else total + line
            lines = [total[:1]] + [
                pltpu.roll(total[row : row + 1], SPAN - row, 1) for row in range(1, 8)
            ]
            diag_ref[0, head : head + 1, :] = functools.reduce(jnp.add, lines)


def attend_back(joined, memory, grad, attended, probs, first, so_far):
    batch = joined.shape[0]

    def lanes(offset):
        return pl.BlockSpec((1, SEG, 128), lambda h, b: (b, 0, offset + first + h))

    half = shape((batch, SEG, D), BF16)
    work = batch * H * SEG * SEG
    return pl.pallas_call(
        attend_back_kernel,
        grid=(PAIRS, batch),
        in_specs=[lanes(0), lanes(2 * PAIRS), lanes(4 * PAIRS), lanes(0), lanes(2 * PAIRS)]
        + [lanes(0)] * 2
        + [pl.BlockSpec((1, 2, 2 * SEG, SEG), lambda h, b: (b, h, 0, 0))]
        + [pl.BlockSpec(memory_space=pl.ANY)] * len(so_far),
        out_specs=[lanes(0)] * 5 + [pl.BlockSpec((1, 2, SPAN), lambda h, b: (h, 0, 0))],
        out_shape=[half] * 5 + [shape((PAIRS, 2, SPAN), F32)],
        scratch_shapes=[pltpu.VMEM((2, 2 * SEG, 128), F32)],
        input_output_aliases={8 + i: i for i in range(len(so_far))},
        compiler_params=params(2),
        cost_estimate=cost(32 * HD * work, 3 * work),
        name="attend_back",
    )(joined, joined, joined, memory, memory, grad, attended, probs, *so_far)


def feed_layout(ff):
    return ((1, D), (1, ff), (ff // D, D))


def feed_scratch(ff):
    return [pltpu.VMEM((D, D), BF16), pltpu.VMEM((D, ff), BF16), pltpu.VMEM((ff, D), BF16)]


def feed_kernel(count, place_ref, x_ref, att_ref, vec_ref, *refs):
    piece_refs = refs[:count]
    (
        after_attn_ref, active_ref, slope_ref, after_ffn_ref, merge_ref, expand_ref, reduce_ref,
    ) = refs[count:]

    @pl.when(pl.program_id(0) == 0)
    def _():
        assemble(place_ref, feed_layout(expand_ref.shape[1]), piece_refs, refs[-3:])

    after_attn = x_ref[...].astype(F32) + nn(att_ref[...], merge_ref[...])
    after_attn_ref[...] = after_attn
    hat_value, _ = norm(after_attn)
    normed = (hat_value * vec_ref[2:3, :D] + vec_ref[3:4, :D]).astype(BF16)
    pre = nn(normed, expand_ref[...]) + vec_ref[6:7, :]
    cdf = 0.5 * (1.0 + lax.erf(pre * (1.0 / math.sqrt(2.0))))
    slope = cdf + pre * jnp.exp(-0.5 * pre * pre) * (1.0 / math.sqrt(2.0 * math.pi))
    slope_ref[...] = slope.astype(BF16)
    active = (pre * cdf).astype(BF16)
    active_ref[...] = active
    after_ffn = after_attn + nn(active, reduce_ref[...]) + vec_ref[4:5, :D]
    after_ffn_ref[...] = after_ffn


def feed(place, x, attended, vec, pieces):
    count = x.shape[0]
    ff = vec.shape[1]

    def rows(width):
        return pl.BlockSpec((ROWS, width), lambda i: (i, 0))

    return pl.pallas_call(
        functools.partial(feed_kernel, len(pieces)),
        grid=(count // ROWS,),
        in_specs=[scalars(), rows(D), rows(D), whole(vec.shape)]
        + [whole(piece.shape) for piece in pieces],
        out_specs=[rows(D), rows(ff), rows(ff), rows(D)],
        out_shape=[
            shape((count, D), F32),
            shape((count, ff), BF16),
            shape((count, ff), BF16),
            shape((count, D), F32),
        ],
        scratch_shapes=feed_scratch(ff),
        compiler_params=params(1),
        cost_estimate=cost(4 * count * D * (ff + D), 12 * count * ff, 2 * count * ff),
        name="feed",
    )(place, x, attended, vec, *pieces)


def add_rows(ref, row, values):
    ref[row : row + 1, : values.shape[1]] += values


def scatter_rows(place_ref, total_ref, near_ref, far_ref, start, chunks):
    steps, rows = near_ref.shape[0], near_ref.shape[1]
    width = total_ref.shape[1]
    for core_step, ref in ((0, near_ref), (1, far_ref)):
        for step in range(steps):
            owner = device_of(place_ref, step, core_step)
            for chunk in range(chunks):
                source = pl.multiple_of((owner * chunks + chunk) * rows, rows)
                column = start + chunk * width
                ref[step, :, column : column + width] = total_ref[
                    pl.ds(source, rows), :
                ].astype(BF16)
    return start + chunks * width


def feed_back_kernel(
    count, place_ref, grad_ref, after_ref, active_ref, slope_ref, att_ref, vec_ref, *refs
):
    piece_refs = refs[:count]
    (
        after_grad_ref, att_grad_ref, small_ref, near_ref, far_ref,
        expand_total, reduce_total, merge_total, merge_ref, expand_ref, reduce_ref,
    ) = refs[count:]
    step = pl.program_id(0)

    @pl.when(step == 0)
    def _():
        assemble(place_ref, feed_layout(expand_ref.shape[1]), piece_refs, refs[-3:])
        expand_total[...] = jnp.zeros_like(expand_total)
        merge_total[...] = jnp.zeros_like(merge_total)
        reduce_total[...] = jnp.zeros_like(reduce_total)
        small_ref[...] = jnp.zeros_like(small_ref)

    grad = grad_ref[...]
    low = grad.astype(BF16)
    add_rows(small_ref, 2, rows_sum(low.astype(F32)))
    reduce_total[...] += tn(active_ref[...], low)
    pre_grad = (nt(low, reduce_ref[...]) * slope_ref[...].astype(F32)).astype(BF16)
    add_rows(small_ref, 3, rows_sum(pre_grad.astype(F32)))
    hat_value, rstd_value = norm(after_ref[...])
    gain = vec_ref[2:3, :D]
    normed = (hat_value * gain + vec_ref[3:4, :D]).astype(BF16)
    expand_total[...] += tn(normed, pre_grad)
    normed_grad = nt(pre_grad, expand_ref[...])
    add_rows(small_ref, 0, rows_sum(normed_grad * hat_value))
    add_rows(small_ref, 1, rows_sum(normed_grad))
    after_grad = grad + norm_back(normed_grad, hat_value, rstd_value, gain)
    after_grad_ref[...] = after_grad
    merge_grad = after_grad.astype(BF16)
    merge_total[...] += tn(att_ref[...], merge_grad)
    att_grad_ref[...] = nt(merge_grad, merge_ref[...]).astype(BF16)

    @pl.when(step == pl.num_programs(0) - 1)
    def _():
        start = scatter_rows(place_ref, expand_total, near_ref, far_ref, 0, 1)
        ratio = reduce_total.shape[0] // D
        start = scatter_rows(place_ref, reduce_total, near_ref, far_ref, start, ratio)
        scatter_rows(place_ref, merge_total, near_ref, far_ref, start, 1)


def feed_back(place, grad, after_attn, active, slope, attended, vec, pieces):
    count = grad.shape[0]
    ff = vec.shape[1]
    devices = len(pieces)

    def rows(width):
        return pl.BlockSpec((ROWS, width), lambda i: (i, 0))

    packed = (devices // 2, D // devices, 2 * ff + D)
    return pl.pallas_call(
        functools.partial(feed_back_kernel, devices),
        grid=(count // ROWS,),
        in_specs=[scalars(), rows(D), rows(D), rows(ff), rows(ff), rows(D), whole(vec.shape)]
        + [whole(piece.shape) for piece in pieces],
        out_specs=[rows(D), rows(D), whole((8, ff)), whole(packed), whole(packed)],
        out_shape=[
            shape((count, D), F32),
            shape((count, D), BF16),
            shape((8, ff), F32),
            shape(packed, BF16),
            shape(packed, BF16),
        ],
        scratch_shapes=[
            pltpu.VMEM((D, ff), F32),
            pltpu.VMEM((ff, D), F32),
            pltpu.VMEM((D, D), F32),
        ]
        + feed_scratch(ff),
        compiler_params=params(1),
        cost_estimate=cost(8 * count * D * (ff + D // 2), 12 * count * ff),
        name="feed_back",
    )(place, grad, after_attn, active, slope, attended, vec, *pieces)


def chosen_rows(ids, slot, rows):
    place = lax.broadcasted_iota(jnp.int32, (ids.shape[0], SEG), 1)
    return nn(jnp.where(ids[:, slot : slot + 1] == place, 1.0, 0.0).astype(BF16), rows)


def ids_down(ids):
    return jnp.concatenate([ids] * 2, axis=0).T


def take_kernel(distance, started, place_ref, ids_ref, rows_ref, *refs):
    out_ref = refs[-1]
    ids = ids_down(ids_ref[0] - (place_ref[1] - distance) * SEG)
    rows = rows_ref[0]
    for slot in range(K):
        taken = chosen_rows(ids, slot, rows).astype(BF16)
        out_ref[0, slot] = refs[0][0, slot] + taken if started else taken


def take(place, ids, rows, distance, so_far):
    batch = ids.shape[0]
    block = pl.BlockSpec((1, K, SEG, D), lambda b: (b, 0, 0, 0))
    return pl.pallas_call(
        functools.partial(take_kernel, distance, len(so_far)),
        grid=(batch,),
        in_specs=[
            scalars(),
            pl.BlockSpec((1, K, SEG), lambda b: (b, 0, 0)),
            pl.BlockSpec((1, SEG, D), lambda b: (b, 0, 0)),
        ]
        + [block] * len(so_far),
        out_specs=block,
        out_shape=shape((batch, K, SEG, D), BF16),
        input_output_aliases={3: 0} if so_far else {},
        compiler_params=params(1),
        cost_estimate=cost(2 * batch * K * SEG * SEG * D, 4 * batch * K * SEG * D),
        name="take",
    )(place, ids, rows, *so_far)


def give_kernel(distances, started, place_ref, ids_ref, grad_ref, *refs):
    out_refs = refs[started:]
    place = lax.broadcasted_iota(jnp.int32, (SEG, SEG), 0)
    for index, distance in enumerate(distances):
        ids = ids_ref[0] - (place_ref[1] - distance) * SEG
        total = None
        for slot in range(K):
            chosen = jnp.where(ids[slot : slot + 1, :] == place, 1.0, 0.0).astype(BF16)
            part = nn(chosen, grad_ref[0, slot])
            total = part if total is None else total + part
        if started and index == 0:
            total = total + refs[0][0].astype(F32)
        out_refs[index][0] = total.astype(out_refs[index].dtype)


def give(place, ids, grads, arrived, distances):
    batch = ids.shape[0]
    block = pl.BlockSpec((1, SEG, D), lambda b: (b, 0, 0))
    started = arrived is not None
    work = len(distances) * batch * K * SEG * D
    return pl.pallas_call(
        functools.partial(give_kernel, distances, started),
        grid=(batch,),
        in_specs=[
            scalars(),
            pl.BlockSpec((1, K, SEG), lambda b: (b, 0, 0)),
            pl.BlockSpec((1, K, SEG, D), lambda b: (b, 0, 0, 0)),
        ]
        + [block] * started,
        out_specs=[block] * len(distances),
        out_shape=[shape((batch, SEG, D), BF16 if d else F32) for d in distances],
        compiler_params=params(1),
        cost_estimate=cost(2 * work * SEG, 2 * work),
        name="give",
    )(place, ids, grads, *([arrived] if started else []))


def near_kernel(
    hops, count, place_ref, ids_ref, rows_ref, after_ref, grad_ref, vec_ref, *refs
):
    state_refs = refs[:hops]
    piece_refs = refs[hops : hops + count]
    (
        out_ref, row_grad_ref, after_grad_ref, small_ref, near_ref, far_ref,
        keys_total, merge_total, query_total, nq_ref, keys_ref, merge_ref,
    ) = refs[hops + count :]
    first = (pl.program_id(0) == 0) & (pl.program_id(1) == 0)
    last = (pl.program_id(0) == pl.num_programs(0) - 1) & (
        pl.program_id(1) == pl.num_programs(1) - 1
    )

    @pl.when(first)
    def _():
        keys_total[...] = jnp.zeros_like(keys_total)
        merge_total[...] = jnp.zeros_like(merge_total)
        query_total[...] = jnp.zeros_like(query_total)
        assemble(place_ref, ((1, D), (1, 2 * D), (1, D)), piece_refs, refs[-3:])
        small_ref[...] = jnp.zeros_like(small_ref)

    scale = HD**-0.5
    place = lax.broadcasted_iota(jnp.int32, (K * D, 128), 0)
    lane = lax.broadcasted_iota(jnp.int32, (K * D, 128), 1)
    group = lax.shift_right_logical(place, 9) * H + jnp.bitwise_and(
        lax.shift_right_logical(place, 6), H - 1
    )
    gather = jnp.where(jnp.bitwise_and(lane, K * H - 1) == group, 1.0, 0.0).astype(BF16)
    lane = lax.broadcasted_iota(jnp.int32, (128, K * D), 0)
    place = lax.broadcasted_iota(jnp.int32, (128, K * D), 1)
    group = lax.shift_right_logical(place, 9) * H + jnp.bitwise_and(
        lax.shift_right_logical(place, 6), H - 1
    )
    spread = jnp.where(
        (jnp.bitwise_and(lane, K * H - 1) == group) & (lane < 2 * K * H), 1.0, 0.0
    ).astype(BF16)

    def over_slots(combine, values):
        values = combine(values, pltpu.roll(values, 2 * H, 1))
        return combine(values, pltpu.roll(values, H, 1))

    def to_rows(values):
        high = values.astype(BF16)
        low = (values - high.astype(F32)).astype(BF16)
        lane = lax.broadcasted_iota(jnp.int32, values.shape, 1)
        return nn(jnp.where(lane < K * H, high, low), spread)

    def slot_of(values, slot):
        return values[:, slot * D : (slot + 1) * D]

    after_ffn = after_ref[0]
    hidden_low = after_ffn.astype(BF16)
    query = nn(hidden_low, nq_ref[...]).astype(BF16)
    query_float = query.astype(F32)
    ids = ids_down(ids_ref[0])
    states = jnp.concatenate([ref[0] for ref in state_refs], axis=0) if hops else None
    taken = []
    for slot in range(K):
        total = rows_ref[0, slot]
        if hops:
            chosen = []
            for hop in range(hops):
                column = ids[:, slot : slot + 1] - (place_ref[1] - hop - 2) * SEG
                here = lax.broadcasted_iota(jnp.int32, (ids.shape[0], SEG), 1)
                chosen.append(jnp.where(column == here, 1.0, 0.0).astype(BF16))
            moved = nn(jnp.concatenate(chosen, axis=1), states)
            total = total + moved.astype(BF16)
        taken.append(total)
    pairs = [nn(rows, keys_ref[...]).astype(BF16) for rows in taken]
    near_key = [pair[:, :D] for pair in pairs]
    near_value = [pair[:, D:] for pair in pairs]
    products = jnp.concatenate([query * key for key in near_key], axis=1)
    scores = nn(products, gather) * scale
    weights = jnp.exp(scores - over_slots(jnp.maximum, scores))
    probs = weights / over_slots(jnp.add, weights)
    prob_rows = to_rows(probs)
    mixed = functools.reduce(
        jnp.add, [slot_of(prob_rows, i) * v.astype(F32) for i, v in enumerate(near_value)]
    ).astype(BF16)
    near_out = nn(mixed, merge_ref[...])
    gate_vector = vec_ref[5:6, :D]
    gate = jax.nn.sigmoid(jnp.sum(after_ffn * gate_vector, axis=-1, keepdims=True))
    out_ref[0] = (gate * after_ffn + (1.0 - gate) * near_out).astype(BF16)
    grad = grad_ref[0].astype(F32)
    gate_grad = (
        jnp.sum(grad * (after_ffn - near_out), axis=-1, keepdims=True) * gate * (1.0 - gate)
    )
    add_rows(small_ref, 0, rows_sum(gate_grad * after_ffn))
    near_grad = ((1.0 - gate) * grad).astype(BF16)
    merge_total[...] += tn(mixed, near_grad)
    mixed_low = nt(near_grad, merge_ref[...]).astype(BF16)
    mixed_grad = mixed_low.astype(F32)
    products = jnp.concatenate([mixed_low * value for value in near_value], axis=1)
    prob_grads = nn(products, gather)
    inner = over_slots(jnp.add, probs * prob_grads)
    score_rows = to_rows(probs * (prob_grads - inner) * scale)
    query_grad = None
    for slot in range(K):
        score_grad = slot_of(score_rows, slot)
        part = score_grad * near_key[slot].astype(F32)
        query_grad = part if query_grad is None else query_grad + part
        pair_grad = jnp.concatenate(
            [
                (score_grad * query_float).astype(BF16),
                (slot_of(prob_rows, slot) * mixed_grad).astype(BF16),
            ],
            axis=1,
        )
        keys_total[...] += tn(taken[slot], pair_grad)
        row_grad_ref[0, slot] = nt(pair_grad, keys_ref[...]).astype(BF16)
    query_grad = query_grad.astype(BF16)
    query_total[...] += tn(hidden_low, query_grad)
    after_grad_ref[0] = gate * grad + gate_grad * gate_vector + nt(query_grad, nq_ref[...])

    @pl.when(last)
    def _():
        start = scatter_rows(place_ref, query_total, near_ref, far_ref, 0, 1)
        start = scatter_rows(place_ref, keys_total, near_ref, far_ref, start, 1)
        scatter_rows(place_ref, merge_total, near_ref, far_ref, start, 1)


def near(place, ids, rows, states, after_ffn, grad, vec, pieces):
    batch = rows.shape[0]
    devices = len(pieces)
    row_block = pl.BlockSpec((1, K, ROWS, D), lambda b, i: (b, 0, i, 0))
    block = pl.BlockSpec((1, ROWS, D), lambda b, i: (b, i, 0))
    packed = (devices // 2, D // devices, 4 * D)
    count = batch * SEG
    return pl.pallas_call(
        functools.partial(near_kernel, len(states), devices),
        grid=(batch, SEG // ROWS),
        in_specs=[scalars(), pl.BlockSpec((1, K, ROWS), lambda b, i: (b, 0, i))]
        + [row_block, block, block, whole(vec.shape)]
        + [pl.BlockSpec((1, SEG, D), lambda b, i: (b, 0, 0))] * len(states)
        + [whole(piece.shape) for piece in pieces],
        out_specs=[block, row_block, block, whole((8, D)), whole(packed), whole(packed)],
        out_shape=[
            shape((batch, SEG, D), BF16),
            shape((batch, K, SEG, D), BF16),
            shape((batch, SEG, D), F32),
            shape((8, D), F32),
            shape(packed, BF16),
            shape(packed, BF16),
        ],
        scratch_shapes=[
            pltpu.VMEM((D, 2 * D), F32),
            pltpu.VMEM((D, D), F32),
            pltpu.VMEM((D, D), F32),
            pltpu.VMEM((D, D), BF16),
            pltpu.VMEM((D, 2 * D), BF16),
            pltpu.VMEM((D, D), BF16),
        ],
        compiler_params=params(2),
        cost_estimate=cost(
            2 * count * D * D * (11 * K + 6), count * D * (4 * K + 12), count * K * D
        ),
        name="near",
    )(place, ids, rows, after_ffn, grad, vec, *states, *pieces)


def finish_kernel(
    x_ref, before_ref, dq_ref, dk_ref, dv_ref, dkm_ref, dvm_ref, grad_ref, own_ref, sent_ref,
    arrived_ref, vec_ref, w_ref,
    part_ref, normed_ref, normed_before_ref, small_ref, *send_refs,
):
    @pl.when(pl.program_id(0) == 0)
    def _():
        small_ref[...] = jnp.zeros_like(small_ref)

    gain = vec_ref[0:1, :D]
    shift_by = vec_ref[1:2, :D]
    hat_before, rstd_before = norm(before_ref[0].astype(F32))
    normed_before_ref[0] = (hat_before * gain + shift_by).astype(BF16)
    before_grad = nt(dkm_ref[0], w_ref[:, D : 2 * D]) + nt(dvm_ref[0], w_ref[:, 2 * D :])
    send = (
        sent_ref[0].astype(F32)
        + arrived_ref[0].astype(F32)
        + norm_back(before_grad, hat_before, rstd_before, gain)
    ).astype(BF16)
    for sequence, send_ref in enumerate(send_refs):

        @pl.when(pl.program_id(0) == sequence)
        def _():
            send_ref[...] = send

    hat_value, rstd_value = norm(x_ref[0].astype(F32))
    normed_ref[0] = (hat_value * gain + shift_by).astype(BF16)
    normed_grad = (
        nt(dq_ref[0], w_ref[:, :D])
        + nt(dk_ref[0], w_ref[:, D : 2 * D])
        + nt(dv_ref[0], w_ref[:, 2 * D :])
    )
    add_rows(small_ref, 0, rows_sum(normed_grad * hat_value) + rows_sum(before_grad * hat_before))
    add_rows(small_ref, 1, rows_sum(normed_grad) + rows_sum(before_grad))
    part_ref[0] = (
        grad_ref[0] + own_ref[0] + norm_back(normed_grad, hat_value, rstd_value, gain)
    )


def finish(x, before, pieces, grad, own, sent, arrived, vec, weight):
    batch = x.shape[0]
    block = pl.BlockSpec((1, SEG, D), lambda b: (b, 0, 0))
    low = shape((batch, SEG, D), BF16)
    return pl.pallas_call(
        finish_kernel,
        grid=(batch,),
        in_specs=[block] * 11 + [whole(w.shape) for w in (vec, weight)],
        out_specs=[block] * 3 + [whole((8, D))] + [whole((SEG, D))] * batch,
        out_shape=[shape((batch, SEG, D), F32), low, low, shape((8, D), F32)]
        + [shape((SEG, D), BF16)] * batch,
        compiler_params=params(1),
        cost_estimate=cost(10 * batch * SEG * D * D, 34 * batch * SEG * D),
        name="finish",
    )(x, before, *pieces, grad, own, sent, arrived, vec, weight)


def project_grad_kernel(
    parts, place_ref, normed_ref, normed_before_ref, dq_ref, dk_ref, dv_ref, dkm_ref, dvm_ref,
    norm_ref, gate_ref, feed_ref, select_ref, first_ref, last_ref,
    near_ref, far_ref, w_total, small_total,
):
    step = pl.program_id(0)

    @pl.when(step == 0)
    def _():
        w_total[...] = jnp.zeros_like(w_total)

    normed = normed_ref[0]
    normed_before = normed_before_ref[0]
    w_total[:, :D] += tn(normed, dq_ref[0])
    w_total[:, D : 2 * D] += tn(normed, dk_ref[0]) + tn(normed_before, dkm_ref[0])
    w_total[:, 2 * D :] += tn(normed, dv_ref[0]) + tn(normed_before, dvm_ref[0])

    @pl.when(step == pl.num_programs(0) - 1)
    def _():
        devices = small_total.shape[0] // 16
        rows = w_total.shape[0] // devices
        small_total[...] = jnp.zeros_like(small_total)
        lines = [
            norm_ref[0:1, :],
            norm_ref[1:2, :],
            feed_ref[0:1, :D],
            feed_ref[1:2, :D],
            feed_ref[2:3, :D],
            gate_ref[0:1, :],
            feed_ref[3:4, :],
        ]
        for index, (line, width) in enumerate(zip(lines, parts)):
            for d in range(devices):
                row = 16 * d + index
                small_total[row : row + 1, :width] = line[:, d * width : (d + 1) * width]
        table = lax.dot_general(
            jnp.concatenate([ref[i] for ref in (first_ref, last_ref) for i in range(PAIRS)], axis=0),
            select_ref[...],
            (((1,), (0,)), ((), ())),
            precision=HIGH,
            preferred_element_type=F32,
        )
        own_buckets = NB // devices
        bucket = lax.broadcasted_iota(jnp.int32, (devices, NB), 1)
        owner = lax.broadcasted_iota(jnp.int32, (devices, NB), 0)
        pieces = []
        for place in range(own_buckets):
            chosen = jnp.where(bucket == owner * own_buckets + place, 1.0, 0.0)
            pieces.append(
                lax.dot_general(
                    chosen,
                    table,
                    (((1,), (1,)), ((), ())),
                    precision=HIGH,
                    preferred_element_type=F32,
                )
            )
        buckets = jnp.concatenate(pieces, axis=1)
        for d in range(devices):
            row = 16 * d + len(parts)
            small_total[row : row + 1, : buckets.shape[1]] = buckets[d : d + 1, :]
        width = small_total.shape[1]
        for core_step, ref in ((0, near_ref), (1, far_ref)):
            for chip_step in range(ref.shape[0]):
                target = device_of(place_ref, chip_step, core_step)
                source = pl.multiple_of(target * rows, rows)
                ref[chip_step, :rows, :] = w_total[pl.ds(source, rows), :].astype(BF16)
                ref[chip_step, rows:, :] = jnp.zeros((16, ref.shape[2]), BF16)
                lines = small_total[pl.ds(pl.multiple_of(target * 16, 16), 16), :]
                ref[chip_step, rows:, :width] = lines.astype(BF16)


def project_grad(place, devices, parts, normed, normed_before, pieces, norm_small, gate, feed_small, diags):
    batch = normed.shape[0]
    block = pl.BlockSpec((1, SEG, D), lambda b: (b, 0, 0))
    packed = (devices // 2, D // devices + 16, 3 * D)
    select = jnp.asarray(backward_selector())
    small_width = -(-max(parts) // 128) * 128
    return pl.pallas_call(
        functools.partial(project_grad_kernel, parts),
        grid=(batch,),
        in_specs=[scalars()]
        + [block] * 7
        + [whole(w.shape) for w in (norm_small, gate, feed_small, select, *diags)],
        out_specs=[whole(packed)] * 2,
        out_shape=[shape(packed, BF16)] * 2,
        scratch_shapes=[
            pltpu.VMEM((D, 3 * D), F32),
            pltpu.VMEM((16 * devices, small_width), F32),
        ],
        compiler_params=params(1),
        cost_estimate=cost(10 * batch * SEG * D * D, 20 * batch * SEG * D),
        name="project_grad",
    )(
        place, normed, normed_before, *pieces, norm_small, gate, feed_small, select, *diags,
    )


def shift(block, distance):
    count = lax.axis_size("seq")
    return lax.ppermute(block, "seq", [(i, (i + distance) % count) for i in range(count)])


def swap(block, axis, bits):
    count = lax.axis_size(axis)
    return lax.ppermute(block, axis, [(i, i ^ bits) for i in range(count)])


def together(*values):
    return lax.optimization_barrier(values)


def chip_steps():
    steps = list(range(1, lax.axis_size("fsdp") // 2))
    cut = (2 * len(steps) + 2) // 3
    return steps[:cut], steps[cut:]


def from_chips(shard, steps):
    return [swap(shard, "fsdp", 2 * step) for step in steps]


def from_core(pieces):
    return [swap(piece, "fsdp", 1) for piece in pieces]


def core_sums(near_half, arrived):
    return [
        (near_half[step].astype(F32) + arrived[step].astype(F32)).astype(BF16)
        for step in range(near_half.shape[0])
    ]


def to_chips(pieces, steps):
    return [swap(pieces[step], "fsdp", 2 * step) for step in steps]


def chip_sum(pieces):
    return functools.reduce(jnp.add, [piece.astype(F32) for piece in pieces]).astype(BF16)


def segment_steps():
    return [1 << bit for bit in range(lax.axis_size("seq").bit_length() - 1)]


def halves(values, bit):
    half = values.shape[1] // 2
    high = jnp.bitwise_and(lax.axis_index("seq"), bit) > 0
    left, right = values[:, :half], values[:, half:]
    return jnp.where(high, right, left), jnp.where(high, left, right)


def joined_halves(mine, other, bit):
    high = jnp.bitwise_and(lax.axis_index("seq"), bit) > 0
    return jnp.concatenate([jnp.where(high, other, mine), jnp.where(high, mine, other)], axis=1)


def pair_sum(left, right):
    return (left.astype(F32) + right.astype(F32)).astype(BF16)


def on_device(
    layer_input,
    neighbour_ids,
    out_grad,
    attn_norm_gain,
    attn_norm_bias,
    attn_project,
    attn_merge,
    position_bias,
    ffn_norm_gain,
    ffn_norm_bias,
    ffn_expand,
    expand_bias,
    ffn_reduce,
    reduce_bias,
    near_query,
    near_keys,
    near_merge,
    gate_vector,
):
    batch = layer_input.shape[0]
    count = batch * SEG
    devices = lax.axis_size("fsdp")
    segments = lax.axis_size("seq")
    rows = attn_project.shape[0]
    ff = ffn_expand.shape[1]
    ratio = ff // D

    place = jnp.stack([lax.axis_index("fsdp"), lax.axis_index("seq")]).astype(jnp.int32)
    vectors = [
        attn_norm_gain, attn_norm_bias, ffn_norm_gain, ffn_norm_bias, reduce_bias, gate_vector,
        expand_bias, position_bias,
    ]
    parts = [v.shape[0] for v in vectors[:-1]]
    steps = segment_steps()
    near_steps, far_steps = chip_steps()
    chips = near_steps + far_steps

    attn_shard = pack_first(attn_project, vectors)
    attn_pieces = [attn_shard] + from_chips(attn_shard, chips)
    before = shift(layer_input, 1)
    ids = jnp.swapaxes(neighbour_ids, 1, 2)
    feed_shard = pack(rows, [attn_merge, ffn_expand, ffn_reduce])
    near_shard = pack(rows, [near_query, near_keys, near_merge])
    near_rows = take(place, ids, layer_input, 0, [])
    near_rows, feed_shard, near_shard, attn_pieces = together(
        near_rows, feed_shard, near_shard, attn_pieces
    )
    feed_pieces = [feed_shard] + from_chips(feed_shard, near_steps)
    attn_w, vec, line, joined = first(
        place, layer_input, attn_pieces + from_core(attn_pieces), parts, ff
    )
    joined, before = together(joined, before)
    states = [before]
    if segments > 2:
        states.append(shift(before, 1))
    memory = remember(before, vec, attn_w)
    attended = None
    probs = []
    for part in range(2):
        attended, part_probs = attend(place, joined, memory, line, part * PAIRS, attended)
        probs.append(part_probs)
        if part == 0:
            attended, memory, feed_pieces, near_rows = together(
                attended, memory, feed_pieces, near_rows
            )
            feed_far = from_core(feed_pieces)
            feed_rest = from_chips(feed_pieces[0], far_steps)
            near_rows = take(place, ids, before, 1, [near_rows])
            attended, near_rows, states = together(attended, near_rows, states)
            if len(states) < segments - 1:
                states.append(shift(states[-1], 1))
    attended, feed_far, feed_rest, near_shard = together(
        attended, feed_far, feed_rest, near_shard
    )
    feed_pieces += feed_rest + feed_far + from_core(feed_rest)
    near_pieces = [near_shard] + from_chips(near_shard, chips)
    flat_attended = attended.reshape(count, D)
    after_attn, active, slope, after_ffn = feed(
        place, layer_input.reshape(count, D), flat_attended, vec, feed_pieces
    )
    after_ffn, near_pieces = together(after_ffn, near_pieces)
    while len(states) < segments - 1:
        states.append(shift(states[-1], 1))
    near_pieces += from_core(near_pieces)
    output, row_grads, after_grad, gate_small, near_half, far_half = near(
        place, ids, near_rows, states[1:], after_ffn.reshape(batch, SEG, D), out_grad, vec,
        near_pieces,
    )

    near_arrived = swap(far_half, "fsdp", 1)
    (message,) = give(place, ids, row_grads, None, (segments - 1,))
    message, near_arrived, after_grad, row_grads = together(
        message, near_arrived, after_grad, row_grads
    )
    arrived = shift(message, -1)
    near_sums = core_sums(near_half, near_arrived)
    near_sums, after_grad = together(near_sums, after_grad)
    near_total = [near_sums[0]] + to_chips(near_sums, chips)
    grad_after, att_grad, feed_small, feed_half, feed_far = feed_back(
        place, after_grad.reshape(count, D), after_attn, active, slope, flat_attended, vec,
        feed_pieces,
    )
    feed_half, feed_far, att_grad, row_grads, arrived, near_total = together(
        feed_half, feed_far, att_grad, row_grads, arrived, near_total
    )
    near_low = chip_sum(near_total)
    feed_arrived = swap(feed_far, "fsdp", 1)
    near_pair = (near_low, swap(near_low, "seq", steps[0]))
    row_grads, near_low = together(row_grads, near_low)
    for distance in range(segments - 2, 1, -1):
        (message,) = give(place, ids, row_grads, arrived, (distance,))
        row_grads, message, feed_arrived, near_pair = together(
            row_grads, message, feed_arrived, near_pair
        )
        arrived = shift(message, -1)
    feed_sums = core_sums(feed_half, feed_arrived)
    feed_sums, row_grads = together(feed_sums, row_grads)
    feed_total = [feed_sums[0]] + to_chips(feed_sums, chips)
    sent, own = give(place, ids, row_grads, None, (1, 0))
    att_grad, sent = together(att_grad, sent)
    *pieces, first_diag = attend_back(
        joined, memory, att_grad.reshape(batch, SEG, D), attended, probs[0], 0, []
    )
    pieces, feed_total, arrived = together(pieces, feed_total, arrived)
    feed_low = chip_sum(feed_total)
    for step in steps[1:]:
        near_low = pair_sum(*near_pair)
        near_low, feed_low = together(near_low, feed_low)
        near_pair = (near_low, swap(near_low, "seq", step))
    kept, passed = halves(feed_low, steps[0])
    feed_pair = (kept, swap(passed, "seq", steps[0]))
    *pieces, last_diag = attend_back(
        joined, memory, att_grad.reshape(batch, SEG, D), attended, probs[1], PAIRS, pieces
    )
    pieces, feed_pair, near_pair = together(pieces, feed_pair, near_pair)
    for step in steps[1:]:
        kept, passed = halves(pair_sum(*feed_pair), step)
        feed_pair = (kept, swap(passed, "seq", step))
    partial, normed, normed_before, norm_small, *message = finish(
        layer_input, before, pieces, grad_after.reshape(batch, SEG, D), own, sent, arrived, vec,
        attn_w,
    )
    partial, message, norm_small, feed_pair = together(partial, message, norm_small, feed_pair)
    feed_low = pair_sum(*feed_pair)
    last = [shift(message[0], -1)]
    attn_half, attn_far = project_grad(
        place, devices, parts, normed, normed_before, pieces, norm_small, gate_small, feed_small,
        [first_diag, last_diag],
    )
    attn_half, attn_far, message, last, feed_low = together(
        attn_half, attn_far, message, last, feed_low
    )
    attn_arrived = swap(attn_far, "fsdp", 1)
    last += [shift(message[sequence], -1) for sequence in range(1, batch)]
    feed_pair = (feed_low, swap(feed_low, "seq", steps[-1]))
    attn_sums = core_sums(attn_half, attn_arrived)
    attn_total = [attn_sums[0]] + to_chips(attn_sums, chips)
    near_grads = unpack(place, near_pair, ((1, D), (1, 2 * D), (1, D)))
    near_grads, attn_total, last, feed_pair = together(near_grads, attn_total, last, feed_pair)
    attn_low = chip_sum(attn_total)
    for step in reversed(steps[:-1]):
        feed_low = joined_halves(*feed_pair, 2 * step)
        feed_pair = (feed_low, swap(feed_low, "seq", step))
    for step in steps[:-1]:
        attn_low = pair_sum(attn_low, swap(attn_low, "seq", step))
    attn_pair = (attn_low, swap(attn_low, "seq", steps[-1]))
    input_grad = partial + jnp.stack(last).astype(F32)
    feed_pair = together(feed_pair, input_grad, attn_low)[0]
    feed_grads = unpack(
        place, feed_pair, ((1, ff), (ratio, D), (1, D)), bit=steps[0]
    )
    feed_grads, attn_pair = together(feed_grads, attn_pair)
    project_out, *smalls = unpack(place, attn_pair, ((1, 3 * D),), parts + [position_bias.shape[0]])
    return (
        output,
        input_grad,
        smalls[0],
        smalls[1],
        project_out,
        feed_grads[2],
        smalls[7],
        smalls[2],
        smalls[3],
        feed_grads[0],
        smalls[6],
        feed_grads[1],
        smalls[4],
        *near_grads,
        smalls[5],
    )


def solution(mesh):
    in_specs = (
        P("fsdp", "seq", None),
        P("fsdp", "seq", None),
        P("fsdp", "seq", None),
        P("fsdp"),
        P("fsdp"),
        P("fsdp", None),
        P("fsdp", None),
        P("fsdp"),
        P("fsdp"),
        P("fsdp"),
        P("fsdp", None),
        P("fsdp"),
        P("fsdp", None),
        P("fsdp"),
        P("fsdp", None),
        P("fsdp", None),
        P("fsdp", None),
        P("fsdp"),
    )
    out_specs = (
        P("fsdp", "seq", None),
        P("fsdp", "seq", None),
        P("fsdp"),
        P("fsdp"),
        P("fsdp", None),
        P("fsdp", None),
        P("fsdp"),
        P("fsdp"),
        P("fsdp"),
        P("fsdp", None),
        P("fsdp"),
        P("fsdp", None),
        P("fsdp"),
        P("fsdp", None),
        P("fsdp", None),
        P("fsdp", None),
        P("fsdp"),
    )
    return jax.shard_map(
        on_device, mesh=mesh, in_specs=in_specs, out_specs=out_specs, check_vma=False
    )
```

```python
import functools
import math

import jax
import jax.numpy as jnp
import numpy as np
from jax import lax
from jax.experimental import pallas as pl
from jax.experimental.pallas import tpu as pltpu
from jax.sharding import PartitionSpec as P

D = 512
H = 8
HD = 64
K = 4
SEG = 512
NB = 32

EPS = 1e-05
HIGH = lax.Precision.HIGHEST
MASKED = -1e30
F32 = jnp.float32
BF16 = jnp.bfloat16
ROWS = 256
SPAN = 2 * SEG + 128
VMEM = 56 << 20


def nn(left, right):
    return lax.dot_general(left, right, (((1,), (0,)), ((), ())), preferred_element_type=F32)


def nt(left, right):
    return lax.dot_general(left, right, (((1,), (1,)), ((), ())), preferred_element_type=F32)


def tn(left, right):
    return lax.dot_general(left, right, (((0,), (0,)), ((), ())), preferred_element_type=F32)


def shape(dims, dtype):
    return jax.ShapeDtypeStruct(tuple(dims), dtype)


def whole(dims):
    zeros = (0,) * len(dims)
    return pl.BlockSpec(tuple(dims), lambda *_: zeros, pipeline_mode=pl.Buffered(1))


def scalars():
    return pl.BlockSpec(memory_space=pltpu.SMEM)


def params(grid_rank):
    return pltpu.CompilerParams(
        dimension_semantics=("arbitrary",) * grid_rank, vmem_limit_bytes=VMEM
    )


def cost(flops, moved, exps=0):
    return pl.CostEstimate(
        flops=int(flops / 30), bytes_accessed=int(moved / 30), transcendentals=int(exps / 30)
    )


def thresholds():
    half_count = NB // 2
    spread_ratio = 2.0 * SEG / half_count
    exact_part = list(range(1, half_count))
    log_part = [
        int(half_count * spread_ratio ** ((bucket_index - half_count) / half_count))
        for bucket_index in range(half_count, NB)
    ]
    return np.array(exact_part + log_part)


def bucket_of(distance):
    return (distance[:, None] >= thresholds()[None, :]).sum(axis=1)


def forward_selector():
    distance = np.arange(SPAN) - 128
    bucket = bucket_of(np.maximum(distance, 0))
    return (np.arange(NB)[:, None] == bucket[None, :]).astype(np.float32)


def backward_selector():
    chosen = forward_selector().T.copy()
    chosen[:128] = 0.0
    return chosen


def norm(values):
    average = jnp.mean(values, axis=-1, keepdims=True)
    centred = values - average
    variance = jnp.mean(centred * centred, axis=-1, keepdims=True)
    rstd_value = lax.rsqrt(variance + EPS)
    return centred * rstd_value, rstd_value


def norm_back(grad_result, hat_value, rstd_value, gain):
    scaled = grad_result * gain
    return rstd_value * (
        scaled
        - jnp.mean(scaled, axis=-1, keepdims=True)
        - hat_value * jnp.mean(scaled * hat_value, axis=-1, keepdims=True)
    )


def rows_sum(values):
    return jnp.sum(values, axis=0, keepdims=True)


def pair_mask(head, values):
    lane = lax.broadcasted_iota(jnp.int32, values.shape, 1)
    keep = lane < HD if head == 0 else lane >= HD
    return jnp.where(keep, values, jnp.zeros_like(values))


def pack_first_kernel(*refs):
    weight_ref, *vector_refs, out_ref = refs
    rows = weight_ref.shape[0]
    out_ref[:rows, :] = weight_ref[...]
    out_ref[rows:, :] = jnp.zeros((16, out_ref.shape[1]), BF16)
    for index, ref in enumerate(vector_refs):
        line = ref[...].astype(F32).reshape(1, -1).astype(BF16)
        out_ref[rows + index : rows + index + 1, : ref.shape[0]] = line


def pack_first(weight, vectors):
    rows, columns = weight.shape
    return pl.pallas_call(
        pack_first_kernel,
        out_shape=shape((rows + 16, columns), BF16),
        cost_estimate=cost(0, 4 * rows * columns),
        name="pack_first",
    )(weight, *vectors)


def pack_kernel(rows, *refs):
    out_ref = refs[-1]
    start = 0
    for ref in refs[:-1]:
        for chunk in range(ref.shape[0] // rows):
            out_ref[:, start : start + ref.shape[1]] = ref[chunk * rows : (chunk + 1) * rows, :]
            start += ref.shape[1]


def pack(rows, weights):
    columns = sum(w.size for w in weights) // rows
    return pl.pallas_call(
        functools.partial(pack_kernel, rows),
        out_shape=shape((rows, columns), BF16),
        cost_estimate=cost(0, 4 * rows * columns),
        name="pack",
    )(*weights)


def unpack_kernel(layout, terms, bit, place_ref, *refs):
    total = [ref[...].astype(F32) for ref in refs[:terms]]
    if bit:
        high = jnp.bitwise_and(place_ref[1], bit) > 0
        mine, other = total
        total = jnp.concatenate(
            [jnp.where(high, other, mine), jnp.where(high, mine, other)], axis=1
        )
    else:
        total = functools.reduce(jnp.add, total)
    refs = refs[terms:]
    rows = refs[0].shape[0]
    start = 0
    for ref, (chunks, width) in zip(refs, layout):
        for chunk in range(chunks):
            ref[chunk * rows : (chunk + 1) * rows, :] = total[:rows, start : start + width]
            start += width
    for index, ref in enumerate(refs[len(layout) :]):
        ref[...] = total[rows + index : rows + index + 1, : ref.shape[0]].reshape(-1)


def unpack_both_kernel(jobs, place_ref, *refs):
    out_refs = refs[sum(terms for _, terms, _, _ in jobs) :]
    start = first_out = 0
    for layout, terms, bit, count in jobs:
        unpack_kernel(
            layout, terms, bit, place_ref, *refs[start : start + terms],
            *out_refs[first_out : first_out + count],
        )
        start += terms
        first_out += count


def unpack(place, *tasks):
    jobs = []
    arrays = []
    outs = []
    for pair, layout, widths, bit in tasks:
        rows = pair[0].shape[0] - (16 if widths else 0)
        part = [shape((rows * chunks, width), F32) for chunks, width in layout]
        part += [shape((width,), F32) for width in widths]
        jobs.append((layout, len(pair), bit, len(part)))
        arrays += pair
        outs += part
    return pl.pallas_call(
        functools.partial(unpack_both_kernel, jobs),
        in_specs=[scalars()] + [pl.BlockSpec(memory_space=pltpu.VMEM)] * len(arrays),
        out_shape=outs,
        compiler_params=pltpu.CompilerParams(vmem_limit_bytes=VMEM),
        cost_estimate=cost(0, sum(8 * array.size for array in arrays)),
        name="unpack",
    )(place, *arrays)


def device_of(place_ref, chip_step, core_step):
    index = place_ref[0]
    chip = lax.shift_right_logical(index, 1)
    core = jnp.bitwise_and(index, 1)
    return jnp.bitwise_xor(chip, chip_step) * 2 + jnp.bitwise_xor(core, core_step)


def assemble(place_ref, layout, piece_refs, out_refs):
    steps = len(piece_refs) // 2
    for core_step in range(2):
        for step in range(steps):
            ref = piece_refs[core_step * steps + step]
            owner = device_of(place_ref, step, core_step)
            rows = D // (2 * steps)
            start = 0
            for out_ref, (chunks, width) in zip(out_refs, layout):
                for chunk in range(chunks):
                    target = pl.multiple_of((owner * chunks + chunk) * rows, rows)
                    out_ref[pl.ds(target, rows), :] = ref[:rows, start : start + width]
                    start += width


def first_kernel(parts, count, place_ref, x_ref, select_ref, *refs):
    piece_refs = refs[:count]
    w_ref, vec_ref, line_ref, joined_ref, small_ref = refs[count:]

    @pl.when(pl.program_id(0) == 0)
    def _():
        assemble(place_ref, ((1, 3 * D),), piece_refs, [w_ref])
        steps = count // 2
        rows = D // count
        for core_step in range(2):
            for step in range(steps):
                owner = device_of(place_ref, step, core_step)
                small_ref[pl.ds(pl.multiple_of(owner * 16, 16), 16), :] = piece_refs[
                    core_step * steps + step
                ][rows:, : small_ref.shape[1]].astype(F32)
        vec_ref[...] = jnp.zeros_like(vec_ref)
        for row, width in enumerate(parts):
            pieces = [small_ref[16 * d + row : 16 * d + row + 1, :width] for d in range(count)]
            vec_ref[row : row + 1, : width * count] = jnp.concatenate(pieces, axis=1)
        row = len(parts)
        table = jnp.concatenate(
            [small_ref[16 * d + row : 16 * d + row + 1, : NB * H // count] for d in range(count)],
            axis=0,
        )
        by_distance = None
        for place in range(NB // count):
            part = lax.dot_general(
                table[:, place * H : (place + 1) * H],
                select_ref[place],
                (((0,), (0,)), ((), ())),
                precision=HIGH,
                preferred_element_type=F32,
            )
            by_distance = part if by_distance is None else by_distance + part
        lane = lax.broadcasted_iota(jnp.int32, by_distance.shape, 1)
        line_ref[...] = jnp.where(lane < 128, MASKED, by_distance)

    hat_value, _ = norm(x_ref[0].astype(F32))
    normed = (hat_value * vec_ref[0:1, :D] + vec_ref[1:2, :D]).astype(BF16)
    joined_ref[0] = nn(normed, w_ref[...]).astype(BF16)


def remember_kernel(x_ref, vec_ref, w_ref, out_ref):
    hat_value, _ = norm(x_ref[0].astype(F32))
    normed = (hat_value * vec_ref[0:1, :D] + vec_ref[1:2, :D]).astype(BF16)
    out_ref[0] = nn(normed, w_ref[:, D:]).astype(BF16)


def remember(before, vec, weight):
    batch = before.shape[0]

    def block(width):
        return pl.BlockSpec((1, SEG, width), lambda b: (b, 0, 0))

    return pl.pallas_call(
        remember_kernel,
        grid=(batch,),
        in_specs=[block(D), whole(vec.shape), whole(weight.shape)],
        out_specs=block(2 * D),
        out_shape=shape((batch, SEG, 2 * D), BF16),
        compiler_params=params(1),
        cost_estimate=cost(4 * batch * SEG * D * D, 6 * batch * SEG * D),
        name="remember",
    )(before, vec, weight)


def first(place, x, pieces, parts, ff):
    batch = x.shape[0]
    count = len(pieces)
    small_width = -(-max(parts) // 128) * 128
    select = forward_selector().reshape(count, NB // count, SPAN).transpose(1, 0, 2)

    def block(width):
        return pl.BlockSpec((1, SEG, width), lambda b: (b, 0, 0))

    return pl.pallas_call(
        functools.partial(first_kernel, parts, count),
        grid=(batch,),
        in_specs=[scalars(), block(D), whole(select.shape)]
        + [whole(piece.shape) for piece in pieces],
        out_specs=[whole((D, 3 * D)), whole((8, ff)), whole((H, SPAN)), block(3 * D)],
        out_shape=[
            shape((D, 3 * D), BF16),
            shape((8, ff), F32),
            shape((H, SPAN), F32),
            shape((batch, SEG, 3 * D), BF16),
        ],
        scratch_shapes=[pltpu.VMEM((16 * count, small_width), F32)],
        compiler_params=params(1),
        cost_estimate=cost(6 * batch * SEG * D * D, 8 * batch * SEG * D),
        name="first",
    )(place, x, jnp.asarray(select), *pieces)


def tiles(place_ref, line_ref, first, own_ref, mem_ref):
    hidden = jnp.where(place_ref[1] > 0, 0.0, MASKED)
    for head in range(2):
        index = 2 * (first + pl.program_id(0)) + head
        line = jnp.broadcast_to(line_ref[pl.ds(index, 1), :], (8, SPAN))
        line = pltpu.roll(line, 0, 1, stride=1, stride_axis=0)
        for group in range(16):
            moved = pltpu.roll(line, 8 * group, 1) if group else line
            for tile in range(2 * SEG // 128):
                start = 2 * SEG - 128 * tile
                row = 128 * tile + 8 * group
                piece = moved[:, start : start + 128]
                own_ref[head, row : row + 8, :] = piece
                mem_ref[head, row : row + 8, :] = piece + hidden


def attend_kernel(first, place_ref, q_ref, k_ref, v_ref, km_ref, vm_ref, line_ref, *refs):
    out_ref, prob_ref, own_ref, mem_ref = refs[-4:]

    @pl.when(pl.program_id(1) == 0)
    def _():
        tiles(place_ref, line_ref, first, own_ref, mem_ref)

    keys = jnp.concatenate([km_ref[0], k_ref[0]], axis=0)
    values = jnp.concatenate([vm_ref[0], v_ref[0]], axis=0)
    for half in range(SEG // ROWS):
        width = SEG + (half + 1) * ROWS
        span = slice(half * ROWS, (half + 1) * ROWS)
        query = q_ref[0, span, :] * BF16(HD**-0.5)
        total = None
        for head in range(2):
            scores = nt(keys[:width], pair_mask(head, query))
            columns = []
            for part in range(ROWS // 128):
                block = half * (ROWS // 128) + part
                bias = jnp.concatenate(
                    [
                        mem_ref[head, (3 - block) * 128 : (7 - block) * 128, :],
                        own_ref[head, (7 - block) * 128 :, :],
                    ],
                    axis=0,
                )
                used = bias.shape[0]
                piece = scores[:used, part * 128 : (part + 1) * 128] + bias
                top = jnp.max(piece, axis=0, keepdims=True)
                weight = jnp.exp(piece - top)
                weight = (weight * (1.0 / jnp.sum(weight, axis=0, keepdims=True))).astype(BF16)
                if used < width:
                    weight = jnp.concatenate(
                        [weight, jnp.zeros((width - used, 128), BF16)], axis=0
                    )
                columns.append(weight)
            probs = jnp.concatenate(columns, axis=1)
            prob_ref[0, head, :width, span] = probs
            product = tn(probs, pair_mask(head, values)[:width])
            total = product if total is None else total + product
        out_ref[0, span, :] = total.astype(BF16)


PAIRS = H // 4


def attend(place, joined, memory, line, first, so_far):
    batch = joined.shape[0]

    def lanes(offset):
        return pl.BlockSpec((1, SEG, 128), lambda h, b: (b, 0, offset + first + h))

    work = batch * H * SEG * SEG
    extra = [] if so_far is None else [so_far]
    return pl.pallas_call(
        functools.partial(attend_kernel, first),
        grid=(PAIRS, batch),
        in_specs=[scalars()]
        + [lanes(0), lanes(2 * PAIRS), lanes(4 * PAIRS), lanes(0), lanes(2 * PAIRS)]
        + [whole(line.shape)]
        + [pl.BlockSpec(memory_space=pl.ANY)] * len(extra),
        out_specs=[
            lanes(0),
            pl.BlockSpec((1, 2, 2 * SEG, SEG), lambda h, b: (b, h, 0, 0)),
        ],
        out_shape=[shape((batch, SEG, D), BF16), shape((batch, H // 2, 2 * SEG, SEG), BF16)],
        scratch_shapes=[pltpu.VMEM((2, 2 * SEG, 128), F32)] * 2,
        input_output_aliases={7: 0} if extra else {},
        compiler_params=params(2),
        cost_estimate=cost(16 * HD * work, 3 * work, work),
        name="attend",
    )(place, joined, joined, joined, memory, memory, line, *extra)


def attend_back_kernel(
    q_ref, k_ref, v_ref, km_ref, vm_ref, grad_ref, out_ref, prob_ref, *refs
):
    dq_ref, dk_ref, dv_ref, dkm_ref, dvm_ref, diag_ref, grid_ref = refs[-7:]
    keys = jnp.concatenate([km_ref[0], k_ref[0]], axis=0)
    values = jnp.concatenate([vm_ref[0], v_ref[0]], axis=0)
    step = pl.program_id(1)

    @pl.when(step == 0)
    def _():
        grid_ref[...] = jnp.zeros_like(grid_ref)

    key_parts = []
    value_parts = []
    for half in range(SEG // ROWS):
        width = SEG + (half + 1) * ROWS
        span = slice(half * ROWS, (half + 1) * ROWS)
        grad = grad_ref[0, span, :]
        query = q_ref[0, span, :] * BF16(HD**-0.5)
        product = (grad.astype(F32) * out_ref[0, span, :].astype(F32)).T
        query_total = key_total = value_total = None
        for head in range(2):
            grad_head = pair_mask(head, grad)
            delta = jnp.sum(product[head * HD : (head + 1) * HD], axis=0, keepdims=True)
            probs = prob_ref[0, head, :width, span]
            scored = probs.astype(F32) * (nt(values[:width], grad_head) - delta)
            for part in range(ROWS // 128):
                block = half * (ROWS // 128) + part
                used = SEG + (block + 1) * 128
                grid_ref[head, (3 - block) * 128 :, :] += scored[
                    :used, part * 128 : (part + 1) * 128
                ]
            scored = scored.astype(BF16)
            for_key = nn(scored, pair_mask(head, query))
            for_value = nn(probs, grad_head)
            for_query = tn(scored, pair_mask(head, keys)[:width])
            key_total = for_key if key_total is None else key_total + for_key
            value_total = for_value if value_total is None else value_total + for_value
            query_total = for_query if query_total is None else query_total + for_query
        dq_ref[0, span, :] = (query_total * HD**-0.5).astype(BF16)
        key_parts.append(key_total)
        value_parts.append(value_total)
    for pieces, mem_ref, own_ref in (
        (key_parts, dkm_ref, dk_ref),
        (value_parts, dvm_ref, dv_ref),
    ):
        both = pieces[0] + pieces[1][: SEG + ROWS]
        mem_ref[0] = both[:SEG].astype(BF16)
        own_ref[0, :ROWS] = both[SEG:].astype(BF16)
        own_ref[0, ROWS:] = pieces[1][SEG + ROWS :].astype(BF16)

    @pl.when(step == pl.num_programs(1) - 1)
    def _():
        for head in range(2):
            total = None
            for group in range(16):
                pieces = [
                    grid_ref[head, 128 * tile + 8 * group : 128 * tile + 8 * group + 8, :]
                    for tile in reversed(range(2 * SEG // 128))
                ]
                line = jnp.concatenate([jnp.zeros((8, 128), F32)] + pieces, axis=1)
                if group:
                    line = pltpu.roll(line, SPAN - 8 * group, 1)
                total = line if total is None else total + line
            lines = [total[:1]] + [
                pltpu.roll(total[row : row + 1], SPAN - row, 1) for row in range(1, 8)
            ]
            diag_ref[0, head : head + 1, :] = functools.reduce(jnp.add, lines)


def attend_back(joined, memory, grad, attended, probs, first, so_far):
    batch = joined.shape[0]

    def lanes(offset):
        return pl.BlockSpec((1, SEG, 128), lambda h, b: (b, 0, offset + first + h))

    half = shape((batch, SEG, D), BF16)
    work = batch * H * SEG * SEG
    return pl.pallas_call(
        attend_back_kernel,
        grid=(PAIRS, batch),
        in_specs=[lanes(0), lanes(2 * PAIRS), lanes(4 * PAIRS), lanes(0), lanes(2 * PAIRS)]
        + [lanes(0)] * 2
        + [pl.BlockSpec((1, 2, 2 * SEG, SEG), lambda h, b: (b, h, 0, 0))]
        + [pl.BlockSpec(memory_space=pl.ANY)] * len(so_far),
        out_specs=[lanes(0)] * 5 + [pl.BlockSpec((1, 2, SPAN), lambda h, b: (h, 0, 0))],
        out_shape=[half] * 5 + [shape((PAIRS, 2, SPAN), F32)],
        scratch_shapes=[pltpu.VMEM((2, 2 * SEG, 128), F32)],
        input_output_aliases={8 + i: i for i in range(len(so_far))},
        compiler_params=params(2),
        cost_estimate=cost(32 * HD * work, 3 * work),
        name="attend_back",
    )(joined, joined, joined, memory, memory, grad, attended, probs, *so_far)


def feed_layout(ff):
    return ((1, D), (1, ff), (ff // D, D))


def feed_scratch(ff):
    return [pltpu.VMEM((D, D), BF16), pltpu.VMEM((D, ff), BF16), pltpu.VMEM((ff, D), BF16)]


def feed_kernel(count, place_ref, x_ref, att_ref, vec_ref, *refs):
    piece_refs = refs[:count]
    (
        after_attn_ref, active_ref, slope_ref, after_ffn_ref, merge_ref, expand_ref, reduce_ref,
    ) = refs[count:]

    @pl.when(pl.program_id(0) == 0)
    def _():
        assemble(place_ref, feed_layout(expand_ref.shape[1]), piece_refs, refs[-3:])

    after_attn = x_ref[...].astype(F32) + nn(att_ref[...], merge_ref[...])
    after_attn_ref[...] = after_attn
    hat_value, _ = norm(after_attn)
    normed = (hat_value * vec_ref[2:3, :D] + vec_ref[3:4, :D]).astype(BF16)
    pre = nn(normed, expand_ref[...]) + vec_ref[6:7, :]
    cdf = 0.5 * (1.0 + lax.erf(pre * (1.0 / math.sqrt(2.0))))
    slope = cdf + pre * jnp.exp(-0.5 * pre * pre) * (1.0 / math.sqrt(2.0 * math.pi))
    slope_ref[...] = slope.astype(BF16)
    active = (pre * cdf).astype(BF16)
    active_ref[...] = active
    after_ffn = after_attn + nn(active, reduce_ref[...]) + vec_ref[4:5, :D]
    after_ffn_ref[...] = after_ffn


def feed(place, x, attended, vec, pieces):
    count = x.shape[0]
    ff = vec.shape[1]

    def rows(width):
        return pl.BlockSpec((ROWS, width), lambda i: (i, 0))

    return pl.pallas_call(
        functools.partial(feed_kernel, len(pieces)),
        grid=(count // ROWS,),
        in_specs=[scalars(), rows(D), rows(D), whole(vec.shape)]
        + [whole(piece.shape) for piece in pieces],
        out_specs=[rows(D), rows(ff), rows(ff), rows(D)],
        out_shape=[
            shape((count, D), F32),
            shape((count, ff), BF16),
            shape((count, ff), BF16),
            shape((count, D), F32),
        ],
        scratch_shapes=feed_scratch(ff),
        compiler_params=params(1),
        cost_estimate=cost(4 * count * D * (ff + D), 12 * count * ff, 2 * count * ff),
        name="feed",
    )(place, x, attended, vec, *pieces)


def add_rows(ref, row, values):
    ref[row : row + 1, : values.shape[1]] += values


def scatter_rows(place_ref, total_ref, near_ref, far_ref, start, chunks):
    steps, rows = near_ref.shape[0], near_ref.shape[1]
    width = total_ref.shape[1]
    for core_step, ref in ((0, near_ref), (1, far_ref)):
        for step in range(steps):
            owner = device_of(place_ref, step, core_step)
            for chunk in range(chunks):
                source = pl.multiple_of((owner * chunks + chunk) * rows, rows)
                column = start + chunk * width
                ref[step, :, column : column + width] = total_ref[
                    pl.ds(source, rows), :
                ].astype(BF16)
    return start + chunks * width


def feed_back_kernel(
    count, place_ref, grad_ref, after_ref, active_ref, slope_ref, att_ref, vec_ref, *refs
):
    piece_refs = refs[:count]
    (
        after_grad_ref, att_grad_ref, small_ref, near_ref, far_ref,
        expand_total, reduce_total, merge_total, merge_ref, expand_ref, reduce_ref,
    ) = refs[count:]
    step = pl.program_id(0)

    @pl.when(step == 0)
    def _():
        assemble(place_ref, feed_layout(expand_ref.shape[1]), piece_refs, refs[-3:])
        expand_total[...] = jnp.zeros_like(expand_total)
        merge_total[...] = jnp.zeros_like(merge_total)
        reduce_total[...] = jnp.zeros_like(reduce_total)
        small_ref[...] = jnp.zeros_like(small_ref)

    grad = grad_ref[...]
    low = grad.astype(BF16)
    add_rows(small_ref, 2, rows_sum(low.astype(F32)))
    reduce_total[...] += tn(active_ref[...], low)
    pre_grad = (nt(low, reduce_ref[...]) * slope_ref[...].astype(F32)).astype(BF16)
    add_rows(small_ref, 3, rows_sum(pre_grad.astype(F32)))
    hat_value, rstd_value = norm(after_ref[...])
    gain = vec_ref[2:3, :D]
    normed = (hat_value * gain + vec_ref[3:4, :D]).astype(BF16)
    expand_total[...] += tn(normed, pre_grad)
    normed_grad = nt(pre_grad, expand_ref[...])
    add_rows(small_ref, 0, rows_sum(normed_grad * hat_value))
    add_rows(small_ref, 1, rows_sum(normed_grad))
    after_grad = grad + norm_back(normed_grad, hat_value, rstd_value, gain)
    after_grad_ref[...] = after_grad
    merge_grad = after_grad.astype(BF16)
    merge_total[...] += tn(att_ref[...], merge_grad)
    att_grad_ref[...] = nt(merge_grad, merge_ref[...]).astype(BF16)

    @pl.when(step == pl.num_programs(0) - 1)
    def _():
        start = scatter_rows(place_ref, expand_total, near_ref, far_ref, 0, 1)
        ratio = reduce_total.shape[0] // D
        start = scatter_rows(place_ref, reduce_total, near_ref, far_ref, start, ratio)
        scatter_rows(place_ref, merge_total, near_ref, far_ref, start, 1)


def feed_back(place, grad, after_attn, active, slope, attended, vec, pieces):
    count = grad.shape[0]
    ff = vec.shape[1]
    devices = len(pieces)

    def rows(width):
        return pl.BlockSpec((ROWS, width), lambda i: (i, 0))

    packed = (devices // 2, D // devices, 2 * ff + D)
    return pl.pallas_call(
        functools.partial(feed_back_kernel, devices),
        grid=(count // ROWS,),
        in_specs=[scalars(), rows(D), rows(D), rows(ff), rows(ff), rows(D), whole(vec.shape)]
        + [whole(piece.shape) for piece in pieces],
        out_specs=[rows(D), rows(D), whole((8, ff)), whole(packed), whole(packed)],
        out_shape=[
            shape((count, D), F32),
            shape((count, D), BF16),
            shape((8, ff), F32),
            shape(packed, BF16),
            shape(packed, BF16),
        ],
        scratch_shapes=[
            pltpu.VMEM((D, ff), F32),
            pltpu.VMEM((ff, D), F32),
            pltpu.VMEM((D, D), F32),
        ]
        + feed_scratch(ff),
        compiler_params=params(1),
        cost_estimate=cost(8 * count * D * (ff + D // 2), 12 * count * ff),
        name="feed_back",
    )(place, grad, after_attn, active, slope, attended, vec, *pieces)


def chosen_rows(ids, slot, rows):
    place = lax.broadcasted_iota(jnp.int32, (ids.shape[0], SEG), 1)
    return nn(jnp.where(ids[:, slot : slot + 1] == place, 1.0, 0.0).astype(BF16), rows)


def ids_down(ids):
    return jnp.concatenate([ids] * 2, axis=0).T


def take_kernel(distance, started, place_ref, ids_ref, rows_ref, *refs):
    out_ref = refs[-1]
    ids = ids_down(ids_ref[0] - (place_ref[1] - distance) * SEG)
    rows = rows_ref[0]
    for slot in range(K):
        taken = chosen_rows(ids, slot, rows).astype(BF16)
        out_ref[0, slot] = refs[0][0, slot] + taken if started else taken


def take(place, ids, rows, distance, so_far):
    batch = ids.shape[0]
    block = pl.BlockSpec((1, K, SEG, D), lambda b: (b, 0, 0, 0))
    return pl.pallas_call(
        functools.partial(take_kernel, distance, len(so_far)),
        grid=(batch,),
        in_specs=[
            scalars(),
            pl.BlockSpec((1, K, SEG), lambda b: (b, 0, 0)),
            pl.BlockSpec((1, SEG, D), lambda b: (b, 0, 0)),
        ]
        + [block] * len(so_far),
        out_specs=block,
        out_shape=shape((batch, K, SEG, D), BF16),
        input_output_aliases={3: 0} if so_far else {},
        compiler_params=params(1),
        cost_estimate=cost(2 * batch * K * SEG * SEG * D, 4 * batch * K * SEG * D),
        name="take",
    )(place, ids, rows, *so_far)


def give_kernel(distances, started, place_ref, ids_ref, grad_ref, *refs):
    out_refs = refs[started:]
    place = lax.broadcasted_iota(jnp.int32, (SEG, SEG), 0)
    for index, distance in enumerate(distances):
        ids = ids_ref[0] - (place_ref[1] - distance) * SEG
        total = None
        for slot in range(K):
            chosen = jnp.where(ids[slot : slot + 1, :] == place, 1.0, 0.0).astype(BF16)
            part = nn(chosen, grad_ref[0, slot])
            total = part if total is None else total + part
        if started and index == 0:
            total = total + refs[0][0].astype(F32)
        out_refs[index][0] = total.astype(out_refs[index].dtype)


def give(place, ids, grads, arrived, distances):
    batch = ids.shape[0]
    block = pl.BlockSpec((1, SEG, D), lambda b: (b, 0, 0))
    started = arrived is not None
    work = len(distances) * batch * K * SEG * D
    return pl.pallas_call(
        functools.partial(give_kernel, distances, started),
        grid=(batch,),
        in_specs=[
            scalars(),
            pl.BlockSpec((1, K, SEG), lambda b: (b, 0, 0)),
            pl.BlockSpec((1, K, SEG, D), lambda b: (b, 0, 0, 0)),
        ]
        + [block] * started,
        out_specs=[block] * len(distances),
        out_shape=[shape((batch, SEG, D), BF16 if d else F32) for d in distances],
        compiler_params=params(1),
        cost_estimate=cost(2 * work * SEG, 2 * work),
        name="give",
    )(place, ids, grads, *([arrived] if started else []))


def near_kernel(
    hops, count, place_ref, ids_ref, rows_ref, after_ref, grad_ref, vec_ref, *refs
):
    state_refs = refs[:hops]
    piece_refs = refs[hops : hops + count]
    (
        out_ref, row_grad_ref, after_grad_ref, small_ref, near_ref, far_ref,
        keys_total, merge_total, query_total, nq_ref, keys_ref, merge_ref,
    ) = refs[hops + count :]
    first = (pl.program_id(0) == 0) & (pl.program_id(1) == 0)
    last = (pl.program_id(0) == pl.num_programs(0) - 1) & (
        pl.program_id(1) == pl.num_programs(1) - 1
    )

    @pl.when(first)
    def _():
        keys_total[...] = jnp.zeros_like(keys_total)
        merge_total[...] = jnp.zeros_like(merge_total)
        query_total[...] = jnp.zeros_like(query_total)
        assemble(place_ref, ((1, D), (1, 2 * D), (1, D)), piece_refs, refs[-3:])
        small_ref[...] = jnp.zeros_like(small_ref)

    scale = HD**-0.5
    place = lax.broadcasted_iota(jnp.int32, (K * D, 128), 0)
    lane = lax.broadcasted_iota(jnp.int32, (K * D, 128), 1)
    group = lax.shift_right_logical(place, 9) * H + jnp.bitwise_and(
        lax.shift_right_logical(place, 6), H - 1
    )
    gather = jnp.where(jnp.bitwise_and(lane, K * H - 1) == group, 1.0, 0.0).astype(BF16)
    lane = lax.broadcasted_iota(jnp.int32, (128, K * D), 0)
    place = lax.broadcasted_iota(jnp.int32, (128, K * D), 1)
    group = lax.shift_right_logical(place, 9) * H + jnp.bitwise_and(
        lax.shift_right_logical(place, 6), H - 1
    )
    spread = jnp.where(
        (jnp.bitwise_and(lane, K * H - 1) == group) & (lane < 2 * K * H), 1.0, 0.0
    ).astype(BF16)

    def over_slots(combine, values):
        values = combine(values, pltpu.roll(values, 2 * H, 1))
        return combine(values, pltpu.roll(values, H, 1))

    def to_rows(values):
        high = values.astype(BF16)
        low = (values - high.astype(F32)).astype(BF16)
        lane = lax.broadcasted_iota(jnp.int32, values.shape, 1)
        return nn(jnp.where(lane < K * H, high, low), spread)

    def slot_of(values, slot):
        return values[:, slot * D : (slot + 1) * D]

    after_ffn = after_ref[0]
    hidden_low = after_ffn.astype(BF16)
    query = nn(hidden_low, nq_ref[...]).astype(BF16)
    query_float = query.astype(F32)
    ids = ids_down(ids_ref[0])
    states = jnp.concatenate([ref[0] for ref in state_refs], axis=0) if hops else None
    taken = []
    for slot in range(K):
        total = rows_ref[0, slot]
        if hops:
            chosen = []
            for hop in range(hops):
                column = ids[:, slot : slot + 1] - (place_ref[1] - hop - 2) * SEG
                here = lax.broadcasted_iota(jnp.int32, (ids.shape[0], SEG), 1)
                chosen.append(jnp.where(column == here, 1.0, 0.0).astype(BF16))
            moved = nn(jnp.concatenate(chosen, axis=1), states)
            total = total + moved.astype(BF16)
        taken.append(total)
    pairs = [nn(rows, keys_ref[...]).astype(BF16) for rows in taken]
    near_key = [pair[:, :D] for pair in pairs]
    near_value = [pair[:, D:] for pair in pairs]
    products = jnp.concatenate([query * key for key in near_key], axis=1)
    scores = nn(products, gather) * scale
    weights = jnp.exp(scores - over_slots(jnp.maximum, scores))
    probs = weights / over_slots(jnp.add, weights)
    prob_rows = to_rows(probs)
    mixed = functools.reduce(
        jnp.add, [slot_of(prob_rows, i) * v.astype(F32) for i, v in enumerate(near_value)]
    ).astype(BF16)
    near_out = nn(mixed, merge_ref[...])
    gate_vector = vec_ref[5:6, :D]
    gate = jax.nn.sigmoid(jnp.sum(after_ffn * gate_vector, axis=-1, keepdims=True))
    out_ref[0] = (gate * after_ffn + (1.0 - gate) * near_out).astype(BF16)
    grad = grad_ref[0].astype(F32)
    gate_grad = (
        jnp.sum(grad * (after_ffn - near_out), axis=-1, keepdims=True) * gate * (1.0 - gate)
    )
    add_rows(small_ref, 0, rows_sum(gate_grad * after_ffn))
    near_grad = ((1.0 - gate) * grad).astype(BF16)
    merge_total[...] += tn(mixed, near_grad)
    mixed_low = nt(near_grad, merge_ref[...]).astype(BF16)
    mixed_grad = mixed_low.astype(F32)
    products = jnp.concatenate([mixed_low * value for value in near_value], axis=1)
    prob_grads = nn(products, gather)
    inner = over_slots(jnp.add, probs * prob_grads)
    score_rows = to_rows(probs * (prob_grads - inner) * scale)
    query_grad = None
    for slot in range(K):
        score_grad = slot_of(score_rows, slot)
        part = score_grad * near_key[slot].astype(F32)
        query_grad = part if query_grad is None else query_grad + part
        pair_grad = jnp.concatenate(
            [
                (score_grad * query_float).astype(BF16),
                (slot_of(prob_rows, slot) * mixed_grad).astype(BF16),
            ],
            axis=1,
        )
        keys_total[...] += tn(taken[slot], pair_grad)
        row_grad_ref[0, slot] = nt(pair_grad, keys_ref[...]).astype(BF16)
    query_grad = query_grad.astype(BF16)
    query_total[...] += tn(hidden_low, query_grad)
    after_grad_ref[0] = gate * grad + gate_grad * gate_vector + nt(query_grad, nq_ref[...])

    @pl.when(last)
    def _():
        start = scatter_rows(place_ref, query_total, near_ref, far_ref, 0, 1)
        start = scatter_rows(place_ref, keys_total, near_ref, far_ref, start, 1)
        scatter_rows(place_ref, merge_total, near_ref, far_ref, start, 1)


def near(place, ids, rows, states, after_ffn, grad, vec, pieces):
    batch = rows.shape[0]
    devices = len(pieces)
    row_block = pl.BlockSpec((1, K, ROWS, D), lambda b, i: (b, 0, i, 0))
    block = pl.BlockSpec((1, ROWS, D), lambda b, i: (b, i, 0))
    packed = (devices // 2, D // devices, 4 * D)
    count = batch * SEG
    return pl.pallas_call(
        functools.partial(near_kernel, len(states), devices),
        grid=(batch, SEG // ROWS),
        in_specs=[scalars(), pl.BlockSpec((1, K, ROWS), lambda b, i: (b, 0, i))]
        + [row_block, block, block, whole(vec.shape)]
        + [pl.BlockSpec((1, SEG, D), lambda b, i: (b, 0, 0))] * len(states)
        + [whole(piece.shape) for piece in pieces],
        out_specs=[block, row_block, block, whole((8, D)), whole(packed), whole(packed)],
        out_shape=[
            shape((batch, SEG, D), BF16),
            shape((batch, K, SEG, D), BF16),
            shape((batch, SEG, D), F32),
            shape((8, D), F32),
            shape(packed, BF16),
            shape(packed, BF16),
        ],
        scratch_shapes=[
            pltpu.VMEM((D, 2 * D), F32),
            pltpu.VMEM((D, D), F32),
            pltpu.VMEM((D, D), F32),
            pltpu.VMEM((D, D), BF16),
            pltpu.VMEM((D, 2 * D), BF16),
            pltpu.VMEM((D, D), BF16),
        ],
        compiler_params=params(2),
        cost_estimate=cost(
            2 * count * D * D * (11 * K + 6), count * D * (4 * K + 12), count * K * D
        ),
        name="near",
    )(place, ids, rows, after_ffn, grad, vec, *states, *pieces)


def finish_kernel(
    x_ref, before_ref, dq_ref, dk_ref, dv_ref, dkm_ref, dvm_ref, grad_ref, own_ref, sent_ref,
    arrived_ref, vec_ref, w_ref,
    part_ref, normed_ref, normed_before_ref, small_ref, *send_refs,
):
    @pl.when(pl.program_id(0) == 0)
    def _():
        small_ref[...] = jnp.zeros_like(small_ref)

    gain = vec_ref[0:1, :D]
    shift_by = vec_ref[1:2, :D]
    hat_before, rstd_before = norm(before_ref[0].astype(F32))
    normed_before_ref[0] = (hat_before * gain + shift_by).astype(BF16)
    before_grad = nt(dkm_ref[0], w_ref[:, D : 2 * D]) + nt(dvm_ref[0], w_ref[:, 2 * D :])
    send = (
        sent_ref[0].astype(F32)
        + arrived_ref[0].astype(F32)
        + norm_back(before_grad, hat_before, rstd_before, gain)
    ).astype(BF16)
    for sequence, send_ref in enumerate(send_refs):

        @pl.when(pl.program_id(0) == sequence)
        def _():
            send_ref[...] = send

    hat_value, rstd_value = norm(x_ref[0].astype(F32))
    normed_ref[0] = (hat_value * gain + shift_by).astype(BF16)
    normed_grad = (
        nt(dq_ref[0], w_ref[:, :D])
        + nt(dk_ref[0], w_ref[:, D : 2 * D])
        + nt(dv_ref[0], w_ref[:, 2 * D :])
    )
    add_rows(small_ref, 0, rows_sum(normed_grad * hat_value) + rows_sum(before_grad * hat_before))
    add_rows(small_ref, 1, rows_sum(normed_grad) + rows_sum(before_grad))
    part_ref[0] = (
        grad_ref[0] + own_ref[0] + norm_back(normed_grad, hat_value, rstd_value, gain)
    )


def finish(x, before, pieces, grad, own, sent, arrived, vec, weight):
    batch = x.shape[0]
    block = pl.BlockSpec((1, SEG, D), lambda b: (b, 0, 0))
    low = shape((batch, SEG, D), BF16)
    return pl.pallas_call(
        finish_kernel,
        grid=(batch,),
        in_specs=[block] * 11 + [whole(w.shape) for w in (vec, weight)],
        out_specs=[block] * 3 + [whole((8, D))] + [whole((SEG, D))] * batch,
        out_shape=[shape((batch, SEG, D), F32), low, low, shape((8, D), F32)]
        + [shape((SEG, D), BF16)] * batch,
        compiler_params=params(1),
        cost_estimate=cost(10 * batch * SEG * D * D, 34 * batch * SEG * D),
        name="finish",
    )(x, before, *pieces, grad, own, sent, arrived, vec, weight)


def project_grad_kernel(
    parts, place_ref, normed_ref, normed_before_ref, dq_ref, dk_ref, dv_ref, dkm_ref, dvm_ref,
    norm_ref, gate_ref, feed_ref, select_ref, first_ref, last_ref,
    near_ref, far_ref, w_total, small_total,
):
    step = pl.program_id(0)

    @pl.when(step == 0)
    def _():
        w_total[...] = jnp.zeros_like(w_total)

    normed = normed_ref[0]
    normed_before = normed_before_ref[0]
    w_total[:, :D] += tn(normed, dq_ref[0])
    w_total[:, D : 2 * D] += tn(normed, dk_ref[0]) + tn(normed_before, dkm_ref[0])
    w_total[:, 2 * D :] += tn(normed, dv_ref[0]) + tn(normed_before, dvm_ref[0])

    @pl.when(step == pl.num_programs(0) - 1)
    def _():
        devices = small_total.shape[0] // 16
        rows = w_total.shape[0] // devices
        small_total[...] = jnp.zeros_like(small_total)
        lines = [
            norm_ref[0:1, :],
            norm_ref[1:2, :],
            feed_ref[0:1, :D],
            feed_ref[1:2, :D],
            feed_ref[2:3, :D],
            gate_ref[0:1, :],
            feed_ref[3:4, :],
        ]
        for index, (line, width) in enumerate(zip(lines, parts)):
            for d in range(devices):
                row = 16 * d + index
                small_total[row : row + 1, :width] = line[:, d * width : (d + 1) * width]
        table = lax.dot_general(
            jnp.concatenate([ref[i] for ref in (first_ref, last_ref) for i in range(PAIRS)], axis=0),
            select_ref[...],
            (((1,), (0,)), ((), ())),
            precision=HIGH,
            preferred_element_type=F32,
        )
        own_buckets = NB // devices
        bucket = lax.broadcasted_iota(jnp.int32, (devices, NB), 1)
        owner = lax.broadcasted_iota(jnp.int32, (devices, NB), 0)
        pieces = []
        for place in range(own_buckets):
            chosen = jnp.where(bucket == owner * own_buckets + place, 1.0, 0.0)
            pieces.append(
                lax.dot_general(
                    chosen,
                    table,
                    (((1,), (1,)), ((), ())),
                    precision=HIGH,
                    preferred_element_type=F32,
                )
            )
        buckets = jnp.concatenate(pieces, axis=1)
        for d in range(devices):
            row = 16 * d + len(parts)
            small_total[row : row + 1, : buckets.shape[1]] = buckets[d : d + 1, :]
        width = small_total.shape[1]
        for core_step, ref in ((0, near_ref), (1, far_ref)):
            for chip_step in range(ref.shape[0]):
                target = device_of(place_ref, chip_step, core_step)
                source = pl.multiple_of(target * rows, rows)
                ref[chip_step, :rows, :] = w_total[pl.ds(source, rows), :].astype(BF16)
                ref[chip_step, rows:, :] = jnp.zeros((16, ref.shape[2]), BF16)
                lines = small_total[pl.ds(pl.multiple_of(target * 16, 16), 16), :]
                ref[chip_step, rows:, :width] = lines.astype(BF16)


def project_grad(place, devices, parts, normed, normed_before, pieces, norm_small, gate, feed_small, diags):
    batch = normed.shape[0]
    block = pl.BlockSpec((1, SEG, D), lambda b: (b, 0, 0))
    packed = (devices // 2, D // devices + 16, 3 * D)
    select = jnp.asarray(backward_selector())
    small_width = -(-max(parts) // 128) * 128
    return pl.pallas_call(
        functools.partial(project_grad_kernel, parts),
        grid=(batch,),
        in_specs=[scalars()]
        + [block] * 7
        + [whole(w.shape) for w in (norm_small, gate, feed_small, select, *diags)],
        out_specs=[whole(packed)] * 2,
        out_shape=[shape(packed, BF16)] * 2,
        scratch_shapes=[
            pltpu.VMEM((D, 3 * D), F32),
            pltpu.VMEM((16 * devices, small_width), F32),
        ],
        compiler_params=params(1),
        cost_estimate=cost(10 * batch * SEG * D * D, 20 * batch * SEG * D),
        name="project_grad",
    )(
        place, normed, normed_before, *pieces, norm_small, gate, feed_small, select, *diags,
    )


def shift(block, distance):
    count = lax.axis_size("seq")
    return lax.ppermute(block, "seq", [(i, (i + distance) % count) for i in range(count)])


def swap(block, axis, bits):
    count = lax.axis_size(axis)
    return lax.ppermute(block, axis, [(i, i ^ bits) for i in range(count)])


def together(*values):
    return lax.optimization_barrier(values)


def chip_steps():
    steps = list(range(1, lax.axis_size("fsdp") // 2))
    cut = (2 * len(steps) + 2) // 3
    return steps[:cut], steps[cut:]


def from_chips(shard, steps):
    return [swap(shard, "fsdp", 2 * step) for step in steps]


def from_core(pieces):
    return [swap(piece, "fsdp", 1) for piece in pieces]


def core_sums(near_half, arrived):
    return [
        (near_half[step].astype(F32) + arrived[step].astype(F32)).astype(BF16)
        for step in range(near_half.shape[0])
    ]


def to_chips(pieces, steps):
    return [swap(pieces[step], "fsdp", 2 * step) for step in steps]


def chip_sum(pieces):
    return functools.reduce(jnp.add, [piece.astype(F32) for piece in pieces]).astype(BF16)


def segment_steps():
    return [1 << bit for bit in range(lax.axis_size("seq").bit_length() - 1)]


def halves(values, bit):
    half = values.shape[1] // 2
    high = jnp.bitwise_and(lax.axis_index("seq"), bit) > 0
    left, right = values[:, :half], values[:, half:]
    return jnp.where(high, right, left), jnp.where(high, left, right)


def joined_halves(mine, other, bit):
    high = jnp.bitwise_and(lax.axis_index("seq"), bit) > 0
    return jnp.concatenate([jnp.where(high, other, mine), jnp.where(high, mine, other)], axis=1)


def pair_sum(left, right):
    return (left.astype(F32) + right.astype(F32)).astype(BF16)


def on_device(
    layer_input,
    neighbour_ids,
    out_grad,
    attn_norm_gain,
    attn_norm_bias,
    attn_project,
    attn_merge,
    position_bias,
    ffn_norm_gain,
    ffn_norm_bias,
    ffn_expand,
    expand_bias,
    ffn_reduce,
    reduce_bias,
    near_query,
    near_keys,
    near_merge,
    gate_vector,
):
    batch = layer_input.shape[0]
    count = batch * SEG
    devices = lax.axis_size("fsdp")
    segments = lax.axis_size("seq")
    rows = attn_project.shape[0]
    ff = ffn_expand.shape[1]
    ratio = ff // D

    place = jnp.stack([lax.axis_index("fsdp"), lax.axis_index("seq")]).astype(jnp.int32)
    vectors = [
        attn_norm_gain, attn_norm_bias, ffn_norm_gain, ffn_norm_bias, reduce_bias, gate_vector,
        expand_bias, position_bias,
    ]
    parts = [v.shape[0] for v in vectors[:-1]]
    steps = segment_steps()
    near_steps, far_steps = chip_steps()
    chips = near_steps + far_steps

    attn_shard = pack_first(attn_project, vectors)
    attn_pieces = [attn_shard] + from_chips(attn_shard, chips)
    before = shift(layer_input, 1)
    ids = jnp.swapaxes(neighbour_ids, 1, 2)
    feed_shard = pack(rows, [attn_merge, ffn_expand, ffn_reduce])
    near_shard = pack(rows, [near_query, near_keys, near_merge])
    near_rows = take(place, ids, layer_input, 0, [])
    near_rows, feed_shard, near_shard, attn_pieces = together(
        near_rows, feed_shard, near_shard, attn_pieces
    )
    feed_pieces = [feed_shard] + from_chips(feed_shard, near_steps)
    attn_w, vec, line, joined = first(
        place, layer_input, attn_pieces + from_core(attn_pieces), parts, ff
    )
    joined, before = together(joined, before)
    states = [before]
    if segments > 2:
        states.append(shift(before, 1))
    memory = remember(before, vec, attn_w)
    attended = None
    probs = []
    for part in range(2):
        attended, part_probs = attend(place, joined, memory, line, part * PAIRS, attended)
        probs.append(part_probs)
        if part == 0:
            attended, memory, feed_pieces, near_rows = together(
                attended, memory, feed_pieces, near_rows
            )
            feed_far = from_core(feed_pieces)
            feed_rest = from_chips(feed_pieces[0], far_steps)
            near_rows = take(place, ids, before, 1, [near_rows])
            attended, near_rows, states = together(attended, near_rows, states)
            if len(states) < segments - 1:
                states.append(shift(states[-1], 1))
    attended, feed_far, feed_rest, near_shard = together(
        attended, feed_far, feed_rest, near_shard
    )
    feed_pieces += feed_rest + feed_far + from_core(feed_rest)
    near_pieces = [near_shard] + from_chips(near_shard, chips)
    flat_attended = attended.reshape(count, D)
    after_attn, active, slope, after_ffn = feed(
        place, layer_input.reshape(count, D), flat_attended, vec, feed_pieces
    )
    after_ffn, near_pieces = together(after_ffn, near_pieces)
    while len(states) < segments - 1:
        states.append(shift(states[-1], 1))
    near_pieces += from_core(near_pieces)
    output, row_grads, after_grad, gate_small, near_half, far_half = near(
        place, ids, near_rows, states[1:], after_ffn.reshape(batch, SEG, D), out_grad, vec,
        near_pieces,
    )

    near_arrived = swap(far_half, "fsdp", 1)
    (message,) = give(place, ids, row_grads, None, (segments - 1,))
    message, near_arrived, after_grad, row_grads = together(
        message, near_arrived, after_grad, row_grads
    )
    arrived = shift(message, -1)
    near_sums = core_sums(near_half, near_arrived)
    near_sums, after_grad = together(near_sums, after_grad)
    near_total = [near_sums[0]] + to_chips(near_sums, chips)
    grad_after, att_grad, feed_small, feed_half, feed_far = feed_back(
        place, after_grad.reshape(count, D), after_attn, active, slope, flat_attended, vec,
        feed_pieces,
    )
    feed_half, feed_far, att_grad, row_grads, arrived, near_total = together(
        feed_half, feed_far, att_grad, row_grads, arrived, near_total
    )
    near_low = chip_sum(near_total)
    feed_arrived = swap(feed_far, "fsdp", 1)
    near_pair = (near_low, swap(near_low, "seq", steps[0]))
    row_grads, near_low = together(row_grads, near_low)
    for distance in range(segments - 2, 1, -1):
        (message,) = give(place, ids, row_grads, arrived, (distance,))
        row_grads, message, feed_arrived = together(row_grads, message, feed_arrived)
        if distance > 2:
            arrived = shift(message, -1)
    feed_sums = core_sums(feed_half, feed_arrived)
    feed_total = [feed_sums[0]] + to_chips(feed_sums, chips)
    if segments > 3:
        message, row_grads, near_pair = together(message, row_grads, near_pair, feed_sums)[:3]
        arrived = shift(message, -1)
    sent, own = give(place, ids, row_grads, None, (1, 0))
    att_grad, sent = together(att_grad, sent)
    *pieces, first_diag = attend_back(
        joined, memory, att_grad.reshape(batch, SEG, D), attended, probs[0], 0, []
    )
    pieces, feed_total, arrived = together(pieces, feed_total, arrived)
    feed_low = chip_sum(feed_total)
    for step in steps[1:]:
        near_low = pair_sum(*near_pair)
        near_low, feed_low = together(near_low, feed_low)
        near_pair = (near_low, swap(near_low, "seq", step))
    kept, passed = halves(feed_low, steps[0])
    feed_pair = (kept, swap(passed, "seq", steps[0]))
    *pieces, last_diag = attend_back(
        joined, memory, att_grad.reshape(batch, SEG, D), attended, probs[1], PAIRS, pieces
    )
    pieces, feed_pair, near_pair = together(pieces, feed_pair, near_pair)
    for step in steps[1:]:
        kept, passed = halves(pair_sum(*feed_pair), step)
        feed_pair = (kept, swap(passed, "seq", step))
    partial, normed, normed_before, norm_small, *message = finish(
        layer_input, before, pieces, grad_after.reshape(batch, SEG, D), own, sent, arrived, vec,
        attn_w,
    )
    partial, message, norm_small, feed_pair = together(partial, message, norm_small, feed_pair)
    feed_low = pair_sum(*feed_pair)
    last = [shift(message[0], -1)]
    attn_half, attn_far = project_grad(
        place, devices, parts, normed, normed_before, pieces, norm_small, gate_small, feed_small,
        [first_diag, last_diag],
    )
    attn_half, attn_far, message, last, feed_low = together(
        attn_half, attn_far, message, last, feed_low
    )
    attn_arrived = swap(attn_far, "fsdp", 1)
    last += [shift(message[sequence], -1) for sequence in range(1, batch)]
    feed_pair = (feed_low, swap(feed_low, "seq", steps[-1]))
    attn_sums = core_sums(attn_half, attn_arrived)
    attn_total = [attn_sums[0]] + to_chips(attn_sums, chips)
    near_grads = unpack(place, (near_pair, ((1, D), (1, 2 * D), (1, D)), (), 0))
    near_grads, attn_total, last, feed_pair = together(near_grads, attn_total, last, feed_pair)
    attn_low = chip_sum(attn_total)
    for step in reversed(steps[:-1]):
        feed_low = joined_halves(*feed_pair, 2 * step)
        feed_pair = (feed_low, swap(feed_low, "seq", step))
    for step in steps[:-1]:
        attn_low = pair_sum(attn_low, swap(attn_low, "seq", step))
    attn_pair = (attn_low, swap(attn_low, "seq", steps[-1]))
    input_grad = partial + jnp.stack(last).astype(F32)
    attn_pair = together(attn_pair, input_grad)[0]
    widths = parts + [position_bias.shape[0]]
    project_out, *rest = unpack(
        place,
        (attn_pair, ((1, 3 * D),), widths, 0),
        (feed_pair, ((1, ff), (ratio, D), (1, D)), (), steps[0]),
    )
    smalls, feed_grads = rest[: len(widths)], rest[len(widths) :]
    return (
        output,
        input_grad,
        smalls[0],
        smalls[1],
        project_out,
        feed_grads[2],
        smalls[7],
        smalls[2],
        smalls[3],
        feed_grads[0],
        smalls[6],
        feed_grads[1],
        smalls[4],
        *near_grads,
        smalls[5],
    )


def solution(mesh):
    in_specs = (
        P("fsdp", "seq", None),
        P("fsdp", "seq", None),
        P("fsdp", "seq", None),
        P("fsdp"),
        P("fsdp"),
        P("fsdp", None),
        P("fsdp", None),
        P("fsdp"),
        P("fsdp"),
        P("fsdp"),
        P("fsdp", None),
        P("fsdp"),
        P("fsdp", None),
        P("fsdp"),
        P("fsdp", None),
        P("fsdp", None),
        P("fsdp", None),
        P("fsdp"),
    )
    out_specs = (
        P("fsdp", "seq", None),
        P("fsdp", "seq", None),
        P("fsdp"),
        P("fsdp"),
        P("fsdp", None),
        P("fsdp", None),
        P("fsdp"),
        P("fsdp"),
        P("fsdp"),
        P("fsdp", None),
        P("fsdp"),
        P("fsdp", None),
        P("fsdp"),
        P("fsdp", None),
        P("fsdp", None),
        P("fsdp", None),
        P("fsdp"),
    )
    return jax.shard_map(
        on_device, mesh=mesh, in_specs=in_specs, out_specs=out_specs, check_vma=False
    )
```

```python
import functools
import math

import jax
import jax.numpy as jnp
import numpy as np
from jax import lax
from jax.experimental import pallas as pl
from jax.experimental.pallas import tpu as pltpu
from jax.sharding import PartitionSpec as P

D = 512
H = 8
HD = 64
K = 4
SEG = 512
NB = 32

EPS = 1e-05
HIGH = lax.Precision.HIGHEST
MASKED = -1e30
F32 = jnp.float32
BF16 = jnp.bfloat16
ROWS = 256
SPAN = 2 * SEG + 128
VMEM = 56 << 20


def nn(left, right):
    return lax.dot_general(left, right, (((1,), (0,)), ((), ())), preferred_element_type=F32)


def nt(left, right):
    return lax.dot_general(left, right, (((1,), (1,)), ((), ())), preferred_element_type=F32)


def tn(left, right):
    return lax.dot_general(left, right, (((0,), (0,)), ((), ())), preferred_element_type=F32)


def shape(dims, dtype):
    return jax.ShapeDtypeStruct(tuple(dims), dtype)


def whole(dims):
    zeros = (0,) * len(dims)
    return pl.BlockSpec(tuple(dims), lambda *_: zeros, pipeline_mode=pl.Buffered(1))


def scalars():
    return pl.BlockSpec(memory_space=pltpu.SMEM)


def params(grid_rank):
    return pltpu.CompilerParams(
        dimension_semantics=("arbitrary",) * grid_rank, vmem_limit_bytes=VMEM
    )


def cost(flops, moved, exps=0):
    return pl.CostEstimate(
        flops=int(flops / 30), bytes_accessed=int(moved / 30), transcendentals=int(exps / 30)
    )


def thresholds():
    half_count = NB // 2
    spread_ratio = 2.0 * SEG / half_count
    exact_part = list(range(1, half_count))
    log_part = [
        int(half_count * spread_ratio ** ((bucket_index - half_count) / half_count))
        for bucket_index in range(half_count, NB)
    ]
    return np.array(exact_part + log_part)


def bucket_of(distance):
    return (distance[:, None] >= thresholds()[None, :]).sum(axis=1)


def forward_selector():
    distance = np.arange(SPAN) - 128
    bucket = bucket_of(np.maximum(distance, 0))
    return (np.arange(NB)[:, None] == bucket[None, :]).astype(np.float32)


def backward_selector():
    chosen = forward_selector().T.copy()
    chosen[:128] = 0.0
    return chosen


def norm(values):
    average = jnp.mean(values, axis=-1, keepdims=True)
    centred = values - average
    variance = jnp.mean(centred * centred, axis=-1, keepdims=True)
    rstd_value = lax.rsqrt(variance + EPS)
    return centred * rstd_value, rstd_value


def norm_back(grad_result, hat_value, rstd_value, gain):
    scaled = grad_result * gain
    return rstd_value * (
        scaled
        - jnp.mean(scaled, axis=-1, keepdims=True)
        - hat_value * jnp.mean(scaled * hat_value, axis=-1, keepdims=True)
    )


def rows_sum(values):
    return jnp.sum(values, axis=0, keepdims=True)


def pair_mask(head, values):
    lane = lax.broadcasted_iota(jnp.int32, values.shape, 1)
    keep = lane < HD if head == 0 else lane >= HD
    return jnp.where(keep, values, jnp.zeros_like(values))


def pack_first_kernel(*refs):
    weight_ref, *vector_refs, out_ref = refs
    rows = weight_ref.shape[0]
    out_ref[:rows, :] = weight_ref[...]
    out_ref[rows:, :] = jnp.zeros((16, out_ref.shape[1]), BF16)
    for index, ref in enumerate(vector_refs):
        line = ref[...].astype(F32).reshape(1, -1).astype(BF16)
        out_ref[rows + index : rows + index + 1, : ref.shape[0]] = line


def pack_first(weight, vectors):
    rows, columns = weight.shape
    return pl.pallas_call(
        pack_first_kernel,
        out_shape=shape((rows + 16, columns), BF16),
        cost_estimate=cost(0, 4 * rows * columns),
        name="pack_first",
    )(weight, *vectors)


def pack_kernel(rows, *refs):
    out_ref = refs[-1]
    start = 0
    for ref in refs[:-1]:
        for chunk in range(ref.shape[0] // rows):
            out_ref[:, start : start + ref.shape[1]] = ref[chunk * rows : (chunk + 1) * rows, :]
            start += ref.shape[1]


def pack(rows, weights):
    columns = sum(w.size for w in weights) // rows
    return pl.pallas_call(
        functools.partial(pack_kernel, rows),
        out_shape=shape((rows, columns), BF16),
        cost_estimate=cost(0, 4 * rows * columns),
        name="pack",
    )(*weights)


def unpack_kernel(layout, terms, bit, place_ref, *refs):
    total = [ref[...].astype(F32) for ref in refs[:terms]]
    if bit:
        high = jnp.bitwise_and(place_ref[1], bit) > 0
        mine, other = total
        total = jnp.concatenate(
            [jnp.where(high, other, mine), jnp.where(high, mine, other)], axis=1
        )
    else:
        total = functools.reduce(jnp.add, total)
    refs = refs[terms:]
    rows = refs[0].shape[0]
    start = 0
    for ref, (chunks, width) in zip(refs, layout):
        for chunk in range(chunks):
            ref[chunk * rows : (chunk + 1) * rows, :] = total[:rows, start : start + width]
            start += width
    for index, ref in enumerate(refs[len(layout) :]):
        ref[...] = total[rows + index : rows + index + 1, : ref.shape[0]].reshape(-1)


def unpack_both_kernel(jobs, place_ref, *refs):
    out_refs = refs[sum(terms for _, terms, _, _ in jobs) :]
    start = first_out = 0
    for layout, terms, bit, count in jobs:
        unpack_kernel(
            layout, terms, bit, place_ref, *refs[start : start + terms],
            *out_refs[first_out : first_out + count],
        )
        start += terms
        first_out += count


def unpack(place, *tasks):
    jobs = []
    arrays = []
    outs = []
    for pair, layout, widths, bit in tasks:
        rows = pair[0].shape[0] - (16 if widths else 0)
        part = [shape((rows * chunks, width), F32) for chunks, width in layout]
        part += [shape((width,), F32) for width in widths]
        jobs.append((layout, len(pair), bit, len(part)))
        arrays += pair
        outs += part
    return pl.pallas_call(
        functools.partial(unpack_both_kernel, jobs),
        in_specs=[scalars()] + [pl.BlockSpec(memory_space=pltpu.VMEM)] * len(arrays),
        out_shape=outs,
        compiler_params=pltpu.CompilerParams(vmem_limit_bytes=VMEM),
        cost_estimate=cost(0, sum(8 * array.size for array in arrays)),
        name="unpack",
    )(place, *arrays)


def device_of(place_ref, chip_step, core_step):
    index = place_ref[0]
    chip = lax.shift_right_logical(index, 1)
    core = jnp.bitwise_and(index, 1)
    return jnp.bitwise_xor(chip, chip_step) * 2 + jnp.bitwise_xor(core, core_step)


def assemble(place_ref, layout, piece_refs, out_refs):
    steps = len(piece_refs) // 2
    for core_step in range(2):
        for step in range(steps):
            ref = piece_refs[core_step * steps + step]
            owner = device_of(place_ref, step, core_step)
            rows = D // (2 * steps)
            start = 0
            for out_ref, (chunks, width) in zip(out_refs, layout):
                for chunk in range(chunks):
                    target = pl.multiple_of((owner * chunks + chunk) * rows, rows)
                    out_ref[pl.ds(target, rows), :] = ref[:rows, start : start + width]
                    start += width


def first_kernel(parts, count, place_ref, x_ref, select_ref, *refs):
    piece_refs = refs[:count]
    w_ref, vec_ref, line_ref, joined_ref, small_ref = refs[count:]

    @pl.when(pl.program_id(0) == 0)
    def _():
        assemble(place_ref, ((1, 3 * D),), piece_refs, [w_ref])
        steps = count // 2
        rows = D // count
        for core_step in range(2):
            for step in range(steps):
                owner = device_of(place_ref, step, core_step)
                small_ref[pl.ds(pl.multiple_of(owner * 16, 16), 16), :] = piece_refs[
                    core_step * steps + step
                ][rows:, : small_ref.shape[1]].astype(F32)
        vec_ref[...] = jnp.zeros_like(vec_ref)
        for row, width in enumerate(parts):
            pieces = [small_ref[16 * d + row : 16 * d + row + 1, :width] for d in range(count)]
            vec_ref[row : row + 1, : width * count] = jnp.concatenate(pieces, axis=1)
        row = len(parts)
        table = jnp.concatenate(
            [small_ref[16 * d + row : 16 * d + row + 1, : NB * H // count] for d in range(count)],
            axis=0,
        )
        by_distance = None
        for place in range(NB // count):
            part = lax.dot_general(
                table[:, place * H : (place + 1) * H],
                select_ref[place],
                (((0,), (0,)), ((), ())),
                precision=HIGH,
                preferred_element_type=F32,
            )
            by_distance = part if by_distance is None else by_distance + part
        lane = lax.broadcasted_iota(jnp.int32, by_distance.shape, 1)
        line_ref[...] = jnp.where(lane < 128, MASKED, by_distance)

    hat_value, _ = norm(x_ref[0].astype(F32))
    normed = (hat_value * vec_ref[0:1, :D] + vec_ref[1:2, :D]).astype(BF16)
    joined_ref[0] = nn(normed, w_ref[...]).astype(BF16)


def remember_kernel(x_ref, vec_ref, w_ref, out_ref):
    hat_value, _ = norm(x_ref[0].astype(F32))
    normed = (hat_value * vec_ref[0:1, :D] + vec_ref[1:2, :D]).astype(BF16)
    out_ref[0] = nn(normed, w_ref[:, D:]).astype(BF16)


def remember(before, vec, weight):
    batch = before.shape[0]

    def block(width):
        return pl.BlockSpec((1, SEG, width), lambda b: (b, 0, 0))

    return pl.pallas_call(
        remember_kernel,
        grid=(batch,),
        in_specs=[block(D), whole(vec.shape), whole(weight.shape)],
        out_specs=block(2 * D),
        out_shape=shape((batch, SEG, 2 * D), BF16),
        compiler_params=params(1),
        cost_estimate=cost(4 * batch * SEG * D * D, 6 * batch * SEG * D),
        name="remember",
    )(before, vec, weight)


def first(place, x, pieces, parts, ff):
    batch = x.shape[0]
    count = len(pieces)
    small_width = -(-max(parts) // 128) * 128
    select = forward_selector().reshape(count, NB // count, SPAN).transpose(1, 0, 2)

    def block(width):
        return pl.BlockSpec((1, SEG, width), lambda b: (b, 0, 0))

    return pl.pallas_call(
        functools.partial(first_kernel, parts, count),
        grid=(batch,),
        in_specs=[scalars(), block(D), whole(select.shape)]
        + [whole(piece.shape) for piece in pieces],
        out_specs=[whole((D, 3 * D)), whole((8, ff)), whole((H, SPAN)), block(3 * D)],
        out_shape=[
            shape((D, 3 * D), BF16),
            shape((8, ff), F32),
            shape((H, SPAN), F32),
            shape((batch, SEG, 3 * D), BF16),
        ],
        scratch_shapes=[pltpu.VMEM((16 * count, small_width), F32)],
        compiler_params=params(1),
        cost_estimate=cost(6 * batch * SEG * D * D, 8 * batch * SEG * D),
        name="first",
    )(place, x, jnp.asarray(select), *pieces)


def tiles(place_ref, line_ref, first, own_ref, mem_ref):
    hidden = jnp.where(place_ref[1] > 0, 0.0, MASKED)
    for head in range(2):
        index = 2 * (first + pl.program_id(0)) + head
        line = jnp.broadcast_to(line_ref[pl.ds(index, 1), :], (8, SPAN))
        line = pltpu.roll(line, 0, 1, stride=1, stride_axis=0)
        for group in range(16):
            moved = pltpu.roll(line, 8 * group, 1) if group else line
            for tile in range(2 * SEG // 128):
                start = 2 * SEG - 128 * tile
                row = 128 * tile + 8 * group
                piece = moved[:, start : start + 128]
                own_ref[head, row : row + 8, :] = piece
                mem_ref[head, row : row + 8, :] = piece + hidden


def attend_kernel(first, place_ref, q_ref, k_ref, v_ref, km_ref, vm_ref, line_ref, *refs):
    out_ref, prob_ref, own_ref, mem_ref = refs[-4:]

    @pl.when(pl.program_id(1) == 0)
    def _():
        tiles(place_ref, line_ref, first, own_ref, mem_ref)

    keys = jnp.concatenate([km_ref[0], k_ref[0]], axis=0)
    values = jnp.concatenate([vm_ref[0], v_ref[0]], axis=0)
    for half in range(SEG // ROWS):
        width = SEG + (half + 1) * ROWS
        span = slice(half * ROWS, (half + 1) * ROWS)
        query = q_ref[0, span, :] * BF16(HD**-0.5)
        total = None
        for head in range(2):
            scores = nt(keys[:width], pair_mask(head, query))
            columns = []
            for part in range(ROWS // 128):
                block = half * (ROWS // 128) + part
                bias = jnp.concatenate(
                    [
                        mem_ref[head, (3 - block) * 128 : (7 - block) * 128, :],
                        own_ref[head, (7 - block) * 128 :, :],
                    ],
                    axis=0,
                )
                used = bias.shape[0]
                piece = scores[:used, part * 128 : (part + 1) * 128] + bias
                top = jnp.max(piece, axis=0, keepdims=True)
                weight = jnp.exp(piece - top)
                weight = (weight * (1.0 / jnp.sum(weight, axis=0, keepdims=True))).astype(BF16)
                if used < width:
                    weight = jnp.concatenate(
                        [weight, jnp.zeros((width - used, 128), BF16)], axis=0
                    )
                columns.append(weight)
            probs = jnp.concatenate(columns, axis=1)
            prob_ref[0, head, :width, span] = probs
            product = tn(probs, pair_mask(head, values)[:width])
            total = product if total is None else total + product
        out_ref[0, span, :] = total.astype(BF16)


PAIRS = H // 4


def attend(place, joined, memory, line, first, so_far):
    batch = joined.shape[0]

    def lanes(offset):
        return pl.BlockSpec((1, SEG, 128), lambda h, b: (b, 0, offset + first + h))

    work = batch * H * SEG * SEG
    extra = [] if so_far is None else [so_far]
    return pl.pallas_call(
        functools.partial(attend_kernel, first),
        grid=(PAIRS, batch),
        in_specs=[scalars()]
        + [lanes(0), lanes(2 * PAIRS), lanes(4 * PAIRS), lanes(0), lanes(2 * PAIRS)]
        + [whole(line.shape)]
        + [pl.BlockSpec(memory_space=pl.ANY)] * len(extra),
        out_specs=[
            lanes(0),
            pl.BlockSpec((1, 2, 2 * SEG, SEG), lambda h, b: (b, h, 0, 0)),
        ],
        out_shape=[shape((batch, SEG, D), BF16), shape((batch, H // 2, 2 * SEG, SEG), BF16)],
        scratch_shapes=[pltpu.VMEM((2, 2 * SEG, 128), F32)] * 2,
        input_output_aliases={7: 0} if extra else {},
        compiler_params=params(2),
        cost_estimate=cost(16 * HD * work, 3 * work, work),
        name="attend",
    )(place, joined, joined, joined, memory, memory, line, *extra)


def attend_back_kernel(
    q_ref, k_ref, v_ref, km_ref, vm_ref, grad_ref, out_ref, prob_ref, *refs
):
    dq_ref, dk_ref, dv_ref, dkm_ref, dvm_ref, diag_ref, grid_ref = refs[-7:]
    keys = jnp.concatenate([km_ref[0], k_ref[0]], axis=0)
    values = jnp.concatenate([vm_ref[0], v_ref[0]], axis=0)
    step = pl.program_id(1)

    @pl.when(step == 0)
    def _():
        grid_ref[...] = jnp.zeros_like(grid_ref)

    key_parts = []
    value_parts = []
    for half in range(SEG // ROWS):
        width = SEG + (half + 1) * ROWS
        span = slice(half * ROWS, (half + 1) * ROWS)
        grad = grad_ref[0, span, :]
        query = q_ref[0, span, :] * BF16(HD**-0.5)
        product = (grad.astype(F32) * out_ref[0, span, :].astype(F32)).T
        query_total = key_total = value_total = None
        for head in range(2):
            grad_head = pair_mask(head, grad)
            delta = jnp.sum(product[head * HD : (head + 1) * HD], axis=0, keepdims=True)
            probs = prob_ref[0, head, :width, span]
            scored = probs.astype(F32) * (nt(values[:width], grad_head) - delta)
            for part in range(ROWS // 128):
                block = half * (ROWS // 128) + part
                used = SEG + (block + 1) * 128
                grid_ref[head, (3 - block) * 128 :, :] += scored[
                    :used, part * 128 : (part + 1) * 128
                ]
            scored = scored.astype(BF16)
            for_key = nn(scored, pair_mask(head, query))
            for_value = nn(probs, grad_head)
            for_query = tn(scored, pair_mask(head, keys)[:width])
            key_total = for_key if key_total is None else key_total + for_key
            value_total = for_value if value_total is None else value_total + for_value
            query_total = for_query if query_total is None else query_total + for_query
        dq_ref[0, span, :] = (query_total * HD**-0.5).astype(BF16)
        key_parts.append(key_total)
        value_parts.append(value_total)
    for pieces, mem_ref, own_ref in (
        (key_parts, dkm_ref, dk_ref),
        (value_parts, dvm_ref, dv_ref),
    ):
        both = pieces[0] + pieces[1][: SEG + ROWS]
        mem_ref[0] = both[:SEG].astype(BF16)
        own_ref[0, :ROWS] = both[SEG:].astype(BF16)
        own_ref[0, ROWS:] = pieces[1][SEG + ROWS :].astype(BF16)

    @pl.when(step == pl.num_programs(1) - 1)
    def _():
        for head in range(2):
            total = None
            for group in range(16):
                pieces = [
                    grid_ref[head, 128 * tile + 8 * group : 128 * tile + 8 * group + 8, :]
                    for tile in reversed(range(2 * SEG // 128))
                ]
                line = jnp.concatenate([jnp.zeros((8, 128), F32)] + pieces, axis=1)
                if group:
                    line = pltpu.roll(line, SPAN - 8 * group, 1)
                total = line if total is None else total + line
            lines = [total[:1]] + [
                pltpu.roll(total[row : row + 1], SPAN - row, 1) for row in range(1, 8)
            ]
            diag_ref[0, head : head + 1, :] = functools.reduce(jnp.add, lines)


def attend_back(joined, memory, grad, attended, probs, first, so_far):
    batch = joined.shape[0]

    def lanes(offset):
        return pl.BlockSpec((1, SEG, 128), lambda h, b: (b, 0, offset + first + h))

    half = shape((batch, SEG, D), BF16)
    work = batch * H * SEG * SEG
    return pl.pallas_call(
        attend_back_kernel,
        grid=(PAIRS, batch),
        in_specs=[lanes(0), lanes(2 * PAIRS), lanes(4 * PAIRS), lanes(0), lanes(2 * PAIRS)]
        + [lanes(0)] * 2
        + [pl.BlockSpec((1, 2, 2 * SEG, SEG), lambda h, b: (b, h, 0, 0))]
        + [pl.BlockSpec(memory_space=pl.ANY)] * len(so_far),
        out_specs=[lanes(0)] * 5 + [pl.BlockSpec((1, 2, SPAN), lambda h, b: (h, 0, 0))],
        out_shape=[half] * 5 + [shape((PAIRS, 2, SPAN), F32)],
        scratch_shapes=[pltpu.VMEM((2, 2 * SEG, 128), F32)],
        input_output_aliases={8 + i: i for i in range(len(so_far))},
        compiler_params=params(2),
        cost_estimate=cost(32 * HD * work, 3 * work),
        name="attend_back",
    )(joined, joined, joined, memory, memory, grad, attended, probs, *so_far)


def feed_layout(ff):
    return ((1, D), (1, ff), (ff // D, D))


def feed_scratch(ff):
    return [pltpu.VMEM((D, D), BF16), pltpu.VMEM((D, ff), BF16), pltpu.VMEM((ff, D), BF16)]


def feed_kernel(count, place_ref, x_ref, att_ref, vec_ref, *refs):
    piece_refs = refs[:count]
    (
        after_attn_ref, active_ref, slope_ref, after_ffn_ref, merge_ref, expand_ref, reduce_ref,
    ) = refs[count:]

    @pl.when(pl.program_id(0) == 0)
    def _():
        assemble(place_ref, feed_layout(expand_ref.shape[1]), piece_refs, refs[-3:])

    after_attn = x_ref[...].astype(F32) + nn(att_ref[...], merge_ref[...])
    after_attn_ref[...] = after_attn
    hat_value, _ = norm(after_attn)
    normed = (hat_value * vec_ref[2:3, :D] + vec_ref[3:4, :D]).astype(BF16)
    pre = nn(normed, expand_ref[...]) + vec_ref[6:7, :]
    cdf = 0.5 * (1.0 + lax.erf(pre * (1.0 / math.sqrt(2.0))))
    slope = cdf + pre * jnp.exp(-0.5 * pre * pre) * (1.0 / math.sqrt(2.0 * math.pi))
    slope_ref[...] = slope.astype(BF16)
    active = (pre * cdf).astype(BF16)
    active_ref[...] = active
    after_ffn = after_attn + nn(active, reduce_ref[...]) + vec_ref[4:5, :D]
    after_ffn_ref[...] = after_ffn


def feed(place, x, attended, vec, pieces):
    count = x.shape[0]
    ff = vec.shape[1]

    def rows(width):
        return pl.BlockSpec((ROWS, width), lambda i: (i, 0))

    return pl.pallas_call(
        functools.partial(feed_kernel, len(pieces)),
        grid=(count // ROWS,),
        in_specs=[scalars(), rows(D), rows(D), whole(vec.shape)]
        + [whole(piece.shape) for piece in pieces],
        out_specs=[rows(D), rows(ff), rows(ff), rows(D)],
        out_shape=[
            shape((count, D), F32),
            shape((count, ff), BF16),
            shape((count, ff), BF16),
            shape((count, D), F32),
        ],
        scratch_shapes=feed_scratch(ff),
        compiler_params=params(1),
        cost_estimate=cost(4 * count * D * (ff + D), 12 * count * ff, 2 * count * ff),
        name="feed",
    )(place, x, attended, vec, *pieces)


def add_rows(ref, row, values):
    ref[row : row + 1, : values.shape[1]] += values


def scatter_rows(place_ref, total_ref, near_ref, far_ref, start, chunks):
    steps, rows = near_ref.shape[0], near_ref.shape[1]
    width = total_ref.shape[1]
    for core_step, ref in ((0, near_ref), (1, far_ref)):
        for step in range(steps):
            owner = device_of(place_ref, step, core_step)
            for chunk in range(chunks):
                source = pl.multiple_of((owner * chunks + chunk) * rows, rows)
                column = start + chunk * width
                ref[step, :, column : column + width] = total_ref[
                    pl.ds(source, rows), :
                ].astype(BF16)
    return start + chunks * width


def feed_back_kernel(
    count, place_ref, grad_ref, after_ref, active_ref, slope_ref, att_ref, vec_ref, *refs
):
    piece_refs = refs[:count]
    (
        after_grad_ref, att_grad_ref, small_ref, near_ref, far_ref,
        expand_total, reduce_total, merge_total, merge_ref, expand_ref, reduce_ref,
    ) = refs[count:]
    step = pl.program_id(0)

    @pl.when(step == 0)
    def _():
        assemble(place_ref, feed_layout(expand_ref.shape[1]), piece_refs, refs[-3:])
        expand_total[...] = jnp.zeros_like(expand_total)
        merge_total[...] = jnp.zeros_like(merge_total)
        reduce_total[...] = jnp.zeros_like(reduce_total)
        small_ref[...] = jnp.zeros_like(small_ref)

    grad = grad_ref[...]
    low = grad.astype(BF16)
    add_rows(small_ref, 2, rows_sum(low.astype(F32)))
    reduce_total[...] += tn(active_ref[...], low)
    pre_grad = (nt(low, reduce_ref[...]) * slope_ref[...].astype(F32)).astype(BF16)
    add_rows(small_ref, 3, rows_sum(pre_grad.astype(F32)))
    hat_value, rstd_value = norm(after_ref[...])
    gain = vec_ref[2:3, :D]
    normed = (hat_value * gain + vec_ref[3:4, :D]).astype(BF16)
    expand_total[...] += tn(normed, pre_grad)
    normed_grad = nt(pre_grad, expand_ref[...])
    add_rows(small_ref, 0, rows_sum(normed_grad * hat_value))
    add_rows(small_ref, 1, rows_sum(normed_grad))
    after_grad = grad + norm_back(normed_grad, hat_value, rstd_value, gain)
    after_grad_ref[...] = after_grad
    merge_grad = after_grad.astype(BF16)
    merge_total[...] += tn(att_ref[...], merge_grad)
    att_grad_ref[...] = nt(merge_grad, merge_ref[...]).astype(BF16)

    @pl.when(step == pl.num_programs(0) - 1)
    def _():
        start = scatter_rows(place_ref, expand_total, near_ref, far_ref, 0, 1)
        ratio = reduce_total.shape[0] // D
        start = scatter_rows(place_ref, reduce_total, near_ref, far_ref, start, ratio)
        scatter_rows(place_ref, merge_total, near_ref, far_ref, start, 1)


def feed_back(place, grad, after_attn, active, slope, attended, vec, pieces):
    count = grad.shape[0]
    ff = vec.shape[1]
    devices = len(pieces)

    def rows(width):
        return pl.BlockSpec((ROWS, width), lambda i: (i, 0))

    packed = (devices // 2, D // devices, 2 * ff + D)
    return pl.pallas_call(
        functools.partial(feed_back_kernel, devices),
        grid=(count // ROWS,),
        in_specs=[scalars(), rows(D), rows(D), rows(ff), rows(ff), rows(D), whole(vec.shape)]
        + [whole(piece.shape) for piece in pieces],
        out_specs=[rows(D), rows(D), whole((8, ff)), whole(packed), whole(packed)],
        out_shape=[
            shape((count, D), F32),
            shape((count, D), BF16),
            shape((8, ff), F32),
            shape(packed, BF16),
            shape(packed, BF16),
        ],
        scratch_shapes=[
            pltpu.VMEM((D, ff), F32),
            pltpu.VMEM((ff, D), F32),
            pltpu.VMEM((D, D), F32),
        ]
        + feed_scratch(ff),
        compiler_params=params(1),
        cost_estimate=cost(8 * count * D * (ff + D // 2), 12 * count * ff),
        name="feed_back",
    )(place, grad, after_attn, active, slope, attended, vec, *pieces)


def chosen_rows(ids, slot, rows):
    place = lax.broadcasted_iota(jnp.int32, (ids.shape[0], SEG), 1)
    return nn(jnp.where(ids[:, slot : slot + 1] == place, 1.0, 0.0).astype(BF16), rows)


def ids_down(ids):
    return jnp.concatenate([ids] * 2, axis=0).T


def take_kernel(distance, started, place_ref, ids_ref, rows_ref, *refs):
    out_ref = refs[-1]
    ids = ids_down(ids_ref[0] - (place_ref[1] - distance) * SEG)
    rows = rows_ref[0]
    for slot in range(K):
        taken = chosen_rows(ids, slot, rows).astype(BF16)
        out_ref[0, slot] = refs[0][0, slot] + taken if started else taken


def take(place, ids, rows, distance, so_far):
    batch = ids.shape[0]
    block = pl.BlockSpec((1, K, SEG, D), lambda b: (b, 0, 0, 0))
    return pl.pallas_call(
        functools.partial(take_kernel, distance, len(so_far)),
        grid=(batch,),
        in_specs=[
            scalars(),
            pl.BlockSpec((1, K, SEG), lambda b: (b, 0, 0)),
            pl.BlockSpec((1, SEG, D), lambda b: (b, 0, 0)),
        ]
        + [block] * len(so_far),
        out_specs=block,
        out_shape=shape((batch, K, SEG, D), BF16),
        input_output_aliases={3: 0} if so_far else {},
        compiler_params=params(1),
        cost_estimate=cost(2 * batch * K * SEG * SEG * D, 4 * batch * K * SEG * D),
        name="take",
    )(place, ids, rows, *so_far)


def give_kernel(distances, started, place_ref, ids_ref, grad_ref, *refs):
    out_refs = refs[started:]
    place = lax.broadcasted_iota(jnp.int32, (SEG, SEG), 0)
    for index, distance in enumerate(distances):
        ids = ids_ref[0] - (place_ref[1] - distance) * SEG
        total = None
        for slot in range(K):
            chosen = jnp.where(ids[slot : slot + 1, :] == place, 1.0, 0.0).astype(BF16)
            part = nn(chosen, grad_ref[0, slot])
            total = part if total is None else total + part
        if started and index == 0:
            total = total + refs[0][0].astype(F32)
        out_refs[index][0] = total.astype(out_refs[index].dtype)


def give(place, ids, grads, arrived, distances):
    batch = ids.shape[0]
    block = pl.BlockSpec((1, SEG, D), lambda b: (b, 0, 0))
    started = arrived is not None
    work = len(distances) * batch * K * SEG * D
    return pl.pallas_call(
        functools.partial(give_kernel, distances, started),
        grid=(batch,),
        in_specs=[
            scalars(),
            pl.BlockSpec((1, K, SEG), lambda b: (b, 0, 0)),
            pl.BlockSpec((1, K, SEG, D), lambda b: (b, 0, 0, 0)),
        ]
        + [block] * started,
        out_specs=[block] * len(distances),
        out_shape=[shape((batch, SEG, D), BF16 if d else F32) for d in distances],
        compiler_params=params(1),
        cost_estimate=cost(2 * work * SEG, 2 * work),
        name="give",
    )(place, ids, grads, *([arrived] if started else []))


def near_kernel(
    hops, count, place_ref, ids_ref, rows_ref, after_ref, grad_ref, vec_ref, *refs
):
    state_refs = refs[:hops]
    piece_refs = refs[hops : hops + count]
    (
        out_ref, row_grad_ref, after_grad_ref, small_ref, near_ref, far_ref,
        keys_total, merge_total, query_total, nq_ref, keys_ref, merge_ref,
    ) = refs[hops + count :]
    first = (pl.program_id(0) == 0) & (pl.program_id(1) == 0)
    last = (pl.program_id(0) == pl.num_programs(0) - 1) & (
        pl.program_id(1) == pl.num_programs(1) - 1
    )

    @pl.when(first)
    def _():
        keys_total[...] = jnp.zeros_like(keys_total)
        merge_total[...] = jnp.zeros_like(merge_total)
        query_total[...] = jnp.zeros_like(query_total)
        assemble(place_ref, ((1, D), (1, 2 * D), (1, D)), piece_refs, refs[-3:])
        small_ref[...] = jnp.zeros_like(small_ref)

    scale = HD**-0.5
    place = lax.broadcasted_iota(jnp.int32, (K * D, 128), 0)
    lane = lax.broadcasted_iota(jnp.int32, (K * D, 128), 1)
    group = lax.shift_right_logical(place, 9) * H + jnp.bitwise_and(
        lax.shift_right_logical(place, 6), H - 1
    )
    gather = jnp.where(jnp.bitwise_and(lane, K * H - 1) == group, 1.0, 0.0).astype(BF16)
    lane = lax.broadcasted_iota(jnp.int32, (128, K * D), 0)
    place = lax.broadcasted_iota(jnp.int32, (128, K * D), 1)
    group = lax.shift_right_logical(place, 9) * H + jnp.bitwise_and(
        lax.shift_right_logical(place, 6), H - 1
    )
    spread = jnp.where(
        (jnp.bitwise_and(lane, K * H - 1) == group) & (lane < 2 * K * H), 1.0, 0.0
    ).astype(BF16)

    def over_slots(combine, values):
        values = combine(values, pltpu.roll(values, 2 * H, 1))
        return combine(values, pltpu.roll(values, H, 1))

    def to_rows(values):
        high = values.astype(BF16)
        low = (values - high.astype(F32)).astype(BF16)
        lane = lax.broadcasted_iota(jnp.int32, values.shape, 1)
        return nn(jnp.where(lane < K * H, high, low), spread)

    def slot_of(values, slot):
        return values[:, slot * D : (slot + 1) * D]

    after_ffn = after_ref[0]
    hidden_low = after_ffn.astype(BF16)
    query = nn(hidden_low, nq_ref[...]).astype(BF16)
    query_float = query.astype(F32)
    ids = ids_down(ids_ref[0])
    states = jnp.concatenate([ref[0] for ref in state_refs], axis=0) if hops else None
    taken = []
    for slot in range(K):
        total = rows_ref[0, slot]
        if hops:
            chosen = []
            for hop in range(hops):
                column = ids[:, slot : slot + 1] - (place_ref[1] - hop - 2) * SEG
                here = lax.broadcasted_iota(jnp.int32, (ids.shape[0], SEG), 1)
                chosen.append(jnp.where(column == here, 1.0, 0.0).astype(BF16))
            moved = nn(jnp.concatenate(chosen, axis=1), states)
            total = total + moved.astype(BF16)
        taken.append(total)
    pairs = [nn(rows, keys_ref[...]).astype(BF16) for rows in taken]
    near_key = [pair[:, :D] for pair in pairs]
    near_value = [pair[:, D:] for pair in pairs]
    products = jnp.concatenate([query * key for key in near_key], axis=1)
    scores = nn(products, gather) * scale
    weights = jnp.exp(scores - over_slots(jnp.maximum, scores))
    probs = weights / over_slots(jnp.add, weights)
    prob_rows = to_rows(probs)
    mixed = functools.reduce(
        jnp.add, [slot_of(prob_rows, i) * v.astype(F32) for i, v in enumerate(near_value)]
    ).astype(BF16)
    near_out = nn(mixed, merge_ref[...])
    gate_vector = vec_ref[5:6, :D]
    gate = jax.nn.sigmoid(jnp.sum(after_ffn * gate_vector, axis=-1, keepdims=True))
    out_ref[0] = (gate * after_ffn + (1.0 - gate) * near_out).astype(BF16)
    grad = grad_ref[0].astype(F32)
    gate_grad = (
        jnp.sum(grad * (after_ffn - near_out), axis=-1, keepdims=True) * gate * (1.0 - gate)
    )
    add_rows(small_ref, 0, rows_sum(gate_grad * after_ffn))
    near_grad = ((1.0 - gate) * grad).astype(BF16)
    merge_total[...] += tn(mixed, near_grad)
    mixed_low = nt(near_grad, merge_ref[...]).astype(BF16)
    mixed_grad = mixed_low.astype(F32)
    products = jnp.concatenate([mixed_low * value for value in near_value], axis=1)
    prob_grads = nn(products, gather)
    inner = over_slots(jnp.add, probs * prob_grads)
    score_rows = to_rows(probs * (prob_grads - inner) * scale)
    query_grad = None
    for slot in range(K):
        score_grad = slot_of(score_rows, slot)
        part = score_grad * near_key[slot].astype(F32)
        query_grad = part if query_grad is None else query_grad + part
        pair_grad = jnp.concatenate(
            [
                (score_grad * query_float).astype(BF16),
                (slot_of(prob_rows, slot) * mixed_grad).astype(BF16),
            ],
            axis=1,
        )
        keys_total[...] += tn(taken[slot], pair_grad)
        row_grad_ref[0, slot] = nt(pair_grad, keys_ref[...]).astype(BF16)
    query_grad = query_grad.astype(BF16)
    query_total[...] += tn(hidden_low, query_grad)
    after_grad_ref[0] = gate * grad + gate_grad * gate_vector + nt(query_grad, nq_ref[...])

    @pl.when(last)
    def _():
        start = scatter_rows(place_ref, query_total, near_ref, far_ref, 0, 1)
        start = scatter_rows(place_ref, keys_total, near_ref, far_ref, start, 1)
        scatter_rows(place_ref, merge_total, near_ref, far_ref, start, 1)


def near(place, ids, rows, states, after_ffn, grad, vec, pieces):
    batch = rows.shape[0]
    devices = len(pieces)
    row_block = pl.BlockSpec((1, K, ROWS, D), lambda b, i: (b, 0, i, 0))
    block = pl.BlockSpec((1, ROWS, D), lambda b, i: (b, i, 0))
    packed = (devices // 2, D // devices, 4 * D)
    count = batch * SEG
    return pl.pallas_call(
        functools.partial(near_kernel, len(states), devices),
        grid=(batch, SEG // ROWS),
        in_specs=[scalars(), pl.BlockSpec((1, K, ROWS), lambda b, i: (b, 0, i))]
        + [row_block, block, block, whole(vec.shape)]
        + [pl.BlockSpec((1, SEG, D), lambda b, i: (b, 0, 0))] * len(states)
        + [whole(piece.shape) for piece in pieces],
        out_specs=[block, row_block, block, whole((8, D)), whole(packed), whole(packed)],
        out_shape=[
            shape((batch, SEG, D), BF16),
            shape((batch, K, SEG, D), BF16),
            shape((batch, SEG, D), F32),
            shape((8, D), F32),
            shape(packed, BF16),
            shape(packed, BF16),
        ],
        scratch_shapes=[
            pltpu.VMEM((D, 2 * D), F32),
            pltpu.VMEM((D, D), F32),
            pltpu.VMEM((D, D), F32),
            pltpu.VMEM((D, D), BF16),
            pltpu.VMEM((D, 2 * D), BF16),
            pltpu.VMEM((D, D), BF16),
        ],
        compiler_params=params(2),
        cost_estimate=cost(
            2 * count * D * D * (11 * K + 6), count * D * (4 * K + 12), count * K * D
        ),
        name="near",
    )(place, ids, rows, after_ffn, grad, vec, *states, *pieces)


def finish_kernel(
    x_ref, before_ref, dq_ref, dk_ref, dv_ref, dkm_ref, dvm_ref, grad_ref, own_ref, sent_ref,
    arrived_ref, vec_ref, w_ref,
    part_ref, normed_ref, normed_before_ref, small_ref, *send_refs,
):
    @pl.when(pl.program_id(0) == 0)
    def _():
        small_ref[...] = jnp.zeros_like(small_ref)

    gain = vec_ref[0:1, :D]
    shift_by = vec_ref[1:2, :D]
    hat_before, rstd_before = norm(before_ref[0].astype(F32))
    normed_before_ref[0] = (hat_before * gain + shift_by).astype(BF16)
    before_grad = nt(dkm_ref[0], w_ref[:, D : 2 * D]) + nt(dvm_ref[0], w_ref[:, 2 * D :])
    send = (
        sent_ref[0].astype(F32)
        + arrived_ref[0].astype(F32)
        + norm_back(before_grad, hat_before, rstd_before, gain)
    ).astype(BF16)
    for sequence, send_ref in enumerate(send_refs):

        @pl.when(pl.program_id(0) == sequence)
        def _():
            send_ref[...] = send

    hat_value, rstd_value = norm(x_ref[0].astype(F32))
    normed_ref[0] = (hat_value * gain + shift_by).astype(BF16)
    normed_grad = (
        nt(dq_ref[0], w_ref[:, :D])
        + nt(dk_ref[0], w_ref[:, D : 2 * D])
        + nt(dv_ref[0], w_ref[:, 2 * D :])
    )
    add_rows(small_ref, 0, rows_sum(normed_grad * hat_value) + rows_sum(before_grad * hat_before))
    add_rows(small_ref, 1, rows_sum(normed_grad) + rows_sum(before_grad))
    part_ref[0] = (
        grad_ref[0] + own_ref[0] + norm_back(normed_grad, hat_value, rstd_value, gain)
    )


def finish(x, before, pieces, grad, own, sent, arrived, vec, weight):
    batch = x.shape[0]
    block = pl.BlockSpec((1, SEG, D), lambda b: (b, 0, 0))
    low = shape((batch, SEG, D), BF16)
    return pl.pallas_call(
        finish_kernel,
        grid=(batch,),
        in_specs=[block] * 11 + [whole(w.shape) for w in (vec, weight)],
        out_specs=[block] * 3 + [whole((8, D))] + [whole((SEG, D))] * batch,
        out_shape=[shape((batch, SEG, D), F32), low, low, shape((8, D), F32)]
        + [shape((SEG, D), BF16)] * batch,
        compiler_params=params(1),
        cost_estimate=cost(10 * batch * SEG * D * D, 34 * batch * SEG * D),
        name="finish",
    )(x, before, *pieces, grad, own, sent, arrived, vec, weight)


def project_grad_kernel(
    parts, place_ref, normed_ref, normed_before_ref, dq_ref, dk_ref, dv_ref, dkm_ref, dvm_ref,
    norm_ref, gate_ref, feed_ref, select_ref, first_ref, last_ref,
    near_ref, far_ref, w_total, small_total,
):
    step = pl.program_id(0)

    @pl.when(step == 0)
    def _():
        w_total[...] = jnp.zeros_like(w_total)

    normed = normed_ref[0]
    normed_before = normed_before_ref[0]
    w_total[:, :D] += tn(normed, dq_ref[0])
    w_total[:, D : 2 * D] += tn(normed, dk_ref[0]) + tn(normed_before, dkm_ref[0])
    w_total[:, 2 * D :] += tn(normed, dv_ref[0]) + tn(normed_before, dvm_ref[0])

    @pl.when(step == pl.num_programs(0) - 1)
    def _():
        devices = small_total.shape[0] // 16
        rows = w_total.shape[0] // devices
        small_total[...] = jnp.zeros_like(small_total)
        lines = [
            norm_ref[0:1, :],
            norm_ref[1:2, :],
            feed_ref[0:1, :D],
            feed_ref[1:2, :D],
            feed_ref[2:3, :D],
            gate_ref[0:1, :],
            feed_ref[3:4, :],
        ]
        for index, (line, width) in enumerate(zip(lines, parts)):
            for d in range(devices):
                row = 16 * d + index
                small_total[row : row + 1, :width] = line[:, d * width : (d + 1) * width]
        table = lax.dot_general(
            jnp.concatenate([ref[i] for ref in (first_ref, last_ref) for i in range(PAIRS)], axis=0),
            select_ref[...],
            (((1,), (0,)), ((), ())),
            precision=HIGH,
            preferred_element_type=F32,
        )
        own_buckets = NB // devices
        bucket = lax.broadcasted_iota(jnp.int32, (devices, NB), 1)
        owner = lax.broadcasted_iota(jnp.int32, (devices, NB), 0)
        pieces = []
        for place in range(own_buckets):
            chosen = jnp.where(bucket == owner * own_buckets + place, 1.0, 0.0)
            pieces.append(
                lax.dot_general(
                    chosen,
                    table,
                    (((1,), (1,)), ((), ())),
                    precision=HIGH,
                    preferred_element_type=F32,
                )
            )
        buckets = jnp.concatenate(pieces, axis=1)
        for d in range(devices):
            row = 16 * d + len(parts)
            small_total[row : row + 1, : buckets.shape[1]] = buckets[d : d + 1, :]
        width = small_total.shape[1]
        for core_step, ref in ((0, near_ref), (1, far_ref)):
            for chip_step in range(ref.shape[0]):
                target = device_of(place_ref, chip_step, core_step)
                source = pl.multiple_of(target * rows, rows)
                ref[chip_step, :rows, :] = w_total[pl.ds(source, rows), :].astype(BF16)
                ref[chip_step, rows:, :] = jnp.zeros((16, ref.shape[2]), BF16)
                lines = small_total[pl.ds(pl.multiple_of(target * 16, 16), 16), :]
                ref[chip_step, rows:, :width] = lines.astype(BF16)


def project_grad(place, devices, parts, normed, normed_before, pieces, norm_small, gate, feed_small, diags):
    batch = normed.shape[0]
    block = pl.BlockSpec((1, SEG, D), lambda b: (b, 0, 0))
    packed = (devices // 2, D // devices + 16, 3 * D)
    select = jnp.asarray(backward_selector())
    small_width = -(-max(parts) // 128) * 128
    return pl.pallas_call(
        functools.partial(project_grad_kernel, parts),
        grid=(batch,),
        in_specs=[scalars()]
        + [block] * 7
        + [whole(w.shape) for w in (norm_small, gate, feed_small, select, *diags)],
        out_specs=[whole(packed)] * 2,
        out_shape=[shape(packed, BF16)] * 2,
        scratch_shapes=[
            pltpu.VMEM((D, 3 * D), F32),
            pltpu.VMEM((16 * devices, small_width), F32),
        ],
        compiler_params=params(1),
        cost_estimate=cost(10 * batch * SEG * D * D, 20 * batch * SEG * D),
        name="project_grad",
    )(
        place, normed, normed_before, *pieces, norm_small, gate, feed_small, select, *diags,
    )


def shift(block, distance):
    count = lax.axis_size("seq")
    return lax.ppermute(block, "seq", [(i, (i + distance) % count) for i in range(count)])


def swap(block, axis, bits):
    count = lax.axis_size(axis)
    return lax.ppermute(block, axis, [(i, i ^ bits) for i in range(count)])


def together(*values):
    return lax.optimization_barrier(values)


def chip_steps():
    steps = list(range(1, lax.axis_size("fsdp") // 2))
    cut = (2 * len(steps) + 2) // 3
    return steps[:cut], steps[cut:]


def from_chips(shard, steps):
    return [swap(shard, "fsdp", 2 * step) for step in steps]


def from_core(pieces):
    return [swap(piece, "fsdp", 1) for piece in pieces]


def core_sums(near_half, arrived):
    return [
        (near_half[step].astype(F32) + arrived[step].astype(F32)).astype(BF16)
        for step in range(near_half.shape[0])
    ]


def to_chips(pieces, steps):
    return [swap(pieces[step], "fsdp", 2 * step) for step in steps]


def chip_sum(pieces):
    return functools.reduce(jnp.add, [piece.astype(F32) for piece in pieces]).astype(BF16)


def segment_steps():
    return [1 << bit for bit in range(lax.axis_size("seq").bit_length() - 1)]


def halves(values, bit):
    half = values.shape[1] // 2
    high = jnp.bitwise_and(lax.axis_index("seq"), bit) > 0
    left, right = values[:, :half], values[:, half:]
    return jnp.where(high, right, left), jnp.where(high, left, right)


def joined_halves(mine, other, bit):
    high = jnp.bitwise_and(lax.axis_index("seq"), bit) > 0
    return jnp.concatenate([jnp.where(high, other, mine), jnp.where(high, mine, other)], axis=1)


def pair_sum(left, right):
    return (left.astype(F32) + right.astype(F32)).astype(BF16)


def on_device(
    layer_input,
    neighbour_ids,
    out_grad,
    attn_norm_gain,
    attn_norm_bias,
    attn_project,
    attn_merge,
    position_bias,
    ffn_norm_gain,
    ffn_norm_bias,
    ffn_expand,
    expand_bias,
    ffn_reduce,
    reduce_bias,
    near_query,
    near_keys,
    near_merge,
    gate_vector,
):
    batch = layer_input.shape[0]
    count = batch * SEG
    devices = lax.axis_size("fsdp")
    segments = lax.axis_size("seq")
    rows = attn_project.shape[0]
    ff = ffn_expand.shape[1]
    ratio = ff // D

    place = jnp.stack([lax.axis_index("fsdp"), lax.axis_index("seq")]).astype(jnp.int32)
    vectors = [
        attn_norm_gain, attn_norm_bias, ffn_norm_gain, ffn_norm_bias, reduce_bias, gate_vector,
        expand_bias, position_bias,
    ]
    parts = [v.shape[0] for v in vectors[:-1]]
    steps = segment_steps()
    near_steps, far_steps = chip_steps()
    chips = near_steps + far_steps

    attn_shard = pack_first(attn_project, vectors)
    attn_pieces = [attn_shard] + from_chips(attn_shard, chips)
    before = shift(layer_input, 1)
    ids = jnp.swapaxes(neighbour_ids, 1, 2)
    feed_shard = pack(rows, [attn_merge, ffn_expand, ffn_reduce])
    near_shard = pack(rows, [near_query, near_keys, near_merge])
    near_rows = take(place, ids, layer_input, 0, [])
    near_rows, feed_shard, near_shard, attn_pieces = together(
        near_rows, feed_shard, near_shard, attn_pieces
    )
    feed_pieces = [feed_shard] + from_chips(feed_shard, near_steps)
    attn_w, vec, line, joined = first(
        place, layer_input, attn_pieces + from_core(attn_pieces), parts, ff
    )
    joined, before = together(joined, before)
    states = [before]
    if segments > 2:
        states.append(shift(before, 1))
    memory = remember(before, vec, attn_w)
    attended = None
    probs = []
    for part in range(2):
        attended, part_probs = attend(place, joined, memory, line, part * PAIRS, attended)
        probs.append(part_probs)
        if part == 0:
            attended, memory, feed_pieces, near_rows = together(
                attended, memory, feed_pieces, near_rows
            )
            feed_far = from_core(feed_pieces)
            feed_rest = from_chips(feed_pieces[0], far_steps)
            near_rows = take(place, ids, before, 1, [near_rows])
            attended, near_rows, states = together(attended, near_rows, states)
            if len(states) < segments - 1:
                states.append(shift(states[-1], 1))
    attended, feed_far, feed_rest, near_shard = together(
        attended, feed_far, feed_rest, near_shard
    )
    feed_pieces += feed_rest + feed_far + from_core(feed_rest)
    near_pieces = [near_shard] + from_chips(near_shard, chips)
    flat_attended = attended.reshape(count, D)
    after_attn, active, slope, after_ffn = feed(
        place, layer_input.reshape(count, D), flat_attended, vec, feed_pieces
    )
    after_ffn, near_pieces = together(after_ffn, near_pieces)
    while len(states) < segments - 1:
        states.append(shift(states[-1], 1))
    near_pieces += from_core(near_pieces)
    output, row_grads, after_grad, gate_small, near_half, far_half = near(
        place, ids, near_rows, states[1:], after_ffn.reshape(batch, SEG, D), out_grad, vec,
        near_pieces,
    )

    near_arrived = swap(far_half, "fsdp", 1)
    (message,) = give(place, ids, row_grads, None, (segments - 1,))
    message, near_arrived, after_grad, row_grads = together(
        message, near_arrived, after_grad, row_grads
    )
    arrived = shift(message, -1)
    near_sums = core_sums(near_half, near_arrived)
    near_sums, after_grad = together(near_sums, after_grad)
    near_total = [near_sums[0]] + to_chips(near_sums, chips)
    grad_after, att_grad, feed_small, feed_half, feed_far = feed_back(
        place, after_grad.reshape(count, D), after_attn, active, slope, flat_attended, vec,
        feed_pieces,
    )
    feed_half, feed_far, att_grad, row_grads, arrived, near_total = together(
        feed_half, feed_far, att_grad, row_grads, arrived, near_total
    )
    near_low = chip_sum(near_total)
    feed_arrived = swap(feed_far, "fsdp", 1)
    near_pair = (near_low, swap(near_low, "seq", steps[0]))
    row_grads, near_low = together(row_grads, near_low)
    for distance in range(segments - 2, 1, -1):
        (message,) = give(place, ids, row_grads, arrived, (distance,))
        row_grads, message, feed_arrived = together(row_grads, message, feed_arrived)
        if distance > 2:
            arrived = shift(message, -1)
    feed_sums = core_sums(feed_half, feed_arrived)
    feed_total = [feed_sums[0]] + to_chips(feed_sums, chips)
    if segments > 3:
        message, row_grads, near_pair = together(message, row_grads, near_pair, feed_sums)[:3]
        arrived = shift(message, -1)
    sent, own = give(place, ids, row_grads, None, (1, 0))
    att_grad, sent = together(att_grad, sent)
    near_low = pair_sum(*near_pair)
    att_grad, near_low = together(att_grad, near_low)
    *pieces, first_diag = attend_back(
        joined, memory, att_grad.reshape(batch, SEG, D), attended, probs[0], 0, []
    )
    pieces, arrived, near_low = together(pieces, arrived, near_low)
    for index, step in enumerate(steps[1:]):
        if index:
            near_low = pair_sum(*near_pair)
        near_pair = (near_low, swap(near_low, "seq", step))
    pieces, feed_total = together(pieces, feed_total)
    feed_low = chip_sum(feed_total)
    kept, passed = halves(feed_low, steps[0])
    feed_pair = (kept, swap(passed, "seq", steps[0]))
    *pieces, last_diag = attend_back(
        joined, memory, att_grad.reshape(batch, SEG, D), attended, probs[1], PAIRS, pieces
    )
    pieces, feed_pair, near_pair = together(pieces, feed_pair, near_pair)
    for step in steps[1:]:
        kept, passed = halves(pair_sum(*feed_pair), step)
        feed_pair = (kept, swap(passed, "seq", step))
    partial, normed, normed_before, norm_small, *message = finish(
        layer_input, before, pieces, grad_after.reshape(batch, SEG, D), own, sent, arrived, vec,
        attn_w,
    )
    partial, message, norm_small, feed_pair = together(partial, message, norm_small, feed_pair)
    feed_low = pair_sum(*feed_pair)
    last = [shift(message[0], -1)]
    attn_half, attn_far = project_grad(
        place, devices, parts, normed, normed_before, pieces, norm_small, gate_small, feed_small,
        [first_diag, last_diag],
    )
    attn_half, attn_far, message, last, feed_low = together(
        attn_half, attn_far, message, last, feed_low
    )
    attn_arrived = swap(attn_far, "fsdp", 1)
    last += [shift(message[sequence], -1) for sequence in range(1, batch)]
    feed_pair = (feed_low, swap(feed_low, "seq", steps[-1]))
    attn_sums = core_sums(attn_half, attn_arrived)
    attn_total = [attn_sums[0]] + to_chips(attn_sums, chips)
    near_grads = unpack(place, (near_pair, ((1, D), (1, 2 * D), (1, D)), (), 0))
    near_grads, attn_total, last, feed_pair = together(near_grads, attn_total, last, feed_pair)
    attn_low = chip_sum(attn_total)
    for step in reversed(steps[:-1]):
        feed_low = joined_halves(*feed_pair, 2 * step)
        feed_pair = (feed_low, swap(feed_low, "seq", step))
    for step in steps[:-1]:
        attn_low = pair_sum(attn_low, swap(attn_low, "seq", step))
    attn_pair = (attn_low, swap(attn_low, "seq", steps[-1]))
    input_grad = partial + jnp.stack(last).astype(F32)
    attn_pair = together(attn_pair, input_grad)[0]
    widths = parts + [position_bias.shape[0]]
    project_out, *rest = unpack(
        place,
        (attn_pair, ((1, 3 * D),), widths, 0),
        (feed_pair, ((1, ff), (ratio, D), (1, D)), (), steps[0]),
    )
    smalls, feed_grads = rest[: len(widths)], rest[len(widths) :]
    return (
        output,
        input_grad,
        smalls[0],
        smalls[1],
        project_out,
        feed_grads[2],
        smalls[7],
        smalls[2],
        smalls[3],
        feed_grads[0],
        smalls[6],
        feed_grads[1],
        smalls[4],
        *near_grads,
        smalls[5],
    )


def solution(mesh):
    in_specs = (
        P("fsdp", "seq", None),
        P("fsdp", "seq", None),
        P("fsdp", "seq", None),
        P("fsdp"),
        P("fsdp"),
        P("fsdp", None),
        P("fsdp", None),
        P("fsdp"),
        P("fsdp"),
        P("fsdp"),
        P("fsdp", None),
        P("fsdp"),
        P("fsdp", None),
        P("fsdp"),
        P("fsdp", None),
        P("fsdp", None),
        P("fsdp", None),
        P("fsdp"),
    )
    out_specs = (
        P("fsdp", "seq", None),
        P("fsdp", "seq", None),
        P("fsdp"),
        P("fsdp"),
        P("fsdp", None),
        P("fsdp", None),
        P("fsdp"),
        P("fsdp"),
        P("fsdp"),
        P("fsdp", None),
        P("fsdp"),
        P("fsdp", None),
        P("fsdp"),
        P("fsdp", None),
        P("fsdp", None),
        P("fsdp", None),
        P("fsdp"),
    )
    return jax.shard_map(
        on_device, mesh=mesh, in_specs=in_specs, out_specs=out_specs, check_vma=False
    )
```
